256 devices in a mesh: req: 128 (over x, y, z), head: 2 (over core).
Axes of the slice: x: 4, y: 4, z: 8, core: 2. Of those that a mesh axis runs over, the one named last changes fastest.
Arguments:
- verify_x: bfloat16 [128, 5, 2048], P('req'), may hold values from -6 to 6
- prefill_x: bfloat16 [32768, 2048], P('req'), may hold values from -6 to 6
- attn_gain: float32 [2048], replicated, may hold values from 0.25 to 1.75
- w_query: bfloat16 [2048, 2048], P(None, 'head'), may hold values from -0.125 to 0.125
- w_keyval: bfloat16 [2048, 1024], P(None, 'head'), may hold values from -0.125 to 0.125
- qk_gain: float32 [2, 256], replicated, may hold values from 0.25 to 8
- w_out: bfloat16 [2048, 2048], P('head'), may hold values from -0.125 to 0.125
- post_gain: float32 [2048], replicated, may hold values from 0.1 to 1.9
- page_pool: bfloat16 [8192, 16, 1024], P('req', None, 'head'), may hold values from -6 to 6
- outbound: int32 [128, 128], P('req'), may hold values from -1 to 63, as said below
- page_table: int32 [128, 64], P('req'), may hold values from 0 to 191, as said below
- cache_len: int32 [128], P('req'), may hold values from 1 to 1024, as said below
- prompt_len: int32 [128, 4], P('req'), may hold values from 1 to 128, 256 in all within a row
- accepted: int32 [128], P('req'), may hold values from 0 to 5
Outputs:
- verify_out: bfloat16 [128, 5, 2048], P('req', None, 'head')
- prefill_out: bfloat16 [32768, 2048], P('req', 'head')
- verify_kv: bfloat16 [128, 5, 1024], P('req', None, 'head')
- prefill_kv: bfloat16 [32768, 1024], P('req', 'head')
The draws below stay inside these ranges and needn't reach their ends.
Inputs may be any that keep to these rules, and one draw needn't show every extreme that they name: `outbound`: row s names a page of device s's pool for every device d other than s; the entry at d = s is -1. `page_table`: an entry below 64 names a page of the device's own pool; an entry 64 + s names the page received from device s, s never the device itself. `cache_len`: some request has exactly 1024 cached tokens.
All inputs are finite; a program needn't handle non-finite values.
Results may differ from the reference program's by a relative error of at most 0.015.
The reference program's roundings to bfloat16 on the way count: a program that leaves them out, or rounds other values in their place, can miss the bound.
Values may be sent and summed in bfloat16 or wider, within the bound.
No kernel may reach another device: no remote copies, remote signals or barrier semaphores. Data moves between devices by JAX's collectives and lax.ppermute only.
A program may use at most 64 MiB of HBM per device.

```python
import math
import jax
import jax.numpy as jnp
import numpy as np
from jax import lax

D = 2048
HEADS = 8
KV_HEADS = 2
HEAD = 256
DRAFT = 5
PAGE = 16
CACHE = 1024
MAXP = 64
REQ_DEV = 1
POOL_DEV = 64
REQS = 128
PREF_DEV = 256
PROMPTS = 4
PREFILL = 32768
N_REQ = 128


def migration_plan(key):
    key_page = jax.random.fold_in(jax.random.fold_in(key, 7), 1)
    send_plan = jax.random.randint(key_page, (N_REQ, N_REQ), 0, POOL_DEV)
    send_plan = send_plan.at[1, 0].set(POOL_DEV - 1)
    send_plan = send_plan.at[N_REQ - 1, 0].set(0)
    on_diagonal = jnp.arange(N_REQ, dtype=jnp.int32)[:, None] == jnp.arange(N_REQ, dtype=jnp.int32)[None, :]
    send_plan = jnp.where(on_diagonal, -1, send_plan)
    return send_plan.astype(jnp.int32)


def draw_outbound(key, part):
    return migration_plan(key)


def draw_page_table(key, part):
    send_plan = migration_plan(key)
    candidate = jax.random.randint(jax.random.fold_in(key, 11), (REQS, MAXP), 0, POOL_DEV + N_REQ)
    device = (jnp.arange(REQS, dtype=jnp.int32) // REQ_DEV)[:, None]
    source = jnp.clip(candidate - POOL_DEV, 0, N_REQ - 1)
    arrived = send_plan[source, device] >= 0
    valid = (candidate < POOL_DEV) | arrived
    page_list = jnp.where(valid, candidate, candidate % POOL_DEV)
    page_list = page_list.at[0, 0].set(POOL_DEV + N_REQ - 1)
    return page_list.astype(jnp.int32)


def draw_cache_len(key, part):
    lengths = jax.random.randint(jax.random.fold_in(key, 13), (REQS,), 1, CACHE + 1)
    return lengths.at[0].set(CACHE).astype(jnp.int32)


def draw_qk_gain(key, part):
    key_base = jax.random.fold_in(jax.random.fold_in(key, 17), 0)
    gains = 1.0 + 0.15 * jnp.clip(jax.random.normal(key_base, (2, HEAD), jnp.float32), -5.0, 5.0)
    return gains


def draw_page_pool(key, part):
    shape = (N_REQ * POOL_DEV, PAGE, KV_HEADS * 2 * HEAD)
    key_body = jax.random.fold_in(jax.random.fold_in(key, 19), 0)
    entries = jnp.clip(jax.random.normal(key_body, shape, jnp.float32), -6.0, 6.0)
    return entries.astype(jnp.bfloat16)


def place_ends(values, own_key, low, top_value):
    shape = values.shape
    spot = [jax.random.randint(jax.random.fold_in(own_key, axis), (), 0, shape[axis]) for axis in range(len(shape))]
    values = values.at[tuple(spot)].set(low)
    longest = shape.index(max(shape))
    spot[longest] = (spot[longest] + 1) % shape[longest]
    return values.at[tuple(spot)].set(top_value)


def shard_levels(rng, extent, cuts, least, high):
    loudness = 1.0
    for dim, parts in cuts:
        draws = jax.random.uniform(jax.random.fold_in(jax.random.fold_in(rng, 6), dim), (parts,), jnp.float32, least / len(cuts), high / len(cuts))
        loudness = loudness * jnp.repeat(jnp.exp(draws), extent[dim] // parts).reshape((-1,) + (1,) * (len(extent) - 1 - dim))
    return loudness


def length_profile(number_of, total, most, slope):
    loads = [(1 << 20) // math.isqrt(rank ** slope) + 1 for rank in range(2, number_of + 1)]
    rest, counts = total - most - (number_of - 1), [1] * (number_of - 1)
    while rest > 0:
        candidates = [i for i in range(number_of - 1) if counts[i] < most]
        mass, left = sum([loads[i] for i in candidates]), rest
        for i in candidates:
            addition = min(most - counts[i], max(1, left * loads[i] // mass), rest)
            counts[i] = counts[i] + addition
            rest = rest - addition
    return np.array([most] + counts)


def ragged_sizes(rng, number_of, total, limit, lean):
    if number_of == 2:
        one = jax.random.randint(rng, (), max(1, total - limit), min(limit, total - 1) + 1)
        return jnp.stack([one, total - one])
    sizes = jnp.asarray(length_profile(number_of, total, limit, lean), jnp.int32)
    pairs = (number_of - 1) // 2
    donor, receiver = sizes[1:1 + 2 * pairs:2], sizes[2:2 + 2 * pairs:2]
    margin = jnp.minimum(donor - 1, limit - receiver)
    moved = jax.random.randint(jax.random.fold_in(rng, 1), (pairs,), 0, 1 << 20) % (margin + 1)
    sizes = sizes.at[1:1 + 2 * pairs:2].set(donor - moved).at[2:2 + 2 * pairs:2].set(receiver + moved)
    return sizes[jax.random.permutation(jax.random.fold_in(rng, 2), number_of)]


def scatter_about(own_key, extent, deviation, most, cuts=(), kind=jnp.bfloat16):
    drawn = jax.random.normal(own_key, extent, jnp.float32) * deviation
    if len(cuts) > 0:
        drawn = shard_levels(own_key, extent, cuts, -0.22, 0.18) * drawn
    return jnp.clip(drawn, min=-most, max=most).astype(kind)


def setup_inputs(seed: int = 0) -> dict:
    key_list = jax.random.split(jax.random.key(seed), 15)
    return {
        "verify_x": scatter_about(key_list[0], (REQS, DRAFT, D), 1.0, 6.0, ((0, 128),)),
        "prefill_x": scatter_about(key_list[1], (PREFILL, D), 1.0, 6.0, ((0, 128),)),
        "attn_gain": jnp.clip(1.0 + 0.15 * jax.random.normal(key_list[2], (D,), jnp.float32), 0.25, 1.75),
        "w_query": scatter_about(key_list[3], (D, HEADS * HEAD), D ** -0.5, 0.125, ((1, 2),)),
        "w_keyval": scatter_about(key_list[4], (D, KV_HEADS * 2 * HEAD), D ** -0.5, 0.125, ((1, 2),)),
        "qk_gain": draw_qk_gain(jax.random.fold_in(key_list[14], 71), 0),
        "w_out": scatter_about(key_list[6], (HEADS * HEAD, D), (HEADS * HEAD) ** -0.5, 0.125, ((0, 2),)),
        "post_gain": jnp.clip(1.0 + 0.18 * jax.random.normal(key_list[7], (D,), jnp.float32), 0.1, 1.9),
        "page_pool": draw_page_pool(jax.random.fold_in(key_list[14], 71), 0),
        "outbound": draw_outbound(jax.random.fold_in(key_list[14], 71), 0),
        "page_table": draw_page_table(jax.random.fold_in(key_list[14], 71), 0),
        "cache_len": draw_cache_len(jax.random.fold_in(key_list[14], 71), 0),
        "prompt_len": jax.vmap(lambda own: ragged_sizes(own, PROMPTS, PREF_DEV, PREF_DEV // 2, 2))(jax.random.split(key_list[12], N_REQ)).reshape((N_REQ, PROMPTS)).astype(jnp.int32),
        "accepted": place_ends(jax.random.randint(key_list[13], (REQS,), 0, DRAFT + 1), jax.random.fold_in(key_list[13], 1), 0, DRAFT).astype(jnp.int32),
    }


eps_norm = 1e-06
rope_base = 1000000.0
neg_large = -1e+30

def rms_scale(values):
    return values * lax.rsqrt(lax.optimization_barrier(jnp.mean(values * values, axis=-1, keepdims=True)) + eps_norm)

def rotate(values, position):
    half_dim = values.shape[-1] // 2
    inv_freq = rope_base ** (-(jnp.arange(half_dim, dtype=jnp.float32) * 2.0) / values.shape[-1])
    angles = position[:, None, None] * inv_freq[None, None, :]
    cosine = jnp.cos(angles)
    sine_part = jnp.sin(angles)
    first = values[..., :half_dim]
    second = values[..., half_dim:]
    return jnp.concatenate([first * cosine - second * sine_part, second * cosine + first * sine_part], axis=-1)

def project(hidden_rows, attn_gain, w_query, w_keyval, qk_gain, position):
    row_count = hidden_rows.shape[0]
    normed = (rms_scale(hidden_rows.astype(jnp.float32)) * attn_gain).astype(jnp.bfloat16)
    query_rows = jnp.dot(normed, w_query, preferred_element_type=jnp.float32).reshape(row_count, -1, HEAD)
    query_rows = rotate(rms_scale(query_rows) * qk_gain[0], position).astype(jnp.bfloat16)
    keyval = jnp.dot(normed, w_keyval, preferred_element_type=jnp.float32).reshape(row_count, -1, 2, HEAD)
    key_rows = rotate(rms_scale(keyval[:, :, 0]) * qk_gain[1], position).astype(jnp.bfloat16)
    value_rows = rms_scale(keyval[:, :, 1]).astype(jnp.bfloat16)
    return (query_rows, key_rows, value_rows)

def attend(query_rows, key_rows, value_rows, allowed):
    row_count = query_rows.shape[0]
    groups = key_rows.shape[1]
    grouped = query_rows.reshape(row_count, groups, -1, HEAD).astype(jnp.float32)
    scores = jnp.einsum('tgqe,jge->gqtj', grouped, key_rows.astype(jnp.float32))
    scores = jnp.where(allowed[None, None], scores, neg_large)
    peak_score = lax.optimization_barrier(jnp.max(scores, axis=-1, keepdims=True))
    weights = jnp.exp(scores - peak_score)
    denom_sum = lax.optimization_barrier(jnp.sum(weights, axis=-1, keepdims=True))
    attn_probs = (weights / denom_sum).astype(jnp.bfloat16)
    mixed_heads = jnp.einsum('gqtj,jge->tgqe', attn_probs.astype(jnp.float32), value_rows.astype(jnp.float32))
    return mixed_heads.reshape(row_count, -1).astype(jnp.bfloat16)

def prompt_layout(lengths, row_count):
    prompt_ends = jnp.cumsum(lengths)
    row_index = jnp.arange(row_count, dtype=jnp.int32)
    segment = lax.optimization_barrier(jnp.sum((row_index[:, None] >= prompt_ends[None, :]).astype(jnp.int32), axis=1))
    starts = prompt_ends - lengths
    which = segment[:, None] == jnp.arange(lengths.shape[0], dtype=jnp.int32)[None, :]
    start_row = lax.optimization_barrier(jnp.sum(jnp.where(which, starts[None, :], 0), axis=1))
    position = (row_index - start_row).astype(jnp.float32)
    allowed = (segment[:, None] == segment[None, :]) & (row_index[None, :] <= row_index[:, None])
    return (position, allowed)

def reference(verify_x, prefill_x, attn_gain, w_query, w_keyval, qk_gain, w_out, post_gain, page_pool, outbound, page_table, cache_len, prompt_len, accepted):
    groups = KV_HEADS

    def one_request(request):
        device = request // REQ_DEV
        position = (cache_len[request] + jnp.arange(DRAFT, dtype=jnp.int32)).astype(jnp.float32)
        query_rows, key_rows, value_rows = project(verify_x[request], attn_gain, w_query, w_keyval, qk_gain, position)
        page_list = page_table[request]
        source = jnp.clip(page_list - POOL_DEV, 0, N_REQ - 1).astype(jnp.int32)
        sent_page = outbound[source, device]
        is_local = page_list < POOL_DEV
        flat_index = jnp.where(is_local, device * POOL_DEV + page_list, source * POOL_DEV + jnp.clip(sent_page, 0, POOL_DEV - 1)).astype(jnp.int32)
        is_live = is_local | (sent_page >= 0)
        page_rows = jnp.take(page_pool, flat_index, axis=0)
        page_rows = jnp.where(is_live[:, None, None], page_rows, jnp.zeros_like(page_rows))
        cached = page_rows.reshape(CACHE, groups, 2, HEAD)
        all_keys = jnp.concatenate([cached[:, :, 0], key_rows], axis=0)
        all_values = jnp.concatenate([cached[:, :, 1], value_rows], axis=0)
        slot = jnp.arange(CACHE + DRAFT, dtype=jnp.int32)
        step_index = jnp.arange(DRAFT, dtype=jnp.int32)
        allowed = jnp.where(slot[None, :] < CACHE, slot[None, :] < cache_len[request], slot[None, :] - CACHE <= step_index[:, None])
        attention = attend(query_rows, all_keys, all_values, allowed)
        new_cache = jnp.stack([key_rows, value_rows], axis=2).reshape(DRAFT, -1)
        return (attention, new_cache)
    verify_attn, verify_cache = lax.map(one_request, jnp.arange(REQS, dtype=jnp.int32))

    def one_device(device):
        hidden_rows = lax.dynamic_slice_in_dim(prefill_x, device * PREF_DEV, PREF_DEV, 0)
        position, allowed = prompt_layout(prompt_len[device], PREF_DEV)
        query_rows, key_rows, value_rows = project(hidden_rows, attn_gain, w_query, w_keyval, qk_gain, position)
        attention = attend(query_rows, key_rows, value_rows, allowed)
        new_cache = jnp.stack([key_rows, value_rows], axis=2).reshape(PREF_DEV, -1)
        return (attention, new_cache)
    prefill_attn, prefill_cache = lax.map(one_device, jnp.arange(N_REQ, dtype=jnp.int32))
    all_rows = jnp.concatenate([verify_x.reshape(-1, D), prefill_x], axis=0)
    all_attn = jnp.concatenate([verify_attn.reshape(-1, HEADS * HEAD), prefill_attn.reshape(-1, HEADS * HEAD)], axis=0)
    projected = jnp.dot(all_attn, w_out, preferred_element_type=jnp.float32)
    final = (all_rows.astype(jnp.float32) + rms_scale(projected) * post_gain).astype(jnp.bfloat16)
    verify_out = final[:REQS * DRAFT].reshape(REQS, DRAFT, D)
    prefill_out = final[REQS * DRAFT:]
    keep_rows = jnp.arange(DRAFT, dtype=jnp.int32)[None, :, None] < accepted[:, None, None]
    verify_kv = jnp.where(keep_rows, verify_cache, jnp.zeros_like(verify_cache))
    prefill_kv = prefill_cache.reshape(PREFILL, -1)
    return (verify_out, prefill_out, verify_kv, prefill_kv)
```

```python
import functools

import jax
import jax.numpy as jnp
from jax import lax
from jax.experimental import pallas as pl
from jax.experimental.pallas import tpu as pltpu
from jax.sharding import PartitionSpec as P

HEAD = 256
PAGE = 16
eps_norm = 1e-06
rope_base = 1000000.0
neg_large = -1e30
bf16, f32 = jnp.bfloat16, jnp.float32
PAD = 8


def dot_t(a, b):
    return lax.dot_general(a, b, (((1,), (1,)), ((), ())), preferred_element_type=f32)


def dot_n(a, b):
    return jnp.dot(a, b, preferred_element_type=f32)


def pick_kernel(index, pool, out):
    base = pl.program_id(0) * out.shape[0]
    for i in range(out.shape[0]):
        page = jnp.clip(index[base + i], 0, pool.shape[0] - 1)
        out[i] = pool[page]


def pick_pages(pool, index):
    count, steps = index.shape[0], 4
    rows = count // steps
    return pl.pallas_call(
        pick_kernel,
        grid_spec=pltpu.PrefetchScalarGridSpec(
            num_scalar_prefetch=1,
            grid=(steps,),
            in_specs=[pl.BlockSpec(pool.shape, lambda i, idx: (0, 0, 0))],
            out_specs=pl.BlockSpec((rows,) + pool.shape[1:], lambda i, idx: (i, 0, 0)),
        ),
        out_shape=jax.ShapeDtypeStruct((count,) + pool.shape[1:], pool.dtype),
        cost_estimate=pl.CostEstimate(flops=0, transcendentals=0, bytes_accessed=3 << 20),
        name="pick_pages",
    )(index, pool)


def project_kernel(x, gain, wq, wkv, qk_gain, cosine, sine, out, kv_out, normed):
    step = pl.program_id(0)
    tail = kv_out.shape[0]

    @pl.when(step == 0)
    def _():
        rows = x[...].astype(f32)
        scale = lax.rsqrt(jnp.mean(rows * rows, axis=-1, keepdims=True) + eps_norm)
        normed[...] = (rows * scale * gain[...]).astype(bf16)

    def normalised(weights):
        acc = dot_n(normed[...], weights)
        return acc * lax.rsqrt(jnp.mean(acc * acc, axis=-1, keepdims=True) + eps_norm)

    def rotated(values):
        half = HEAD // 2
        a, b = values[:, :half], values[:, half:]
        c, s = cosine[...], sine[...]
        return jnp.concatenate([a * c - b * s, b * c + a * s], axis=-1).astype(bf16)

    @pl.when(step < 4)
    def _():
        out[0] = rotated(normalised(wq[...]) * qk_gain[0:1, :])

    @pl.when(step == 4)
    def _():
        key = rotated(normalised(wkv[...]) * qk_gain[1:2, :])
        out[0] = key
        kv_out[...] = key[:tail]

    @pl.when(step == 5)
    def _():
        value = normalised(wkv[...]).astype(bf16)
        out[0] = value
        kv_out[...] = value[:tail]


def project(rows, gain, w_query, w_keyval, qk_gain, cosine, sine, tail):
    count, width = rows.shape
    whole = lambda shape: pl.BlockSpec(shape, lambda i: (0, 0))
    return pl.pallas_call(
        project_kernel,
        grid=(6,),
        in_specs=[
            whole((count, width)),
            whole((1, width)),
            pl.BlockSpec((width, HEAD), lambda i: (0, jnp.minimum(i, 3))),
            pl.BlockSpec((width, HEAD), lambda i: (0, jnp.maximum(i - 4, 0))),
            whole((2, HEAD)),
            whole((count, HEAD // 2)),
            whole((count, HEAD // 2)),
        ],
        out_specs=[
            pl.BlockSpec((1, count, HEAD), lambda i: (i, 0, 0)),
            pl.BlockSpec((tail, HEAD), lambda i: (0, jnp.maximum(i - 4, 0))),
        ],
        out_shape=[
            jax.ShapeDtypeStruct((6, count, HEAD), bf16),
            jax.ShapeDtypeStruct((tail, 2 * HEAD), bf16),
        ],
        scratch_shapes=[pltpu.VMEM((count, width), bf16)],
        compiler_params=pltpu.CompilerParams(vmem_limit_bytes=24 << 20),
        cost_estimate=pl.CostEstimate(
            flops=2 * count * width * 1536, transcendentals=0, bytes_accessed=9 << 20
        ),
        name="project",
    )(rows, gain, w_query, w_keyval, qk_gain, cosine, sine)


def prompt_kernel(ends, q, k, v, w_out, out, attn):
    rows = attn.shape[0]

    @pl.when(pl.program_id(0) == 0)
    def _():
        row = lax.broadcasted_iota(jnp.int32, (rows, rows), 0)
        col = lax.broadcasted_iota(jnp.int32, (rows, rows), 1)
        start = jnp.zeros((rows, rows), jnp.int32)
        for i in range(3):
            start = jnp.where(row >= ends[i], ends[i], start)
        allowed = (col <= row) & (col >= start)
        key, value = k[0, :rows], v[0, :rows]
        for h in range(4):
            scores = jnp.where(allowed, dot_t(q[h, :rows], key), neg_large)
            weights = jnp.exp(scores - jnp.max(scores, axis=-1, keepdims=True))
            probs = (weights / jnp.sum(weights, axis=-1, keepdims=True)).astype(bf16)
            attn[:, h * HEAD : (h + 1) * HEAD] = dot_n(probs, value).astype(bf16)

    out[...] = dot_n(attn[...], w_out[...]).astype(out.dtype)


def prompts(ends, qkv, w_out, rows):
    count = qkv.shape[1]
    depth, width = w_out.shape
    cols = 512
    return pl.pallas_call(
        prompt_kernel,
        grid_spec=pltpu.PrefetchScalarGridSpec(
            num_scalar_prefetch=1,
            grid=(width // cols,),
            in_specs=[
                pl.BlockSpec((4, count, HEAD), lambda i, e: (0, 0, 0)),
                pl.BlockSpec((1, count, HEAD), lambda i, e: (4, 0, 0)),
                pl.BlockSpec((1, count, HEAD), lambda i, e: (5, 0, 0)),
                pl.BlockSpec((depth, cols), lambda i, e: (0, i)),
            ],
            out_specs=pl.BlockSpec((rows, cols), lambda i, e: (0, i)),
            scratch_shapes=[pltpu.VMEM((rows, depth), bf16)],
        ),
        out_shape=jax.ShapeDtypeStruct((rows, width), bf16),
        compiler_params=pltpu.CompilerParams(vmem_limit_bytes=24 << 20),
        cost_estimate=pl.CostEstimate(
            flops=2 * rows * depth * width, transcendentals=4 * rows * rows, bytes_accessed=6 << 20
        ),
        name="prompts",
    )(ends, qkv, qkv, qkv, w_out)


def piece(scores, count):
    live = count > 0.0
    scores = jnp.where(live, scores, neg_large)
    peak = jnp.max(scores, axis=-1, keepdims=True).astype(bf16).astype(f32)
    weights = jnp.where(live, jnp.exp(scores - peak) * count, 0.0)
    return weights, peak, jnp.sum(weights, axis=-1, keepdims=True)


def remote_kernel(queries, pages, out):
    groups, rows = queries.shape[0], queries.shape[1]
    lane = lax.broadcasted_iota(jnp.int32, (rows, 128), 1)
    for z in range(groups):
        query = queries[z]
        count = query[5:6, :].astype(f32)
        held = pages[:, z].reshape(-1, 2 * HEAD)
        weights, peak, denom = piece(dot_t(query, held[:, :HEAD]), count)
        total = dot_n(weights.astype(bf16), held[:, HEAD:])
        high = denom.astype(bf16).astype(f32)
        stats = jnp.where(lane < 32, peak, jnp.where(lane < 64, high, denom - high))
        out[z, :, :HEAD] = total.astype(bf16)
        out[z, :, HEAD:] = stats.astype(bf16)


def remote_pieces(queries, pages):
    groups, rows, _ = queries.shape
    return pl.pallas_call(
        remote_kernel,
        out_shape=jax.ShapeDtypeStruct((groups, rows, HEAD + 128), bf16),
        compiler_params=pltpu.CompilerParams(vmem_limit_bytes=24 << 20),
        cost_estimate=pl.CostEstimate(flops=1 << 26, transcendentals=1 << 16, bytes_accessed=3 << 20),
        name="remote_pieces",
    )(queries, pages)


def local_kernel(qkv, pool, count, out):
    rows = 4 * PAD
    query = qkv[0:4].reshape(rows, HEAD)
    key, value = qkv[4], qkv[5]
    scores = dot_t(query, pool[:, :HEAD])
    live = count[...] > 0.0
    scores = jnp.where(live, scores, neg_large)
    fresh = dot_t(query, key)
    token = lax.broadcasted_iota(jnp.int32, fresh.shape, 0) % PAD
    col = lax.broadcasted_iota(jnp.int32, fresh.shape, 1)
    allowed = col <= token
    fresh = jnp.where(allowed, fresh, neg_large)
    peak = jnp.maximum(
        jnp.max(scores, axis=-1, keepdims=True), jnp.max(fresh, axis=-1, keepdims=True)
    )
    weights = jnp.where(live, jnp.exp(scores - peak) * count[...], 0.0)
    fresh = jnp.where(allowed, jnp.exp(fresh - peak), 0.0)
    denom = jnp.sum(weights, axis=-1, keepdims=True) + jnp.sum(fresh, axis=-1, keepdims=True)
    out[:, :HEAD] = dot_n(weights.astype(bf16), pool[:, HEAD:]) + dot_n(
        fresh.astype(bf16), value
    )
    out[:, HEAD : HEAD + 128] = jnp.broadcast_to(peak, (rows, 128))
    out[:, HEAD + 128 :] = jnp.broadcast_to(denom, (rows, 128))


def local_piece(qkv, pool, count):
    return pl.pallas_call(
        local_kernel,
        out_shape=jax.ShapeDtypeStruct((4 * PAD, 2 * HEAD), f32),
        compiler_params=pltpu.CompilerParams(vmem_limit_bytes=24 << 20),
        cost_estimate=pl.CostEstimate(flops=1 << 26, transcendentals=1 << 15, bytes_accessed=2 << 20),
        name="local_piece",
    )(qkv, pool, count)


def join_kernel(pieces, local, w_out, out, attn):
    @pl.when(pl.program_id(0) == 0)
    def _():
        groups = pieces.shape[0]
        peaks = [pieces[z, :, HEAD : HEAD + 1].astype(f32) for z in range(groups)]
        own = local[:, HEAD : HEAD + 1]
        top = functools.reduce(jnp.maximum, peaks, own)
        scale = jnp.exp(own - top)
        total = local[:, :HEAD] * scale
        denom = local[:, HEAD + 128 : HEAD + 129] * scale
        for z in range(groups):
            scale = jnp.exp(peaks[z] - top)
            total += pieces[z, :, :HEAD].astype(f32) * scale
            denom += scale * (
                pieces[z, :, HEAD + 32 : HEAD + 33].astype(f32)
                + pieces[z, :, HEAD + 64 : HEAD + 65].astype(f32)
            )
        attn[...] = total / denom

    acc = None
    for h in range(4):
        part = dot_n(
            attn[h * PAD : (h + 1) * PAD, :].astype(bf16), w_out[h * HEAD : (h + 1) * HEAD, :]
        )
        acc = part if acc is None else acc + part
    out[...] = acc


def join(pieces, local, w_out):
    depth, width = w_out.shape
    cols = 512
    return pl.pallas_call(
        join_kernel,
        grid=(width // cols,),
        in_specs=[
            pl.BlockSpec(pieces.shape, lambda i: (0, 0, 0)),
            pl.BlockSpec(local.shape, lambda i: (0, 0)),
            pl.BlockSpec((depth, cols), lambda i: (0, i)),
        ],
        out_specs=pl.BlockSpec((PAD, cols), lambda i: (0, i)),
        out_shape=jax.ShapeDtypeStruct((PAD, width), f32),
        scratch_shapes=[pltpu.VMEM((4 * PAD, HEAD), f32)],
        compiler_params=pltpu.CompilerParams(vmem_limit_bytes=24 << 20),
        cost_estimate=pl.CostEstimate(flops=1 << 25, transcendentals=0, bytes_accessed=4 << 20),
        name="join",
    )(pieces, local, w_out)


def finish_kernel(side, own, other, x, gain, out):
    half = out.shape[1]
    total = own[...].astype(f32) + other[...].astype(f32)
    scale = lax.rsqrt(jnp.mean(total * total, axis=-1, keepdims=True) + eps_norm)
    mine = jnp.where(side[0] == 0, total[:, :half], total[:, half:])
    out[...] = (x[...].astype(f32) + mine * scale * gain[...]).astype(bf16)


def finish(side, own, other, x, gain, name):
    rows, width = own.shape
    half = width // 2
    block = min(rows, 64)
    return pl.pallas_call(
        finish_kernel,
        grid_spec=pltpu.PrefetchScalarGridSpec(
            num_scalar_prefetch=1,
            grid=(rows // block,),
            in_specs=[
                pl.BlockSpec((block, width), lambda i, s: (i, 0)),
                pl.BlockSpec((block, width), lambda i, s: (i, 0)),
                pl.BlockSpec((block, half), lambda i, s: (i, s[0])),
                pl.BlockSpec((1, half), lambda i, s: (0, s[0])),
            ],
            out_specs=pl.BlockSpec((block, half), lambda i, s: (i, 0)),
        ),
        out_shape=jax.ShapeDtypeStruct((rows, half), bf16),
        cost_estimate=pl.CostEstimate(
            flops=8 * rows * width, transcendentals=0, bytes_accessed=6 * rows * width
        ),
        name=name,
    )(side, own, other, x, gain)


def on_device(
    plane,
    column,
    verify_x,
    prefill_x,
    attn_gain,
    w_query,
    w_keyval,
    qk_gain,
    w_out,
    post_gain,
    page_pool,
    outbound,
    page_table,
    cache_len,
    prompt_len,
    accepted,
):
    _, draft, width = verify_x.shape
    rows = prefill_x.shape[0]
    pool_pages = page_pool.shape[0]
    planes, depth = len(plane[0]), len(column[0])

    outgoing = pick_pages(page_pool, outbound[0])
    arrived = lax.all_to_all(
        outgoing, "req", 0, 0, tiled=True, axis_index_groups=plane
    )

    length = cache_len[0]
    slot_page = page_table[0]
    pages = pool_pages + planes * depth
    slots = slot_page.shape[0]
    offset = (
        jnp.arange(slots, dtype=jnp.int32)[:, None] * PAGE
        + jnp.arange(PAGE, dtype=jnp.int32)[None, :]
    )
    valid = (offset < length).astype(bf16)
    names = (slot_page[None, :] == jnp.arange(pages, dtype=jnp.int32)[:, None]).astype(bf16)
    counts = jnp.dot(names, valid, preferred_element_type=f32)
    own_count = counts[:pool_pages].reshape(1, pool_pages * PAGE)
    sent_count = (
        counts[pool_pages:]
        .reshape(planes, depth, PAGE)
        .transpose(1, 0, 2)
        .reshape(depth, 1, planes * PAGE)
        .astype(bf16)
    )

    lengths = prompt_len[0]
    ends = jnp.stack([lengths[0], lengths[0] + lengths[1], lengths[0] + lengths[1] + lengths[2]])
    row = jnp.arange(rows, dtype=jnp.int32)
    start = jnp.max(
        jnp.where(row[:, None] >= ends[None, :], ends[None, :], 0), axis=1
    )
    position = jnp.concatenate(
        [row - start, length + jnp.arange(PAD, dtype=jnp.int32)]
    ).astype(f32)
    half_dim = HEAD // 2
    inv_freq = rope_base ** (-(jnp.arange(half_dim, dtype=f32) * 2.0) / HEAD)
    angles = position[:, None] * inv_freq[None, :]
    cosine, sine = jnp.cos(angles), jnp.sin(angles)

    drafted = jnp.pad(verify_x[0], ((0, PAD - draft), (0, 0)))
    all_rows = jnp.concatenate([prefill_x, drafted], axis=0)
    qkv, prefill_kv = project(
        all_rows, attn_gain[None], w_query, w_keyval, qk_gain, cosine, sine, rows
    )
    draft_qkv = qkv[:, rows:]
    query = draft_qkv[:4].reshape(1, 4 * PAD, HEAD)
    mark = jnp.arange(4 * PAD, dtype=jnp.int32)[None, :, None] == draft
    queries = lax.all_to_all(
        jnp.where(mark, sent_count, query),
        "req", 0, 0, tiled=True, axis_index_groups=column,
    )

    own = local_piece(draft_qkv, page_pool.reshape(pool_pages * PAGE, -1), own_count)
    side = lax.axis_index("head").reshape(1)
    swap = [(0, 1), (1, 0)]
    partial = prompts(ends, qkv, w_out, rows)
    other = lax.ppermute(partial, "head", swap)
    prefill_out = finish(side, partial, other, prefill_x, post_gain[None], "finish_prompts")

    sent = remote_pieces(queries, arrived.reshape(planes, depth, PAGE, -1))
    pieces = lax.all_to_all(sent, "req", 0, 0, tiled=True, axis_index_groups=column)
    partial_v = join(pieces, own, w_out)
    other_v = lax.ppermute(partial_v, "head", swap)
    verify_out = finish(side, partial_v, other_v, drafted, post_gain[None], "finish_drafts")
    verify_out = verify_out[None, :draft]

    fresh = jnp.concatenate([draft_qkv[4, :draft], draft_qkv[5, :draft]], axis=-1)
    keep = jnp.arange(draft, dtype=jnp.int32)[:, None] < accepted[0]
    verify_kv = jnp.where(keep, fresh, jnp.zeros_like(fresh))[None]
    return (verify_out, prefill_out, verify_kv, prefill_kv)


def solution(mesh):
    devices = mesh.shape["req"]
    deep = 8
    plane = [[i for i in range(devices) if i % deep == z] for z in range(deep)]
    column = [list(range(i, i + deep)) for i in range(0, devices, deep)]
    placed = (
        P("req", None, None),
        P("req", None),
        P(),
        P(None, "head"),
        P(None, "head"),
        P(),
        P("head", None),
        P(),
        P("req", None, "head"),
        P("req", None),
        P("req", None),
        P("req"),
        P("req", None),
        P("req"),
    )
    return jax.shard_map(
        functools.partial(on_device, plane, column),
        mesh=mesh,
        in_specs=placed,
        out_specs=(
            P("req", None, "head"),
            P("req", "head"),
            P("req", None, "head"),
            P("req", "head"),
        ),
        check_vma=False,
    )
```

```python
import functools

import jax
import jax.numpy as jnp
from jax import lax
from jax.experimental import pallas as pl
from jax.experimental.pallas import tpu as pltpu
from jax.sharding import PartitionSpec as P

HEAD = 256
PAGE = 16
QH = 4
PAD = 8
DEEP = 8
eps_norm = 1e-06
rope_base = 1000000.0
neg_large = -1e30
bf16, f32, i32 = jnp.bfloat16, jnp.float32, jnp.int32
HBM = pl.BlockSpec(memory_space=pltpu.MemorySpace.HBM)
VMEM = pl.BlockSpec(memory_space=pltpu.MemorySpace.VMEM)
SMEM = pl.BlockSpec(memory_space=pltpu.MemorySpace.SMEM)


def dot_t(a, b):
    return lax.dot_general(a, b, (((1,), (1,)), ((), ())), preferred_element_type=f32)


def dot_n(a, b):
    return jnp.dot(a, b, preferred_element_type=f32)


def iota(shape, dim):
    return lax.broadcasted_iota(i32, shape, dim)


def unit(values):
    return values * lax.rsqrt(jnp.mean(values * values, axis=-1, keepdims=True) + eps_norm)


def pick_kernel(index, pool, out, sem):
    def send(i, carry):
        page = jnp.clip(index[0, i], 0, pool.shape[0] - 1)
        pltpu.make_async_copy(pool.at[page], out.at[i], sem).start()
        return carry

    lax.fori_loop(0, out.shape[0], send, 0, unroll=8)
    pltpu.make_async_copy(out, out, sem).wait()


def pick_pages(index, pool):
    count = index.shape[1]
    return pl.pallas_call(
        pick_kernel,
        in_specs=[SMEM, HBM],
        out_specs=HBM,
        out_shape=jax.ShapeDtypeStruct((count,) + pool.shape[1:], pool.dtype),
        scratch_shapes=[pltpu.SemaphoreType.DMA],
        cost_estimate=pl.CostEstimate(flops=0, transcendentals=0, bytes_accessed=4 << 20),
        name="pick_pages",
    )(index, pool)


def project_kernel(
    length, accepted, x, draft, gain, wq, wkv, qk_gain, cosine, sine, table,
    queries, prompt_kv, sent, draft_kv, own_count, verify_kv,
    weights, normed, wide, rows_q, sems,
):
    rows, drafted = x.shape[0], draft.shape[1]
    copies = []
    for h in range(QH + 2):
        part = wq if h < QH else wkv
        col = (h if h < QH else h - QH) * HEAD
        copy = pltpu.make_async_copy(part.at[:, col : col + HEAD], weights.at[h], sems.at[h])
        copy.start()
        copies.append(copy)

    normed[:rows] = (unit(x[...].astype(f32)) * gain[...]).astype(bf16)
    wide[...] = jnp.zeros_like(wide)
    wide[:drafted] = unit(draft[0].astype(f32)) * gain[...]
    normed[rows:] = wide[...].astype(bf16)

    slots = table.shape[1]
    eye = iota((slots, slots), 0) == iota((slots, slots), 1)
    page = jnp.sum(jnp.where(eye, table[...], 0), axis=1, keepdims=True)
    base = iota((slots, 1), 0) * PAGE

    def tally(lanes, first, step):
        lane = iota((slots, lanes), 1)
        named = page == first + (lane // PAGE) * step
        valid = base + lane % PAGE < length[0]
        return jnp.sum(jnp.where(named & valid, 1.0, 0.0), axis=0, keepdims=True)

    own = own_count.shape[1]
    own_count[...] = tally(own, 0, 1)
    far = [tally(HEAD, own // PAGE + z, DEEP) for z in range(DEEP)]

    half = HEAD // 2
    cos, sin = cosine[...], sine[...]

    def rotated(values):
        a, b = values[:, :half], values[:, half:]
        return jnp.concatenate([a * cos - b * sin, b * cos + a * sin], axis=-1)

    row = iota((PAD, HEAD), 0)
    for h in range(QH):
        copies[h].wait()
        query = rotated(unit(dot_n(normed[...], weights[h])) * qk_gain[0:1, :])
        queries[h] = query[:rows].astype(bf16)
        mine = query[rows : rows + PAD]
        mine = jnp.where(row == drafted, far[h], mine)
        mine = jnp.where(row == drafted + 1, far[h + QH], mine)
        rows_q[h * PAD : (h + 1) * PAD, :] = mine
    sent[...] = rows_q[...].astype(bf16)

    keep = iota((PAD, HEAD), 0) < accepted[0]
    for part in range(2):
        copies[QH + part].wait()
        value = unit(dot_n(normed[...], weights[QH + part]))
        if part == 0:
            value = rotated(value * qk_gain[1:2, :])
        cols = slice(part * HEAD, (part + 1) * HEAD)
        prompt_kv[:, cols] = value[:rows].astype(bf16)
        mine = value[rows : rows + PAD]
        draft_kv[:, cols] = mine
        verify_kv[0, :, cols] = jnp.where(keep, mine, 0.0)[:drafted].astype(bf16)


def project(length, accepted, x, draft, gain, wq, wkv, qk_gain, cosine, sine, table, own):
    rows, width = x.shape
    drafted = draft.shape[1]
    total = rows + 16
    shapes = [
        jax.ShapeDtypeStruct((QH, rows, HEAD), bf16),
        jax.ShapeDtypeStruct((rows, 2 * HEAD), bf16),
        jax.ShapeDtypeStruct((QH * PAD, HEAD), bf16),
        jax.ShapeDtypeStruct((PAD, 2 * HEAD), f32),
        jax.ShapeDtypeStruct((1, own), f32),
        jax.ShapeDtypeStruct((1, drafted, 2 * HEAD), bf16),
    ]
    return pl.pallas_call(
        project_kernel,
        in_specs=[SMEM, SMEM, VMEM, VMEM, VMEM, HBM, HBM, VMEM, VMEM, VMEM, VMEM],
        out_specs=[VMEM] * len(shapes),
        out_shape=shapes,
        scratch_shapes=[
            pltpu.VMEM((QH + 2, width, HEAD), bf16),
            pltpu.VMEM((total, width), bf16),
            pltpu.VMEM((16, width), f32),
            pltpu.VMEM((QH * PAD, HEAD), f32),
            pltpu.SemaphoreType.DMA((QH + 2,)),
        ],
        compiler_params=pltpu.CompilerParams(vmem_limit_bytes=24 << 20),
        cost_estimate=pl.CostEstimate(
            flops=2 * total * width * 6 * HEAD, transcendentals=0, bytes_accessed=9 << 20
        ),
        name="project",
    )(length, accepted, x, draft, gain, wq, wkv, qk_gain, cosine, sine, table)


def prompt_kernel(
    lengths, q, kv, w_out, query, draft_kv, pool, count, out, local, attn, weights, sem
):
    copy = pltpu.make_async_copy(w_out, weights, sem)
    copy.start()
    rows = attn.shape[0]
    row, col = iota((rows, rows), 0), iota((rows, rows), 1)
    start = jnp.zeros((rows, rows), i32)
    end = jnp.int32(0)
    for i in range(3):
        end = end + lengths[0, i]
        start = jnp.where(row >= end, end, start)
    allowed = (col <= row) & (col >= start)
    key, value = kv[:, :HEAD], kv[:, HEAD:]
    for h in range(QH):
        scores = jnp.where(allowed, dot_t(q[h], key), neg_large)
        parts = jnp.exp(scores - jnp.max(scores, axis=-1, keepdims=True))
        probs = (parts / jnp.sum(parts, axis=-1, keepdims=True)).astype(bf16)
        attn[:, h * HEAD : (h + 1) * HEAD] = dot_n(probs, value).astype(bf16)

    mine = query[...]
    times = count[...]
    scores = jnp.where(times > 0.0, dot_t(mine, pool[:, :HEAD]), neg_large)
    fresh = dot_t(mine, draft_kv[:, :HEAD].astype(bf16))
    allowed = iota(fresh.shape, 1) <= iota(fresh.shape, 0) % PAD
    fresh = jnp.where(allowed, fresh, neg_large)
    peak = jnp.maximum(
        jnp.max(scores, axis=-1, keepdims=True), jnp.max(fresh, axis=-1, keepdims=True)
    )
    parts = jnp.where(times > 0.0, jnp.exp(scores - peak) * times, 0.0)
    fresh = jnp.where(allowed, jnp.exp(fresh - peak), 0.0)
    denom = jnp.sum(parts, axis=-1, keepdims=True) + jnp.sum(fresh, axis=-1, keepdims=True)
    local[:, :HEAD] = dot_n(parts.astype(bf16), pool[:, HEAD:]) + dot_n(
        fresh.astype(bf16), draft_kv[:, HEAD:].astype(bf16)
    )
    local[:, HEAD : HEAD + 128] = jnp.broadcast_to(peak, (QH * PAD, 128))
    local[:, HEAD + 128 :] = jnp.broadcast_to(denom, (QH * PAD, 128))

    copy.wait()
    cols = 512
    for i in range(out.shape[1] // cols):
        part = slice(i * cols, (i + 1) * cols)
        out[:, part] = dot_n(attn[...], weights[:, part]).astype(bf16)


def prompts(lengths, q, kv, w_out, query, draft_kv, pool, count):
    rows = kv.shape[0]
    depth, width = w_out.shape
    return pl.pallas_call(
        prompt_kernel,
        in_specs=[SMEM, VMEM, VMEM, HBM, VMEM, VMEM, VMEM, VMEM],
        out_specs=[VMEM, VMEM],
        out_shape=[
            jax.ShapeDtypeStruct((rows, width), bf16),
            jax.ShapeDtypeStruct((QH * PAD, 2 * HEAD), f32),
        ],
        scratch_shapes=[
            pltpu.VMEM((rows, depth), bf16),
            pltpu.VMEM((depth, width), bf16),
            pltpu.SemaphoreType.DMA,
        ],
        compiler_params=pltpu.CompilerParams(vmem_limit_bytes=24 << 20),
        cost_estimate=pl.CostEstimate(
            flops=2 * rows * depth * width, transcendentals=4 * rows * rows, bytes_accessed=6 << 20
        ),
        name="prompts",
    )(lengths, q, kv, w_out, query, draft_kv, pool, count)


def remote_kernel(where, queries, pages, out):
    here = where[0]
    groups, rows = queries.shape[0], queries.shape[1]
    pick = iota((rows, HEAD), 0) == (here % QH) * PAD + 5 + here // QH
    asked = [here ^ mask for mask in ORDER]
    scores, counts = [], []
    for e in range(groups):
        query = queries[e]
        count = jnp.sum(jnp.where(pick, query.astype(f32), 0.0), axis=0, keepdims=True)
        held = pages[:, asked[e], :, :HEAD].reshape(HEAD, HEAD)
        scores.append(jnp.where(count > 0.0, dot_t(query, held), neg_large))
        counts.append(jnp.broadcast_to(count, (rows, HEAD)))
    score = jnp.concatenate(scores, axis=0)
    count = jnp.concatenate(counts, axis=0)
    peak = jnp.max(score, axis=-1, keepdims=True).astype(bf16).astype(f32)
    parts = jnp.where(count > 0.0, jnp.exp(score - peak) * count, 0.0)
    denom = jnp.sum(parts, axis=-1, keepdims=True)
    high = denom.astype(bf16).astype(f32)
    lane = iota((groups * rows, 128), 1)
    stats = jnp.where(lane < 32, peak, jnp.where(lane < 64, high, denom - high)).astype(bf16)
    parts = parts.astype(bf16)
    for e in range(groups):
        own = slice(e * rows, (e + 1) * rows)
        held = pages[:, asked[e], :, HEAD:].reshape(HEAD, HEAD)
        out[asked[e], :, :HEAD] = dot_n(parts[own], held).astype(bf16)
        out[asked[e], :, HEAD:] = stats[own]


ORDER = (0, 4, 2, 6, 1, 5, 3, 7)


def remote_pieces(where, queries, pages):
    groups, rows, _ = queries.shape
    return pl.pallas_call(
        remote_kernel,
        in_specs=[SMEM, VMEM, VMEM],
        out_specs=VMEM,
        out_shape=jax.ShapeDtypeStruct((groups, rows, HEAD + 128), bf16),
        compiler_params=pltpu.CompilerParams(vmem_limit_bytes=12 << 20),
        cost_estimate=pl.CostEstimate(flops=1 << 26, transcendentals=1 << 16, bytes_accessed=3 << 20),
        name="remote_pieces",
    )(where, queries, pages)


def join_kernel(pieces, local, w_out, out, attn, weights, sems):
    depth, width = w_out.shape
    parts = sems.shape[0]
    cols = width // parts
    copies = []
    for i in range(parts):
        part = slice(i * cols, (i + 1) * cols)
        copy = pltpu.make_async_copy(w_out.at[:, part], weights.at[:, part], sems.at[i])
        copy.start()
        copies.append(copy)
    groups = pieces.shape[0]
    peaks = [pieces[z, :, HEAD : HEAD + 1].astype(f32) for z in range(groups)]
    own = local[:, HEAD : HEAD + 1]
    top = functools.reduce(jnp.maximum, peaks, own)
    scale = jnp.exp(own - top)
    total = local[:, :HEAD] * scale
    denom = local[:, HEAD + 128 : HEAD + 129] * scale
    for z in range(groups):
        scale = jnp.exp(peaks[z] - top)
        total += pieces[z, :, :HEAD].astype(f32) * scale
        denom += scale * (
            pieces[z, :, HEAD + 32 : HEAD + 33].astype(f32)
            + pieces[z, :, HEAD + 64 : HEAD + 65].astype(f32)
        )
    attn[...] = total / denom
    heads = [attn[h * PAD : (h + 1) * PAD, :].astype(bf16) for h in range(QH)]
    for i in range(parts):
        copies[i].wait()
        part = slice(i * cols, (i + 1) * cols)
        out[:, part] = functools.reduce(
            jnp.add,
            [dot_n(heads[h], weights[h * HEAD : (h + 1) * HEAD, part]) for h in range(QH)],
        )


def join(pieces, local, w_out):
    depth, width = w_out.shape
    return pl.pallas_call(
        join_kernel,
        in_specs=[VMEM, VMEM, HBM],
        out_specs=VMEM,
        out_shape=jax.ShapeDtypeStruct((PAD, width), f32),
        scratch_shapes=[
            pltpu.VMEM((QH * PAD, HEAD), f32),
            pltpu.VMEM((depth, width), bf16),
            pltpu.SemaphoreType.DMA((4,)),
        ],
        compiler_params=pltpu.CompilerParams(vmem_limit_bytes=12 << 20),
        cost_estimate=pl.CostEstimate(flops=1 << 25, transcendentals=0, bytes_accessed=4 << 20),
        name="join",
    )(pieces, local, w_out)


def finish_kernel(side, own, other, x, gain, out):
    half = out.shape[-1]
    total = own[...].astype(f32) + other[...].astype(f32)
    scale = lax.rsqrt(jnp.mean(total * total, axis=-1, keepdims=True) + eps_norm)
    mine = jnp.where(side[0] == 0, total[:, :half], total[:, half:]) * scale * gain[...]
    if len(out.shape) == 3:
        out[0] = (x[0].astype(f32) + mine[: out.shape[1]]).astype(bf16)
    else:
        out[...] = (x[...].astype(f32) + mine).astype(bf16)


def finish(side, own, other, x, gain, name):
    rows, width = own.shape
    half = width // 2
    block = min(rows, 128)
    if x.ndim == 3:
        shape = x.shape[:2] + (half,)
        x_spec = pl.BlockSpec(shape, lambda i, s: (0, 0, s[0]))
        o_spec = pl.BlockSpec(shape, lambda i, s: (0, 0, 0))
    else:
        shape = (rows, half)
        x_spec = pl.BlockSpec((block, half), lambda i, s: (i, s[0]))
        o_spec = pl.BlockSpec((block, half), lambda i, s: (i, 0))
    return pl.pallas_call(
        finish_kernel,
        grid_spec=pltpu.PrefetchScalarGridSpec(
            num_scalar_prefetch=1,
            grid=(rows // block,),
            in_specs=[
                pl.BlockSpec((block, width), lambda i, s: (i, 0)),
                pl.BlockSpec((block, width), lambda i, s: (i, 0)),
                x_spec,
                pl.BlockSpec((1, half), lambda i, s: (0, s[0])),
            ],
            out_specs=o_spec,
        ),
        out_shape=jax.ShapeDtypeStruct(shape, bf16),
        compiler_params=pltpu.CompilerParams(vmem_limit_bytes=12 << 20),
        cost_estimate=pl.CostEstimate(
            flops=8 * rows * width, transcendentals=0, bytes_accessed=6 * rows * width
        ),
        name=name,
    )(side, own, other, x, gain)


def on_device(
    plane,
    verify_x,
    prefill_x,
    attn_gain,
    w_query,
    w_keyval,
    qk_gain,
    w_out,
    post_gain,
    page_pool,
    outbound,
    page_table,
    cache_len,
    prompt_len,
    accepted,
):
    devices = outbound.shape[1]
    rows = prefill_x.shape[0]
    pool_pages = page_pool.shape[0]
    planes = len(plane[0])
    column = [list(range(i, i + DEEP)) for i in range(0, devices, DEEP)]

    outgoing = pick_pages(outbound, page_pool)
    outgoing, prefill_x = lax.optimization_barrier((outgoing, prefill_x))
    arrived = lax.all_to_all(outgoing, "req", 0, 0, tiled=True, axis_index_groups=plane)

    lengths = prompt_len[0]
    order = jnp.arange(3, dtype=i32)[:, None] >= jnp.arange(4, dtype=i32)[None, :]
    ends = jnp.sum(jnp.where(order, lengths[None, :], 0), axis=1)
    row = jnp.arange(rows, dtype=i32)
    start = jnp.max(jnp.where(row[:, None] >= ends[None, :], ends[None, :], 0), axis=1)
    position = jnp.concatenate(
        [row - start, cache_len[0] + jnp.arange(16, dtype=i32)]
    ).astype(f32)
    inv_freq = rope_base ** (-(jnp.arange(HEAD // 2, dtype=f32) * 2.0) / HEAD)
    angles = position[:, None] * inv_freq[None, :]

    queries, prefill_kv, sent, draft_kv, own_count, verify_kv = project(
        cache_len, accepted, prefill_x, verify_x, attn_gain[None], w_query, w_keyval,
        qk_gain, jnp.cos(angles), jnp.sin(angles), page_table, pool_pages * PAGE,
    )

    asked = sent[None]
    for mask in (4, 2, 1):
        pairs = [(i, i ^ mask) for i in range(devices)]
        asked = jnp.concatenate([asked, lax.ppermute(asked, "req", pairs)], axis=0)

    side = lax.axis_index("head").reshape(1)
    where = (lax.axis_index("req") % DEEP).reshape(1)
    swap = [(0, 1), (1, 0)]
    partial, own = prompts(
        prompt_len, queries, prefill_kv, w_out, sent, draft_kv,
        page_pool.reshape(pool_pages * PAGE, -1), own_count,
    )
    other = lax.ppermute(partial, "head", swap)
    prefill_out = finish(side, partial, other, prefill_x, post_gain[None], "finish_prompts")

    arrived, prefill_out = lax.optimization_barrier((arrived, prefill_out))
    pieces = remote_pieces(where, asked, arrived.reshape(planes, DEEP, PAGE, -1))
    pieces = lax.all_to_all(pieces, "req", 0, 0, tiled=True, axis_index_groups=column)
    partial = join(pieces, own, w_out)
    other = lax.ppermute(partial, "head", swap)
    verify_out = finish(side, partial, other, verify_x, post_gain[None], "finish_drafts")
    return (verify_out, prefill_out, verify_kv, prefill_kv)


def solution(mesh):
    devices = mesh.shape["req"]
    plane = [list(range(z, devices, DEEP)) for z in range(DEEP)]
    placed = (
        P("req", None, None),
        P("req", None),
        P(),
        P(None, "head"),
        P(None, "head"),
        P(),
        P("head", None),
        P(),
        P("req", None, "head"),
        P("req", None),
        P("req", None),
        P("req"),
        P("req", None),
        P("req"),
    )
    return jax.shard_map(
        functools.partial(on_device, plane),
        mesh=mesh,
        in_specs=placed,
        out_specs=(
            P("req", None, "head"),
            P("req", "head"),
            P("req", None, "head"),
            P("req", "head"),
        ),
        check_vma=False,
    )
```

```python
import functools

import jax
import jax.numpy as jnp
from jax import lax
from jax.experimental import pallas as pl
from jax.experimental.pallas import tpu as pltpu
from jax.sharding import PartitionSpec as P

HEAD = 256
PAGE = 16
QH = 4
PAD = 8
DEEP = 8
eps_norm = 1e-06
rope_base = 1000000.0
neg_large = -1e30
BIG = 52 << 20
bf16, f32, i32 = jnp.bfloat16, jnp.float32, jnp.int32
HBM = pl.BlockSpec(memory_space=pltpu.MemorySpace.HBM)
VMEM = pl.BlockSpec(memory_space=pltpu.MemorySpace.VMEM)
SMEM = pl.BlockSpec(memory_space=pltpu.MemorySpace.SMEM)


def dot_t(a, b):
    return lax.dot_general(a, b, (((1,), (1,)), ((), ())), preferred_element_type=f32)


def dot_n(a, b):
    return jnp.dot(a, b, preferred_element_type=f32)


def iota(shape, dim):
    return lax.broadcasted_iota(i32, shape, dim)


def unit(values):
    return values * lax.rsqrt(jnp.mean(values * values, axis=-1, keepdims=True) + eps_norm)


def pick_kernel(index, pool, out):
    for i in range(out.shape[0]):
        out[i] = pool[jnp.clip(index[0, i], 0, pool.shape[0] - 1)]


def pick_pages(index, pool):
    count = index.shape[1]
    return pl.pallas_call(
        pick_kernel,
        in_specs=[SMEM, VMEM],
        out_specs=VMEM,
        out_shape=jax.ShapeDtypeStruct((count,) + pool.shape[1:], pool.dtype),
        cost_estimate=pl.CostEstimate(flops=0, transcendentals=0, bytes_accessed=4 << 20),
        name="pick_pages",
    )(index, pool)


def project_kernel(
    length, accepted, x, draft, gain, wq, wkv, qk_gain, cosine, sine, table,
    queries, prompt_kv, sent, draft_kv, own_count, verify_kv,
    weights, normed, wide, rows_q, sems,
):
    rows, drafted = x.shape[0], draft.shape[1]
    copies = []
    for h in range(QH + 2):
        part = wq if h < QH else wkv
        col = (h if h < QH else h - QH) * HEAD
        copy = pltpu.make_async_copy(part.at[:, col : col + HEAD], weights.at[h], sems.at[h])
        copy.start()
        copies.append(copy)

    normed[:rows] = (unit(x[...].astype(f32)) * gain[...]).astype(bf16)
    wide[...] = jnp.zeros_like(wide)
    wide[:drafted] = unit(draft[0].astype(f32)) * gain[...]
    normed[rows:] = wide[...].astype(bf16)

    slots = table.shape[1]
    eye = iota((slots, slots), 0) == iota((slots, slots), 1)
    page = jnp.sum(jnp.where(eye, table[...], 0), axis=1, keepdims=True)
    base = iota((slots, 1), 0) * PAGE

    def tally(lanes, first, step):
        lane = iota((slots, lanes), 1)
        named = page == first + (lane >> 4) * step
        valid = base + (lane & (PAGE - 1)) < length[0]
        return jnp.sum(jnp.where(named & valid, 1.0, 0.0), axis=0, keepdims=True)

    own = own_count.shape[1]
    own_count[...] = tally(own, 0, 1)
    far = [tally(HEAD, own // PAGE + z, DEEP) for z in range(DEEP)]

    half = HEAD // 2
    cos, sin = cosine[...], sine[...]

    def rotated(values):
        a, b = values[:, :half], values[:, half:]
        return jnp.concatenate([a * cos - b * sin, b * cos + a * sin], axis=-1)

    row = iota((PAD, HEAD), 0)
    for h in range(QH):
        copies[h].wait()
        query = rotated(unit(dot_n(normed[...], weights[h])) * qk_gain[0:1, :])
        queries[h] = query[:rows].astype(bf16)
        mine = query[rows : rows + PAD]
        mine = jnp.where(row == drafted, far[h], mine)
        mine = jnp.where(row == drafted + 1, far[h + QH], mine)
        rows_q[h * PAD : (h + 1) * PAD, :] = mine
    sent[...] = rows_q[...].astype(bf16)

    keep = iota((PAD, HEAD), 0) < accepted[0]
    for part in range(2):
        copies[QH + part].wait()
        value = unit(dot_n(normed[...], weights[QH + part]))
        if part == 0:
            value = rotated(value * qk_gain[1:2, :])
        cols = slice(part * HEAD, (part + 1) * HEAD)
        prompt_kv[:, cols] = value[:rows].astype(bf16)
        mine = value[rows : rows + PAD]
        draft_kv[:, cols] = mine
        verify_kv[0, :, cols] = jnp.where(keep, mine, 0.0)[:drafted].astype(bf16)


def project(length, accepted, x, draft, gain, wq, wkv, qk_gain, cosine, sine, table, own):
    rows, width = x.shape
    drafted = draft.shape[1]
    total = rows + 16
    shapes = [
        jax.ShapeDtypeStruct((QH, rows, HEAD), bf16),
        jax.ShapeDtypeStruct((rows, 2 * HEAD), bf16),
        jax.ShapeDtypeStruct((QH * PAD, HEAD), bf16),
        jax.ShapeDtypeStruct((PAD, 2 * HEAD), f32),
        jax.ShapeDtypeStruct((1, own), f32),
        jax.ShapeDtypeStruct((1, drafted, 2 * HEAD), bf16),
    ]
    return pl.pallas_call(
        project_kernel,
        in_specs=[SMEM, SMEM, VMEM, VMEM, VMEM, HBM, HBM, VMEM, VMEM, VMEM, VMEM],
        out_specs=[VMEM] * len(shapes),
        out_shape=shapes,
        scratch_shapes=[
            pltpu.VMEM((QH + 2, width, HEAD), bf16),
            pltpu.VMEM((total, width), bf16),
            pltpu.VMEM((16, width), f32),
            pltpu.VMEM((QH * PAD, HEAD), f32),
            pltpu.SemaphoreType.DMA((QH + 2,)),
        ],
        compiler_params=pltpu.CompilerParams(vmem_limit_bytes=BIG),
        cost_estimate=pl.CostEstimate(
            flops=2 * total * width * 6 * HEAD, transcendentals=0, bytes_accessed=9 << 20
        ),
        name="project",
    )(length, accepted, x, draft, gain, wq, wkv, qk_gain, cosine, sine, table)


def prompt_kernel(lengths, q, kv, query, draft_kv, pool, count, attn, local):
    rows = attn.shape[0]
    row, col = iota((rows, rows), 0), iota((rows, rows), 1)
    start = jnp.zeros((rows, rows), i32)
    end = jnp.int32(0)
    for i in range(3):
        end = end + lengths[0, i]
        start = jnp.where(row >= end, end, start)
    allowed = (col <= row) & (col >= start)
    key, value = kv[:, :HEAD], kv[:, HEAD:]
    for h in range(QH):
        scores = jnp.where(allowed, dot_t(q[h], key), neg_large)
        parts = jnp.exp(scores - jnp.max(scores, axis=-1, keepdims=True))
        probs = (parts / jnp.sum(parts, axis=-1, keepdims=True)).astype(bf16)
        attn[:, h * HEAD : (h + 1) * HEAD] = dot_n(probs, value).astype(bf16)

    mine = query[...]
    times = count[...]
    scores = jnp.where(times > 0.0, dot_t(mine, pool[:, :HEAD]), neg_large)
    fresh = dot_t(mine, draft_kv[:, :HEAD].astype(bf16))
    allowed = iota(fresh.shape, 1) <= (iota(fresh.shape, 0) & (PAD - 1))
    fresh = jnp.where(allowed, fresh, neg_large)
    peak = jnp.maximum(
        jnp.max(scores, axis=-1, keepdims=True), jnp.max(fresh, axis=-1, keepdims=True)
    )
    parts = jnp.where(times > 0.0, jnp.exp(scores - peak) * times, 0.0)
    fresh = jnp.where(allowed, jnp.exp(fresh - peak), 0.0)
    denom = jnp.sum(parts, axis=-1, keepdims=True) + jnp.sum(fresh, axis=-1, keepdims=True)
    local[:, :HEAD] = dot_n(parts.astype(bf16), pool[:, HEAD:]) + dot_n(
        fresh.astype(bf16), draft_kv[:, HEAD:].astype(bf16)
    )
    local[:, HEAD : HEAD + 128] = jnp.broadcast_to(peak, (QH * PAD, 128))
    local[:, HEAD + 128 :] = jnp.broadcast_to(denom, (QH * PAD, 128))


def prompts(lengths, q, kv, query, draft_kv, pool, count):
    rows = kv.shape[0]
    return pl.pallas_call(
        prompt_kernel,
        in_specs=[SMEM] + [VMEM] * 6,
        out_specs=[VMEM, VMEM],
        out_shape=[
            jax.ShapeDtypeStruct((rows, QH * HEAD), bf16),
            jax.ShapeDtypeStruct((QH * PAD, 2 * HEAD), f32),
        ],
        compiler_params=pltpu.CompilerParams(vmem_limit_bytes=16 << 20),
        cost_estimate=pl.CostEstimate(
            flops=16 * rows * rows * HEAD, transcendentals=4 * rows * rows, bytes_accessed=4 << 20
        ),
        name="prompts",
    )(lengths, q, kv, query, draft_kv, pool, count)


def spread_kernel(attn, w_out, out, weights, sems):
    parts = sems.shape[0]
    cols = out.shape[1] // parts
    copies = []
    for i in range(parts):
        part = slice(i * cols, (i + 1) * cols)
        copy = pltpu.make_async_copy(w_out.at[:, part], weights.at[:, part], sems.at[i])
        copy.start()
        copies.append(copy)
    for i in range(parts):
        copies[i].wait()
        part = slice(i * cols, (i + 1) * cols)
        out[:, part] = dot_n(attn[...], weights[:, part]).astype(bf16)


def spread(attn, w_out):
    rows = attn.shape[0]
    depth, width = w_out.shape
    return pl.pallas_call(
        spread_kernel,
        in_specs=[VMEM, HBM],
        out_specs=VMEM,
        out_shape=jax.ShapeDtypeStruct((rows, width), bf16),
        scratch_shapes=[pltpu.VMEM((depth, width), bf16), pltpu.SemaphoreType.DMA((4,))],
        compiler_params=pltpu.CompilerParams(vmem_limit_bytes=BIG),
        cost_estimate=pl.CostEstimate(
            flops=2 * rows * depth * width, transcendentals=0, bytes_accessed=6 << 20
        ),
        name="spread",
    )(attn, w_out)


def remote_kernel(where, queries, pages, out):
    here = where[0]
    groups, rows = queries.shape[0], queries.shape[1]
    pick = iota((rows, HEAD), 0) == (here % QH) * PAD + 5 + here // QH
    asked = [here ^ mask for mask in ORDER]
    scores, counts = [], []
    for e in range(groups):
        query = queries[e]
        count = jnp.sum(jnp.where(pick, query.astype(f32), 0.0), axis=0, keepdims=True)
        held = pages[:, asked[e], :, :HEAD].reshape(HEAD, HEAD)
        scores.append(jnp.where(count > 0.0, dot_t(query, held), neg_large))
        counts.append(jnp.broadcast_to(count, (rows, HEAD)))
    score = jnp.concatenate(scores, axis=0)
    count = jnp.concatenate(counts, axis=0)
    peak = jnp.max(score, axis=-1, keepdims=True).astype(bf16).astype(f32)
    parts = jnp.where(count > 0.0, jnp.exp(score - peak) * count, 0.0)
    denom = jnp.sum(parts, axis=-1, keepdims=True)
    high = denom.astype(bf16).astype(f32)
    lane = iota((groups * rows, 128), 1)
    stats = jnp.where(lane < 32, peak, jnp.where(lane < 64, high, denom - high)).astype(bf16)
    parts = parts.astype(bf16)
    for e in range(groups):
        own = slice(e * rows, (e + 1) * rows)
        held = pages[:, asked[e], :, HEAD:].reshape(HEAD, HEAD)
        out[asked[e], :, :HEAD] = dot_n(parts[own], held).astype(bf16)
        out[asked[e], :, HEAD:] = stats[own]


ORDER = (0, 4, 2, 6, 1, 5, 3, 7)


def remote_pieces(where, queries, pages):
    groups, rows, _ = queries.shape
    return pl.pallas_call(
        remote_kernel,
        in_specs=[SMEM, VMEM, VMEM],
        out_specs=VMEM,
        out_shape=jax.ShapeDtypeStruct((groups, rows, HEAD + 128), bf16),
        compiler_params=pltpu.CompilerParams(vmem_limit_bytes=12 << 20),
        cost_estimate=pl.CostEstimate(flops=1 << 26, transcendentals=1 << 16, bytes_accessed=3 << 20),
        name="remote_pieces",
    )(where, queries, pages)


def join_kernel(pieces, local, w_out, out, attn, weights, sems):
    depth, width = w_out.shape
    parts = sems.shape[0]
    cols = width // parts
    copies = []
    for i in range(parts):
        part = slice(i * cols, (i + 1) * cols)
        copy = pltpu.make_async_copy(w_out.at[:, part], weights.at[:, part], sems.at[i])
        copy.start()
        copies.append(copy)
    groups = pieces.shape[0]
    peaks = [pieces[z, :, HEAD : HEAD + 1].astype(f32) for z in range(groups)]
    own = local[:, HEAD : HEAD + 1]
    top = functools.reduce(jnp.maximum, peaks, own)
    scale = jnp.exp(own - top)
    total = local[:, :HEAD] * scale
    denom = local[:, HEAD + 128 : HEAD + 129] * scale
    for z in range(groups):
        scale = jnp.exp(peaks[z] - top)
        total += pieces[z, :, :HEAD].astype(f32) * scale
        denom += scale * (
            pieces[z, :, HEAD + 32 : HEAD + 33].astype(f32)
            + pieces[z, :, HEAD + 64 : HEAD + 65].astype(f32)
        )
    attn[...] = total / denom
    heads = [attn[h * PAD : (h + 1) * PAD, :].astype(bf16) for h in range(QH)]
    for i in range(parts):
        copies[i].wait()
        part = slice(i * cols, (i + 1) * cols)
        out[:, part] = functools.reduce(
            jnp.add,
            [dot_n(heads[h], weights[h * HEAD : (h + 1) * HEAD, part]) for h in range(QH)],
        )


def join(pieces, local, w_out):
    depth, width = w_out.shape
    return pl.pallas_call(
        join_kernel,
        in_specs=[VMEM, VMEM, HBM],
        out_specs=VMEM,
        out_shape=jax.ShapeDtypeStruct((PAD, width), f32),
        scratch_shapes=[
            pltpu.VMEM((QH * PAD, HEAD), f32),
            pltpu.VMEM((depth, width), bf16),
            pltpu.SemaphoreType.DMA((4,)),
        ],
        compiler_params=pltpu.CompilerParams(vmem_limit_bytes=BIG),
        cost_estimate=pl.CostEstimate(flops=1 << 25, transcendentals=0, bytes_accessed=4 << 20),
        name="join",
    )(pieces, local, w_out)


def finish_kernel(side, own, other, x, gain, out):
    half = out.shape[-1]
    total = own[...].astype(f32) + other[...].astype(f32)
    scale = lax.rsqrt(jnp.mean(total * total, axis=-1, keepdims=True) + eps_norm)
    mine = jnp.where(side[0] == 0, total[:, :half], total[:, half:]) * scale * gain[...]
    if len(out.shape) == 3:
        out[0] = (x[0].astype(f32) + mine[: out.shape[1]]).astype(bf16)
    else:
        out[...] = (x[...].astype(f32) + mine).astype(bf16)


def finish(side, own, other, x, gain, name):
    rows, width = own.shape
    half = width // 2
    block = min(rows, 128)
    if x.ndim == 3:
        shape = x.shape[:2] + (half,)
        x_spec = pl.BlockSpec(shape, lambda i, s: (0, 0, s[0]))
        o_spec = pl.BlockSpec(shape, lambda i, s: (0, 0, 0))
    else:
        shape = (rows, half)
        x_spec = pl.BlockSpec((block, half), lambda i, s: (i, s[0]))
        o_spec = pl.BlockSpec((block, half), lambda i, s: (i, 0))
    return pl.pallas_call(
        finish_kernel,
        grid_spec=pltpu.PrefetchScalarGridSpec(
            num_scalar_prefetch=1,
            grid=(rows // block,),
            in_specs=[
                pl.BlockSpec((block, width), lambda i, s: (i, 0)),
                pl.BlockSpec((block, width), lambda i, s: (i, 0)),
                x_spec,
                pl.BlockSpec((1, half), lambda i, s: (0, s[0])),
            ],
            out_specs=o_spec,
        ),
        out_shape=jax.ShapeDtypeStruct(shape, bf16),
        compiler_params=pltpu.CompilerParams(vmem_limit_bytes=12 << 20),
        cost_estimate=pl.CostEstimate(
            flops=8 * rows * width, transcendentals=0, bytes_accessed=6 * rows * width
        ),
        name=name,
    )(side, own, other, x, gain)


def on_device(
    plane,
    verify_x,
    prefill_x,
    attn_gain,
    w_query,
    w_keyval,
    qk_gain,
    w_out,
    post_gain,
    page_pool,
    outbound,
    page_table,
    cache_len,
    prompt_len,
    accepted,
):
    devices = outbound.shape[1]
    rows = prefill_x.shape[0]
    pool_pages = page_pool.shape[0]
    planes = len(plane[0])
    column = [list(range(i, i + DEEP)) for i in range(0, devices, DEEP)]

    outgoing = pick_pages(outbound, page_pool)
    outgoing, prefill_x = lax.optimization_barrier((outgoing, prefill_x))
    arrived = lax.all_to_all(outgoing, "req", 0, 0, tiled=True, axis_index_groups=plane)

    lengths = prompt_len[0]
    order = jnp.arange(3, dtype=i32)[:, None] >= jnp.arange(4, dtype=i32)[None, :]
    ends = jnp.sum(jnp.where(order, lengths[None, :], 0), axis=1)
    row = jnp.arange(rows, dtype=i32)
    start = jnp.max(jnp.where(row[:, None] >= ends[None, :], ends[None, :], 0), axis=1)
    position = jnp.concatenate(
        [row - start, cache_len[0] + jnp.arange(16, dtype=i32)]
    ).astype(f32)
    inv_freq = rope_base ** (-(jnp.arange(HEAD // 2, dtype=f32) * 2.0) / HEAD)
    angles = position[:, None] * inv_freq[None, :]

    queries, prefill_kv, sent, draft_kv, own_count, verify_kv = project(
        cache_len, accepted, prefill_x, verify_x, attn_gain[None], w_query, w_keyval,
        qk_gain, jnp.cos(angles), jnp.sin(angles), page_table, pool_pages * PAGE,
    )

    side = lax.axis_index("head").reshape(1)
    where = (lax.axis_index("req") & (DEEP - 1)).reshape(1)
    swap = [(0, 1), (1, 0)]

    def beside(values, mask):
        pairs = [(i, i ^ mask) for i in range(devices)]
        return jnp.concatenate([values, lax.ppermute(values, "req", pairs)], axis=0)

    asked = beside(sent[None], 4)
    attn, own = prompts(
        prompt_len, queries, prefill_kv, sent, draft_kv,
        page_pool.reshape(pool_pages * PAGE, -1), own_count,
    )
    asked, attn = lax.optimization_barrier((asked, attn))
    asked = beside(asked, 2)
    partial = spread(attn, w_out)
    asked, partial = lax.optimization_barrier((asked, partial))
    asked = beside(asked, 1)
    other = lax.ppermute(partial, "head", swap)
    pieces = remote_pieces(where, asked, arrived.reshape(planes, DEEP, PAGE, -1))
    pieces, other = lax.optimization_barrier((pieces, other))
    prefill_out = finish(side, partial, other, prefill_x, post_gain[None], "finish_prompts")
    pieces = lax.all_to_all(pieces, "req", 0, 0, tiled=True, axis_index_groups=column)
    pieces, prefill_out = lax.optimization_barrier((pieces, prefill_out))
    partial = join(pieces, own, w_out)
    other = lax.ppermute(partial, "head", swap)
    verify_out = finish(side, partial, other, verify_x, post_gain[None], "finish_drafts")
    return (verify_out, prefill_out, verify_kv, prefill_kv)


def solution(mesh):
    devices = mesh.shape["req"]
    plane = [list(range(z, devices, DEEP)) for z in range(DEEP)]
    placed = (
        P("req", None, None),
        P("req", None),
        P(),
        P(None, "head"),
        P(None, "head"),
        P(),
        P("head", None),
        P(),
        P("req", None, "head"),
        P("req", None),
        P("req", None),
        P("req"),
        P("req", None),
        P("req"),
    )
    return jax.shard_map(
        functools.partial(on_device, plane),
        mesh=mesh,
        in_specs=placed,
        out_specs=(
            P("req", None, "head"),
            P("req", "head"),
            P("req", None, "head"),
            P("req", "head"),
        ),
        check_vma=False,
    )
```

```python
import functools

import jax
import jax.numpy as jnp
from jax import lax
from jax.experimental import pallas as pl
from jax.experimental.pallas import tpu as pltpu
from jax.sharding import PartitionSpec as P

HEAD = 256
PAGE = 16
QH = 4
PAD = 8
DEEP = 8
eps_norm = 1e-06
rope_base = 1000000.0
neg_large = -1e30
BIG = 52 << 20
bf16, f32, i32 = jnp.bfloat16, jnp.float32, jnp.int32
HBM = pl.BlockSpec(memory_space=pltpu.MemorySpace.HBM)
VMEM = pl.BlockSpec(memory_space=pltpu.MemorySpace.VMEM)
SMEM = pl.BlockSpec(memory_space=pltpu.MemorySpace.SMEM)


def dot_t(a, b):
    return lax.dot_general(a, b, (((1,), (1,)), ((), ())), preferred_element_type=f32)


def dot_n(a, b):
    return jnp.dot(a, b, preferred_element_type=f32)


def iota(shape, dim):
    return lax.broadcasted_iota(i32, shape, dim)


def unit(values):
    return values * lax.rsqrt(jnp.mean(values * values, axis=-1, keepdims=True) + eps_norm)


def pick_kernel(index, pool, out):
    for i in range(out.shape[0]):
        out[i] = pool[jnp.clip(index[0, i], 0, pool.shape[0] - 1)]


def pick_pages(index, pool):
    count = index.shape[1]
    return pl.pallas_call(
        pick_kernel,
        in_specs=[SMEM, VMEM],
        out_specs=VMEM,
        out_shape=jax.ShapeDtypeStruct((count,) + pool.shape[1:], pool.dtype),
        cost_estimate=pl.CostEstimate(flops=0, transcendentals=0, bytes_accessed=4 << 20),
        name="pick_pages",
    )(index, pool)


def project_kernel(
    meta, x, draft, gain, wq, wkv, qk_gain, cosine, sine, table,
    queries, prompt_kv, near_kv, sent, draft_kv, own_count, verify_kv,
    weights, normed, wide, rows_q, sems,
):
    rows, drafted = x.shape[0], draft.shape[1]
    copies = []
    for h in range(3):
        part = wq.at[:, h * 2 * HEAD : (h + 1) * 2 * HEAD] if h < 2 else wkv
        copy = pltpu.make_async_copy(part, weights.at[h], sems.at[h])
        copy.start()
        copies.append(copy)

    normed[:rows] = (unit(x[...].astype(f32)) * gain[...]).astype(bf16)
    wide[...] = jnp.zeros_like(wide)
    wide[:drafted] = unit(draft[0].astype(f32)) * gain[...]
    normed[rows:] = wide[...].astype(bf16)

    slots = table.shape[1]
    eye = iota((slots, slots), 0) == iota((slots, slots), 1)
    page = jnp.sum(jnp.where(eye, table[...], 0), axis=1, keepdims=True)
    base = iota((slots, 1), 0) * PAGE

    def tally(lanes, first, step):
        lane = iota((slots, lanes), 1)
        named = page == first + (lane >> 4) * step
        valid = base + (lane & (PAGE - 1)) < meta[0]
        return jnp.sum(jnp.where(named & valid, 1.0, 0.0), axis=0, keepdims=True)

    own = own_count.shape[1]
    own_count[...] = tally(own, 0, 1)
    far = [tally(HEAD, own // PAGE + z, DEEP) for z in range(DEEP)]

    half = HEAD // 2
    cos, sin = cosine[...], sine[...]

    def rotated(values):
        a, b = values[:, :half], values[:, half:]
        return jnp.concatenate([a * cos - b * sin, b * cos + a * sin], axis=-1)

    row = iota((PAD, HEAD), 0)
    keep = iota((PAD, HEAD), 0) < meta[1]

    for pair in range(3):
        copies[pair].wait()
        both = dot_n(normed[...], weights[pair])
        for j in range(2):
            h = 2 * pair + j
            value = unit(both[:, j * HEAD : (j + 1) * HEAD])
            if h < QH:
                query = rotated(value * qk_gain[0:1, :])
                queries[h] = query[:rows].astype(bf16)
                mine = query[rows : rows + PAD]
                mine = jnp.where(row == drafted, far[h], mine)
                mine = jnp.where(row == drafted + 1, far[h + QH], mine)
                rows_q[h * PAD : (h + 1) * PAD, :] = mine
                continue
            if h == QH:
                value = rotated(value * qk_gain[1:2, :])
            cols = slice(j * HEAD, (j + 1) * HEAD)
            prompt_kv[:, cols] = value[:rows].astype(bf16)
            near_kv[:, cols] = value[:rows].astype(bf16)
            mine = value[rows : rows + PAD]
            draft_kv[:, cols] = mine
            verify_kv[0, :, cols] = jnp.where(keep, mine, 0.0)[:drafted].astype(bf16)
    sent[...] = rows_q[...].astype(bf16)


def project(meta, x, draft, gain, wq, wkv, qk_gain, cosine, sine, table, own):
    rows, width = x.shape
    drafted = draft.shape[1]
    total = rows + 16
    shapes = [
        jax.ShapeDtypeStruct((QH, rows, HEAD), bf16),
        jax.ShapeDtypeStruct((rows, 2 * HEAD), bf16),
        jax.ShapeDtypeStruct((rows, 2 * HEAD), bf16),
        jax.ShapeDtypeStruct((QH * PAD, HEAD), bf16),
        jax.ShapeDtypeStruct((PAD, 2 * HEAD), f32),
        jax.ShapeDtypeStruct((1, own), f32),
        jax.ShapeDtypeStruct((1, drafted, 2 * HEAD), bf16),
    ]
    return pl.pallas_call(
        project_kernel,
        in_specs=[SMEM, VMEM, VMEM, VMEM, HBM, HBM, VMEM, VMEM, VMEM, VMEM],
        out_specs=[VMEM] * len(shapes),
        out_shape=shapes,
        scratch_shapes=[
            pltpu.VMEM((3, width, 2 * HEAD), bf16),
            pltpu.VMEM((total, width), bf16),
            pltpu.VMEM((16, width), f32),
            pltpu.VMEM((QH * PAD, HEAD), f32),
            pltpu.SemaphoreType.DMA((3,)),
        ],
        compiler_params=pltpu.CompilerParams(vmem_limit_bytes=BIG),
        cost_estimate=pl.CostEstimate(
            flops=2 * total * width * 6 * HEAD, transcendentals=0, bytes_accessed=9 << 20
        ),
        name="project",
    )(meta, x, draft, gain, wq, wkv, qk_gain, cosine, sine, table)


def prompt_kernel(lengths, q, kv, query, draft_kv, pool, count, attn, local):
    rows = attn.shape[0]
    row, col = iota((rows, rows), 0), iota((rows, rows), 1)
    start = jnp.zeros((rows, rows), i32)
    end = jnp.int32(0)
    for i in range(3):
        end = end + lengths[0, i]
        start = jnp.where(row >= end, end, start)
    allowed = (col <= row) & (col >= start)
    key, value = kv[:, :HEAD], kv[:, HEAD:]
    for h in range(QH):
        scores = jnp.where(allowed, dot_t(q[h], key), neg_large)
        parts = jnp.exp(scores - jnp.max(scores, axis=-1, keepdims=True))
        probs = (parts / jnp.sum(parts, axis=-1, keepdims=True)).astype(bf16)
        attn[:, h * HEAD : (h + 1) * HEAD] = dot_n(probs, value).astype(bf16)

    mine = query[...]
    times = count[...]
    scores = jnp.where(times > 0.0, dot_t(mine, pool[:, :HEAD]), neg_large)
    fresh = dot_t(mine, draft_kv[:, :HEAD].astype(bf16))
    allowed = iota(fresh.shape, 1) <= (iota(fresh.shape, 0) & (PAD - 1))
    fresh = jnp.where(allowed, fresh, neg_large)
    peak = jnp.maximum(
        jnp.max(scores, axis=-1, keepdims=True), jnp.max(fresh, axis=-1, keepdims=True)
    )
    parts = jnp.where(times > 0.0, jnp.exp(scores - peak) * times, 0.0)
    fresh = jnp.where(allowed, jnp.exp(fresh - peak), 0.0)
    denom = jnp.sum(parts, axis=-1, keepdims=True) + jnp.sum(fresh, axis=-1, keepdims=True)
    local[:, :HEAD] = dot_n(parts.astype(bf16), pool[:, HEAD:]) + dot_n(
        fresh.astype(bf16), draft_kv[:, HEAD:].astype(bf16)
    )
    local[:, HEAD : HEAD + 128] = jnp.broadcast_to(peak, (QH * PAD, 128))
    local[:, HEAD + 128 :] = jnp.broadcast_to(denom, (QH * PAD, 128))


def prompts(lengths, q, kv, query, draft_kv, pool, count):
    rows = kv.shape[0]
    return pl.pallas_call(
        prompt_kernel,
        in_specs=[SMEM] + [VMEM] * 6,
        out_specs=[VMEM, VMEM],
        out_shape=[
            jax.ShapeDtypeStruct((rows, QH * HEAD), bf16),
            jax.ShapeDtypeStruct((QH * PAD, 2 * HEAD), f32),
        ],
        compiler_params=pltpu.CompilerParams(vmem_limit_bytes=16 << 20),
        cost_estimate=pl.CostEstimate(
            flops=16 * rows * rows * HEAD, transcendentals=4 * rows * rows, bytes_accessed=4 << 20
        ),
        name="prompts",
    )(lengths, q, kv, query, draft_kv, pool, count)


def spread_kernel(attn, w_out, out):
    out[...] = dot_n(attn[...], w_out[...]).astype(bf16)


def spread(attn, w_out):
    rows = attn.shape[0]
    depth, width = w_out.shape
    return pl.pallas_call(
        spread_kernel,
        in_specs=[VMEM, VMEM],
        out_specs=VMEM,
        out_shape=jax.ShapeDtypeStruct((rows, width), bf16),
        compiler_params=pltpu.CompilerParams(vmem_limit_bytes=12 << 20),
        cost_estimate=pl.CostEstimate(
            flops=2 * rows * depth * width, transcendentals=0, bytes_accessed=6 << 20
        ),
        name="spread",
    )(attn, w_out)


def remote_kernel(where, queries, pages, out):
    here = where[0]
    groups, rows = queries.shape[0], queries.shape[1]
    pick = iota((rows, HEAD), 0) == (here % QH) * PAD + 5 + here // QH
    asked = [here ^ mask for mask in ORDER]
    scores, counts = [], []
    for e in range(groups):
        query = queries[e]
        count = jnp.sum(jnp.where(pick, query.astype(f32), 0.0), axis=0, keepdims=True)
        held = pages[:, asked[e], :, :HEAD].reshape(HEAD, HEAD)
        scores.append(jnp.where(count > 0.0, dot_t(query, held), neg_large))
        counts.append(jnp.broadcast_to(count, (rows, HEAD)))
    score = jnp.concatenate(scores, axis=0)
    count = jnp.concatenate(counts, axis=0)
    peak = jnp.max(score, axis=-1, keepdims=True).astype(bf16).astype(f32)
    parts = jnp.where(count > 0.0, jnp.exp(score - peak) * count, 0.0)
    denom = jnp.sum(parts, axis=-1, keepdims=True)
    high = denom.astype(bf16).astype(f32)

    shape = (groups * rows // PAD, PAD, 128)
    token, lane = iota(shape, 1), iota(shape, 2)

    def along(values):
        wide = jnp.broadcast_to(values, (groups * rows, 128)).reshape(shape)
        wide = jnp.sum(jnp.where(token == lane, wide, 0.0), axis=1, keepdims=True)
        return jnp.broadcast_to(wide, shape)

    stats = jnp.where(
        token == 5, along(peak), jnp.where(token == 6, along(high), along(denom - high))
    ).reshape(groups * rows, 128)
    spare = (iota((rows, 128), 0) & (PAD - 1)) >= 5
    parts = parts.astype(bf16)
    for e in range(groups):
        own = slice(e * rows, (e + 1) * rows)
        held = pages[:, asked[e], :, HEAD:].reshape(HEAD, HEAD)
        total = dot_n(parts[own], held)
        out[asked[e], :, :128] = jnp.where(spare, stats[own], total[:, :128]).astype(bf16)
        out[asked[e], :, 128:] = total[:, 128:].astype(bf16)


ORDER = (0, 4, 2, 6, 1, 5, 3, 7)


def remote_pieces(where, queries, pages):
    groups, rows, _ = queries.shape
    return pl.pallas_call(
        remote_kernel,
        in_specs=[SMEM, VMEM, VMEM],
        out_specs=VMEM,
        out_shape=jax.ShapeDtypeStruct((groups, rows, HEAD), bf16),
        compiler_params=pltpu.CompilerParams(vmem_limit_bytes=12 << 20),
        cost_estimate=pl.CostEstimate(flops=1 << 26, transcendentals=1 << 16, bytes_accessed=3 << 20),
        name="remote_pieces",
    )(where, queries, pages)


def join_kernel(pieces, local, w_out, out, attn, weights, sems):
    depth, width = w_out.shape
    parts = sems.shape[0]
    cols = width // parts
    copies = []
    for i in range(parts):
        part = slice(i * cols, (i + 1) * cols)
        copy = pltpu.make_async_copy(w_out.at[:, part], weights.at[:, part], sems.at[i])
        copy.start()
        copies.append(copy)
    groups, rows = pieces.shape[0], pieces.shape[1]
    shape = (groups * rows // PAD, PAD, 128)
    token, lane = iota(shape, 1), iota(shape, 2)
    spare = pieces[:, :, :128].astype(f32).reshape(shape)

    def upright(which):
        row = jnp.sum(jnp.where(token == which, spare, 0.0), axis=1, keepdims=True)
        row = jnp.where(token == lane, jnp.broadcast_to(row, shape), 0.0)
        return jnp.sum(row, axis=2, keepdims=True).reshape(groups, rows, 1)

    peaks = upright(5)
    sums = upright(6) + upright(7)
    own = local[:, HEAD : HEAD + 1]
    top = jnp.maximum(jnp.max(peaks, axis=0), own)
    scale = jnp.exp(peaks - top[None])
    near = jnp.exp(own - top)
    total = local[:, :HEAD] * near + jnp.sum(pieces[...].astype(f32) * scale, axis=0)
    denom = local[:, HEAD + 128 : HEAD + 129] * near + jnp.sum(sums * scale, axis=0)
    attn[...] = total / denom
    heads = [attn[h * PAD : (h + 1) * PAD, :].astype(bf16) for h in range(QH)]
    for i in range(parts):
        copies[i].wait()
        part = slice(i * cols, (i + 1) * cols)
        out[:, part] = functools.reduce(
            jnp.add,
            [dot_n(heads[h], weights[h * HEAD : (h + 1) * HEAD, part]) for h in range(QH)],
        )


def join(pieces, local, w_out):
    depth, width = w_out.shape
    return pl.pallas_call(
        join_kernel,
        in_specs=[VMEM, VMEM, HBM],
        out_specs=VMEM,
        out_shape=jax.ShapeDtypeStruct((PAD, width), f32),
        scratch_shapes=[
            pltpu.VMEM((QH * PAD, HEAD), f32),
            pltpu.VMEM((depth, width), bf16),
            pltpu.SemaphoreType.DMA((4,)),
        ],
        compiler_params=pltpu.CompilerParams(vmem_limit_bytes=BIG),
        cost_estimate=pl.CostEstimate(flops=1 << 25, transcendentals=0, bytes_accessed=4 << 20),
        name="join",
    )(pieces, local, w_out)


def finish_kernel(side, own, other, x, gain, out):
    half = out.shape[-1]
    total = own[...].astype(f32) + other[...].astype(f32)
    scale = lax.rsqrt(jnp.mean(total * total, axis=-1, keepdims=True) + eps_norm)
    mine = jnp.where(side[0] == 0, total[:, :half], total[:, half:]) * scale * gain[...]
    if len(out.shape) == 3:
        out[0] = (x[0].astype(f32) + mine[: out.shape[1]]).astype(bf16)
    else:
        out[...] = (x[...].astype(f32) + mine).astype(bf16)


def finish(side, own, other, x, gain, name):
    rows, width = own.shape
    half = width // 2
    block = min(rows, 128)
    if x.ndim == 3:
        shape = x.shape[:2] + (half,)
        x_spec = pl.BlockSpec(shape, lambda i, s: (0, 0, s[0]))
        o_spec = pl.BlockSpec(shape, lambda i, s: (0, 0, 0))
    else:
        shape = (rows, half)
        x_spec = pl.BlockSpec((block, half), lambda i, s: (i, s[0]))
        o_spec = pl.BlockSpec((block, half), lambda i, s: (i, 0))
    return pl.pallas_call(
        finish_kernel,
        grid_spec=pltpu.PrefetchScalarGridSpec(
            num_scalar_prefetch=1,
            grid=(rows // block,),
            in_specs=[
                pl.BlockSpec((block, width), lambda i, s: (i, 0)),
                pl.BlockSpec((block, width), lambda i, s: (i, 0)),
                x_spec,
                pl.BlockSpec((1, half), lambda i, s: (0, s[0])),
            ],
            out_specs=o_spec,
        ),
        out_shape=jax.ShapeDtypeStruct(shape, bf16),
        compiler_params=pltpu.CompilerParams(vmem_limit_bytes=12 << 20),
        cost_estimate=pl.CostEstimate(
            flops=8 * rows * width, transcendentals=0, bytes_accessed=6 * rows * width
        ),
        name=name,
    )(side, own, other, x, gain)


def on_device(
    plane,
    verify_x,
    prefill_x,
    attn_gain,
    w_query,
    w_keyval,
    qk_gain,
    w_out,
    post_gain,
    page_pool,
    outbound,
    page_table,
    cache_len,
    prompt_len,
    accepted,
):
    devices = outbound.shape[1]
    rows = prefill_x.shape[0]
    pool_pages = page_pool.shape[0]
    planes = len(plane[0])
    column = [list(range(i, i + DEEP)) for i in range(0, devices, DEEP)]

    outgoing = pick_pages(outbound, page_pool)
    outgoing, prefill_x = lax.optimization_barrier((outgoing, prefill_x))
    arrived = lax.all_to_all(outgoing, "req", 0, 0, tiled=True, axis_index_groups=plane)

    lengths = prompt_len[0]
    order = jnp.arange(3, dtype=i32)[:, None] >= jnp.arange(4, dtype=i32)[None, :]
    ends = jnp.sum(jnp.where(order, lengths[None, :], 0), axis=1)
    row = jnp.arange(rows, dtype=i32)
    start = jnp.max(jnp.where(row[:, None] >= ends[None, :], ends[None, :], 0), axis=1)
    position = jnp.concatenate(
        [row - start, cache_len[0] + jnp.arange(16, dtype=i32)]
    ).astype(f32)
    inv_freq = rope_base ** (-(jnp.arange(HEAD // 2, dtype=f32) * 2.0) / HEAD)
    angles = position[:, None] * inv_freq[None, :]

    meta = jnp.where(jnp.arange(8, dtype=i32) == 0, cache_len[0], accepted[0])
    queries, prefill_kv, near_kv, sent, draft_kv, own_count, verify_kv = project(
        meta, prefill_x, verify_x, attn_gain[None], w_query, w_keyval,
        qk_gain, jnp.cos(angles), jnp.sin(angles), page_table, pool_pages * PAGE,
    )

    side = lax.axis_index("head").reshape(1)
    where = (lax.axis_index("req") & (DEEP - 1)).reshape(1)
    swap = [(0, 1), (1, 0)]

    def beside(values, mask):
        pairs = [(i, i ^ mask) for i in range(devices)]
        return jnp.concatenate([values, lax.ppermute(values, "req", pairs)], axis=0)

    asked = beside(sent[None], 4)
    attn, own = prompts(
        prompt_len, queries, near_kv, sent, draft_kv,
        page_pool.reshape(pool_pages * PAGE, -1), own_count,
    )
    asked, attn = lax.optimization_barrier((asked, attn))
    asked = beside(asked, 2)
    partial = spread(attn, w_out)
    asked, partial = lax.optimization_barrier((asked, partial))
    asked = beside(asked, 1)
    other = lax.ppermute(partial, "head", swap)
    pieces = remote_pieces(where, asked, arrived.reshape(planes, DEEP, PAGE, -1))
    pieces, other = lax.optimization_barrier((pieces, other))
    prefill_out = finish(side, partial, other, prefill_x, post_gain[None], "finish_prompts")
    pieces = lax.all_to_all(pieces, "req", 0, 0, tiled=True, axis_index_groups=column)
    pieces, prefill_out = lax.optimization_barrier((pieces, prefill_out))
    partial = join(pieces, own, w_out)
    other = lax.ppermute(partial, "head", swap)
    verify_out = finish(side, partial, other, verify_x, post_gain[None], "finish_drafts")
    return (verify_out, prefill_out, verify_kv, prefill_kv)


def solution(mesh):
    devices = mesh.shape["req"]
    plane = [list(range(z, devices, DEEP)) for z in range(DEEP)]
    placed = (
        P("req", None, None),
        P("req", None),
        P(),
        P(None, "head"),
        P(None, "head"),
        P(),
        P("head", None),
        P(),
        P("req", None, "head"),
        P("req", None),
        P("req", None),
        P("req"),
        P("req", None),
        P("req"),
    )
    return jax.shard_map(
        functools.partial(on_device, plane),
        mesh=mesh,
        in_specs=placed,
        out_specs=(
            P("req", None, "head"),
            P("req", "head"),
            P("req", None, "head"),
            P("req", "head"),
        ),
        check_vma=False,
    )
```

```python
import functools

import jax
import jax.numpy as jnp
from jax import lax
from jax.experimental import pallas as pl
from jax.experimental.pallas import tpu as pltpu
from jax.sharding import PartitionSpec as P

HEAD = 256
PAGE = 16
QH = 4
PAD = 8
DEEP = 8
eps_norm = 1e-06
rope_base = 1000000.0
neg_large = -1e30
BIG = 52 << 20
bf16, f32, i32 = jnp.bfloat16, jnp.float32, jnp.int32
HBM = pl.BlockSpec(memory_space=pltpu.MemorySpace.HBM)
VMEM = pl.BlockSpec(memory_space=pltpu.MemorySpace.VMEM)
SMEM = pl.BlockSpec(memory_space=pltpu.MemorySpace.SMEM)


def dot_t(a, b):
    return lax.dot_general(a, b, (((1,), (1,)), ((), ())), preferred_element_type=f32)


def dot_n(a, b):
    return jnp.dot(a, b, preferred_element_type=f32)


def iota(shape, dim):
    return lax.broadcasted_iota(i32, shape, dim)


def unit(values):
    return values * lax.rsqrt(jnp.mean(values * values, axis=-1, keepdims=True) + eps_norm)


def tally(table, length, lanes, first, step):
    slots = table.shape[1]
    eye = iota((slots, slots), 0) == iota((slots, slots), 1)
    page = jnp.sum(jnp.where(eye, table, 0), axis=1, keepdims=True)
    base = iota((slots, 1), 0) * PAGE
    lane = iota((slots, lanes), 1)
    named = page == first + (lane >> 4) * step
    valid = base + (lane & (PAGE - 1)) < length
    return jnp.sum(jnp.where(named & valid, 1.0, 0.0), axis=0, keepdims=True)


def pick_kernel(index, pool, out):
    for i in range(out.shape[0]):
        out[i] = pool[jnp.clip(index[0, i], 0, pool.shape[0] - 1)]


def pick_pages(index, pool):
    count = index.shape[1]
    return pl.pallas_call(
        pick_kernel,
        in_specs=[SMEM, VMEM],
        out_specs=VMEM,
        out_shape=jax.ShapeDtypeStruct((count,) + pool.shape[1:], pool.dtype),
        cost_estimate=pl.CostEstimate(flops=0, transcendentals=0, bytes_accessed=4 << 20),
        name="pick_pages",
    )(index, pool)


def project_kernel(
    meta, x, draft, gain, wq, wkv, qk_gain, cosine, sine, table,
    queries, prompt_kv, near_kv, sent, draft_kv, own_count, verify_kv,
    weights, normed, wide, rows_q, sems,
):
    rows, drafted = x.shape[0], draft.shape[1]
    copies = []
    for h in range(3):
        part = wq.at[:, h * 2 * HEAD : (h + 1) * 2 * HEAD] if h < 2 else wkv
        copy = pltpu.make_async_copy(part, weights.at[h], sems.at[h])
        copy.start()
        copies.append(copy)

    normed[:rows] = (unit(x[...].astype(f32)) * gain[...]).astype(bf16)
    wide[...] = jnp.zeros_like(wide)
    wide[:drafted] = unit(draft[0].astype(f32)) * gain[...]
    normed[rows:] = wide[...].astype(bf16)

    own_count[...] = tally(table[...], meta[0], own_count.shape[1], 0, 1)

    half = HEAD // 2
    cos, sin = cosine[...], sine[...]

    def rotated(values):
        a, b = values[:, :half], values[:, half:]
        return jnp.concatenate([a * cos - b * sin, b * cos + a * sin], axis=-1)

    keep = iota((PAD, HEAD), 0) < meta[1]

    for pair in range(3):
        copies[pair].wait()
        both = dot_n(normed[...], weights[pair])
        for j in range(2):
            h = 2 * pair + j
            value = unit(both[:, j * HEAD : (j + 1) * HEAD])
            if h < QH:
                query = rotated(value * qk_gain[0:1, :])
                queries[h] = query[:rows].astype(bf16)
                mine = query[rows : rows + PAD]
                rows_q[h * PAD : (h + 1) * PAD, :] = mine
                continue
            if h == QH:
                value = rotated(value * qk_gain[1:2, :])
            cols = slice(j * HEAD, (j + 1) * HEAD)
            prompt_kv[:, cols] = value[:rows].astype(bf16)
            near_kv[:, cols] = value[:rows].astype(bf16)
            mine = value[rows : rows + PAD]
            draft_kv[:, cols] = mine
            verify_kv[0, :, cols] = jnp.where(keep, mine, 0.0)[:drafted].astype(bf16)
    sent[...] = rows_q[...].astype(bf16)


def project(meta, x, draft, gain, wq, wkv, qk_gain, cosine, sine, table, own):
    rows, width = x.shape
    drafted = draft.shape[1]
    total = rows + 16
    shapes = [
        jax.ShapeDtypeStruct((QH, rows, HEAD), bf16),
        jax.ShapeDtypeStruct((rows, 2 * HEAD), bf16),
        jax.ShapeDtypeStruct((rows, 2 * HEAD), bf16),
        jax.ShapeDtypeStruct((QH * PAD, HEAD), bf16),
        jax.ShapeDtypeStruct((PAD, 2 * HEAD), f32),
        jax.ShapeDtypeStruct((1, own), f32),
        jax.ShapeDtypeStruct((1, drafted, 2 * HEAD), bf16),
    ]
    return pl.pallas_call(
        project_kernel,
        in_specs=[SMEM, VMEM, VMEM, VMEM, HBM, HBM, VMEM, VMEM, VMEM, VMEM],
        out_specs=[VMEM] * len(shapes),
        out_shape=shapes,
        scratch_shapes=[
            pltpu.VMEM((3, width, 2 * HEAD), bf16),
            pltpu.VMEM((total, width), bf16),
            pltpu.VMEM((16, width), f32),
            pltpu.VMEM((QH * PAD, HEAD), f32),
            pltpu.SemaphoreType.DMA((3,)),
        ],
        compiler_params=pltpu.CompilerParams(vmem_limit_bytes=BIG),
        cost_estimate=pl.CostEstimate(
            flops=2 * total * width * 6 * HEAD, transcendentals=0, bytes_accessed=9 << 20
        ),
        name="project",
    )(meta, x, draft, gain, wq, wkv, qk_gain, cosine, sine, table)


def pack_kernel(meta, draft, table, out, wide):
    drafted, slots = draft.shape[1], table.shape[1]
    wide[...] = jnp.zeros_like(wide)
    wide[:drafted] = draft[0].astype(f32)
    lane = iota((1, 128), 1)
    size = jnp.where(lane == slots, meta[0] >> 3, jnp.where(lane == slots + 1, meta[0] & 7, 0))
    wide[5:6, :128] = size.astype(f32)
    wide[5:6, :slots] = table[...].astype(f32)
    out[0] = wide[...].astype(bf16)


def pack(meta, draft, table):
    width = draft.shape[2]
    return pl.pallas_call(
        pack_kernel,
        in_specs=[SMEM, VMEM, VMEM],
        out_specs=VMEM,
        out_shape=jax.ShapeDtypeStruct((1, PAD, width), bf16),
        scratch_shapes=[pltpu.VMEM((PAD, width), f32)],
        compiler_params=pltpu.CompilerParams(vmem_limit_bytes=4 << 20),
        cost_estimate=pl.CostEstimate(flops=0, transcendentals=0, bytes_accessed=1 << 17),
        name="pack",
    )(meta, draft, table)


def ask_kernel(where, x, gain, wq, qk_gain, cosine, sine, out, weights, sems):
    groups = x.shape[0]
    copies = []
    for i in range(2):
        cols = slice(i * 2 * HEAD, (i + 1) * 2 * HEAD)
        copy = pltpu.make_async_copy(wq.at[:, cols], weights.at[i], sems.at[i])
        copy.start()
        copies.append(copy)
    rows = x[...].astype(f32).reshape(groups * PAD, -1)
    normed = (unit(rows) * gain[...]).astype(bf16)
    counts = []
    for e in range(groups):
        note = x[e][5:6, :128].astype(f32).astype(i32)
        size = jnp.sum(jnp.where(iota((1, 128), 1) == 64, note * 8, 0), keepdims=True)
        size += jnp.sum(jnp.where(iota((1, 128), 1) == 65, note, 0), keepdims=True)
        counts.append(tally(note[:, :64], size, HEAD, 64 + where[0], DEEP))
    count = jnp.concatenate(counts, axis=0).reshape(groups, 1, HEAD)
    half = HEAD // 2
    cos, sin = cosine[...], sine[...]
    mark = iota((groups, PAD, HEAD), 1) == 5
    heads = []
    for i in range(2):
        copies[i].wait()
        both = dot_n(normed, weights[i])
        for j in range(2):
            value = unit(both[:, j * HEAD : (j + 1) * HEAD]) * qk_gain[0:1, :]
            a, b = value[:, :half], value[:, half:]
            value = jnp.concatenate([a * cos - b * sin, b * cos + a * sin], axis=-1)
            value = value.reshape(groups, PAD, HEAD)
            heads.append(jnp.where(mark, count, value) if not heads else value)
    out[...] = jnp.concatenate(heads, axis=1).astype(bf16)


def ask(where, x, gain, wq, qk_gain, cosine, sine):
    groups, _, width = x.shape
    return pl.pallas_call(
        ask_kernel,
        in_specs=[SMEM, VMEM, VMEM, HBM, VMEM, VMEM, VMEM],
        out_specs=VMEM,
        out_shape=jax.ShapeDtypeStruct((groups, QH * PAD, HEAD), bf16),
        scratch_shapes=[
            pltpu.VMEM((2, width, 2 * HEAD), bf16),
            pltpu.SemaphoreType.DMA((2,)),
        ],
        compiler_params=pltpu.CompilerParams(vmem_limit_bytes=BIG),
        cost_estimate=pl.CostEstimate(
            flops=2 * groups * PAD * width * QH * HEAD, transcendentals=0, bytes_accessed=5 << 20
        ),
        name="ask",
    )(where, x, gain, wq, qk_gain, cosine, sine)


def prompt_kernel(lengths, q, kv, query, draft_kv, pool, count, attn, local):
    rows = attn.shape[0]
    row, col = iota((rows, rows), 0), iota((rows, rows), 1)
    start = jnp.zeros((rows, rows), i32)
    end = jnp.int32(0)
    for i in range(3):
        end = end + lengths[0, i]
        start = jnp.where(row >= end, end, start)
    allowed = (col <= row) & (col >= start)
    key, value = kv[:, :HEAD], kv[:, HEAD:]
    for h in range(QH):
        scores = jnp.where(allowed, dot_t(q[h], key), neg_large)
        parts = jnp.exp(scores - jnp.max(scores, axis=-1, keepdims=True))
        probs = (parts / jnp.sum(parts, axis=-1, keepdims=True)).astype(bf16)
        attn[:, h * HEAD : (h + 1) * HEAD] = dot_n(probs, value).astype(bf16)

    mine = query[...]
    times = count[...]
    scores = jnp.where(times > 0.0, dot_t(mine, pool[:, :HEAD]), neg_large)
    fresh = dot_t(mine, draft_kv[:, :HEAD].astype(bf16))
    allowed = iota(fresh.shape, 1) <= (iota(fresh.shape, 0) & (PAD - 1))
    fresh = jnp.where(allowed, fresh, neg_large)
    peak = jnp.maximum(
        jnp.max(scores, axis=-1, keepdims=True), jnp.max(fresh, axis=-1, keepdims=True)
    )
    parts = jnp.where(times > 0.0, jnp.exp(scores - peak) * times, 0.0)
    fresh = jnp.where(allowed, jnp.exp(fresh - peak), 0.0)
    denom = jnp.sum(parts, axis=-1, keepdims=True) + jnp.sum(fresh, axis=-1, keepdims=True)
    local[:, :HEAD] = dot_n(parts.astype(bf16), pool[:, HEAD:]) + dot_n(
        fresh.astype(bf16), draft_kv[:, HEAD:].astype(bf16)
    )
    local[:, HEAD : HEAD + 128] = jnp.broadcast_to(peak, (QH * PAD, 128))
    local[:, HEAD + 128 :] = jnp.broadcast_to(denom, (QH * PAD, 128))


def prompts(lengths, q, kv, query, draft_kv, pool, count):
    rows = kv.shape[0]
    return pl.pallas_call(
        prompt_kernel,
        in_specs=[SMEM] + [VMEM] * 6,
        out_specs=[VMEM, VMEM],
        out_shape=[
            jax.ShapeDtypeStruct((rows, QH * HEAD), bf16),
            jax.ShapeDtypeStruct((QH * PAD, 2 * HEAD), f32),
        ],
        compiler_params=pltpu.CompilerParams(vmem_limit_bytes=16 << 20),
        cost_estimate=pl.CostEstimate(
            flops=16 * rows * rows * HEAD, transcendentals=4 * rows * rows, bytes_accessed=4 << 20
        ),
        name="prompts",
    )(lengths, q, kv, query, draft_kv, pool, count)


def spread_kernel(attn, w_out, out):
    out[...] = dot_n(attn[...], w_out[...]).astype(bf16)


def spread(attn, w_out):
    rows = attn.shape[0]
    depth, width = w_out.shape
    return pl.pallas_call(
        spread_kernel,
        in_specs=[VMEM, VMEM],
        out_specs=VMEM,
        out_shape=jax.ShapeDtypeStruct((rows, width), bf16),
        compiler_params=pltpu.CompilerParams(vmem_limit_bytes=12 << 20),
        cost_estimate=pl.CostEstimate(
            flops=2 * rows * depth * width, transcendentals=0, bytes_accessed=6 << 20
        ),
        name="spread",
    )(attn, w_out)


def remote_kernel(where, queries, pages, out):
    here = where[0]
    groups, rows = queries.shape[0], queries.shape[1]
    asked = [here ^ mask for mask in ORDER]
    scores, counts = [], []
    for e in range(groups):
        query = queries[e]
        count = query.astype(f32)[5:6, :]
        held = pages[:, asked[e], :, :HEAD].reshape(HEAD, HEAD)
        scores.append(jnp.where(count > 0.0, dot_t(query, held), neg_large))
        counts.append(jnp.broadcast_to(count, (rows, HEAD)))
    score = jnp.concatenate(scores, axis=0)
    count = jnp.concatenate(counts, axis=0)
    peak = jnp.max(score, axis=-1, keepdims=True).astype(bf16).astype(f32)
    parts = jnp.where(count > 0.0, jnp.exp(score - peak) * count, 0.0)
    denom = jnp.sum(parts, axis=-1, keepdims=True)
    high = denom.astype(bf16).astype(f32)

    shape = (groups * rows // PAD, PAD, 128)
    token, lane = iota(shape, 1), iota(shape, 2)

    def along(values):
        wide = jnp.broadcast_to(values, (groups * rows, 128)).reshape(shape)
        wide = jnp.sum(jnp.where(token == lane, wide, 0.0), axis=1, keepdims=True)
        return jnp.broadcast_to(wide, shape)

    stats = jnp.where(
        token == 5, along(peak), jnp.where(token == 6, along(high), along(denom - high))
    ).reshape(groups * rows, 128)
    spare = (iota((rows, 128), 0) & (PAD - 1)) >= 5
    parts = parts.astype(bf16)
    for e in range(groups):
        own = slice(e * rows, (e + 1) * rows)
        held = pages[:, asked[e], :, HEAD:].reshape(HEAD, HEAD)
        total = dot_n(parts[own], held)
        out[asked[e], :, :128] = jnp.where(spare, stats[own], total[:, :128]).astype(bf16)
        out[asked[e], :, 128:] = total[:, 128:].astype(bf16)


ORDER = (0, 4, 2, 6, 1, 5, 3, 7)


def remote_pieces(where, queries, pages):
    groups, rows, _ = queries.shape
    return pl.pallas_call(
        remote_kernel,
        in_specs=[SMEM, VMEM, VMEM],
        out_specs=VMEM,
        out_shape=jax.ShapeDtypeStruct((groups, rows, HEAD), bf16),
        compiler_params=pltpu.CompilerParams(vmem_limit_bytes=12 << 20),
        cost_estimate=pl.CostEstimate(flops=1 << 26, transcendentals=1 << 16, bytes_accessed=3 << 20),
        name="remote_pieces",
    )(where, queries, pages)


def join_kernel(pieces, local, w_out, out, attn, weights, sems):
    depth, width = w_out.shape
    parts = sems.shape[0]
    cols = width // parts
    copies = []
    for i in range(parts):
        part = slice(i * cols, (i + 1) * cols)
        copy = pltpu.make_async_copy(w_out.at[:, part], weights.at[:, part], sems.at[i])
        copy.start()
        copies.append(copy)
    groups, rows = pieces.shape[0], pieces.shape[1]
    shape = (groups * rows // PAD, PAD, 128)
    token, lane = iota(shape, 1), iota(shape, 2)
    spare = pieces[:, :, :128].astype(f32).reshape(shape)

    def upright(which):
        row = jnp.sum(jnp.where(token == which, spare, 0.0), axis=1, keepdims=True)
        row = jnp.where(token == lane, jnp.broadcast_to(row, shape), 0.0)
        return jnp.sum(row, axis=2, keepdims=True).reshape(groups, rows, 1)

    peaks = upright(5)
    sums = upright(6) + upright(7)
    own = local[:, HEAD : HEAD + 1]
    top = jnp.maximum(jnp.max(peaks, axis=0), own)
    scale = jnp.exp(peaks - top[None])
    near = jnp.exp(own - top)
    total = local[:, :HEAD] * near + jnp.sum(pieces[...].astype(f32) * scale, axis=0)
    denom = local[:, HEAD + 128 : HEAD + 129] * near + jnp.sum(sums * scale, axis=0)
    attn[...] = total / denom
    heads = [attn[h * PAD : (h + 1) * PAD, :].astype(bf16) for h in range(QH)]
    for i in range(parts):
        copies[i].wait()
        part = slice(i * cols, (i + 1) * cols)
        out[:, part] = functools.reduce(
            jnp.add,
            [dot_n(heads[h], weights[h * HEAD : (h + 1) * HEAD, part]) for h in range(QH)],
        )


def join(pieces, local, w_out):
    depth, width = w_out.shape
    return pl.pallas_call(
        join_kernel,
        in_specs=[VMEM, VMEM, HBM],
        out_specs=VMEM,
        out_shape=jax.ShapeDtypeStruct((PAD, width), f32),
        scratch_shapes=[
            pltpu.VMEM((QH * PAD, HEAD), f32),
            pltpu.VMEM((depth, width), bf16),
            pltpu.SemaphoreType.DMA((4,)),
        ],
        compiler_params=pltpu.CompilerParams(vmem_limit_bytes=BIG),
        cost_estimate=pl.CostEstimate(flops=1 << 25, transcendentals=0, bytes_accessed=4 << 20),
        name="join",
    )(pieces, local, w_out)


def finish_kernel(side, own, other, x, gain, out):
    half = out.shape[-1]
    total = own[...].astype(f32) + other[...].astype(f32)
    scale = lax.rsqrt(jnp.mean(total * total, axis=-1, keepdims=True) + eps_norm)
    mine = jnp.where(side[0] == 0, total[:, :half], total[:, half:]) * scale * gain[...]
    if len(out.shape) == 3:
        out[0] = (x[0].astype(f32) + mine[: out.shape[1]]).astype(bf16)
    else:
        out[...] = (x[...].astype(f32) + mine).astype(bf16)


def finish(side, own, other, x, gain, name):
    rows, width = own.shape
    half = width // 2
    block = min(rows, 128)
    if x.ndim == 3:
        shape = x.shape[:2] + (half,)
        x_spec = pl.BlockSpec(shape, lambda i, s: (0, 0, s[0]))
        o_spec = pl.BlockSpec(shape, lambda i, s: (0, 0, 0))
    else:
        shape = (rows, half)
        x_spec = pl.BlockSpec((block, half), lambda i, s: (i, s[0]))
        o_spec = pl.BlockSpec((block, half), lambda i, s: (i, 0))
    return pl.pallas_call(
        finish_kernel,
        grid_spec=pltpu.PrefetchScalarGridSpec(
            num_scalar_prefetch=1,
            grid=(rows // block,),
            in_specs=[
                pl.BlockSpec((block, width), lambda i, s: (i, 0)),
                pl.BlockSpec((block, width), lambda i, s: (i, 0)),
                x_spec,
                pl.BlockSpec((1, half), lambda i, s: (0, s[0])),
            ],
            out_specs=o_spec,
        ),
        out_shape=jax.ShapeDtypeStruct(shape, bf16),
        compiler_params=pltpu.CompilerParams(vmem_limit_bytes=12 << 20),
        cost_estimate=pl.CostEstimate(
            flops=8 * rows * width, transcendentals=0, bytes_accessed=6 * rows * width
        ),
        name=name,
    )(side, own, other, x, gain)


def on_device(
    plane,
    verify_x,
    prefill_x,
    attn_gain,
    w_query,
    w_keyval,
    qk_gain,
    w_out,
    post_gain,
    page_pool,
    outbound,
    page_table,
    cache_len,
    prompt_len,
    accepted,
):
    devices = outbound.shape[1]
    rows = prefill_x.shape[0]
    pool_pages = page_pool.shape[0]
    planes = len(plane[0])
    column = [list(range(i, i + DEEP)) for i in range(0, devices, DEEP)]

    outgoing = pick_pages(outbound, page_pool)
    outgoing, prefill_x, cache_len = lax.optimization_barrier((outgoing, prefill_x, cache_len))
    arrived = lax.all_to_all(outgoing, "req", 0, 0, tiled=True, axis_index_groups=plane)

    meta = jnp.where(jnp.arange(8, dtype=i32) == 0, cache_len[0], accepted[0])
    meta, verify_x = lax.optimization_barrier((meta, verify_x))
    side = lax.axis_index("head").reshape(1)
    where = (lax.axis_index("req") & (DEEP - 1)).reshape(1)
    swap = [(0, 1), (1, 0)]

    def beside(values, mask):
        pairs = [(i, i ^ mask) for i in range(devices)]
        return jnp.concatenate([values, lax.ppermute(values, "req", pairs)], axis=0)

    asked = beside(pack(meta, verify_x, page_table), 4)

    inv_freq = rope_base ** (-(jnp.arange(HEAD // 2, dtype=f32) * 2.0) / HEAD)
    lengths = prompt_len[0]
    order = jnp.arange(3, dtype=i32)[:, None] >= jnp.arange(4, dtype=i32)[None, :]
    ends = jnp.sum(jnp.where(order, lengths[None, :], 0), axis=1)
    row = jnp.arange(rows, dtype=i32)
    start = jnp.max(jnp.where(row[:, None] >= ends[None, :], ends[None, :], 0), axis=1)
    position = jnp.concatenate(
        [row - start, cache_len[0] + jnp.arange(16, dtype=i32)]
    ).astype(f32)
    angles = position[:, None] * inv_freq[None, :]

    queries, prefill_kv, near_kv, sent, draft_kv, own_count, verify_kv = project(
        meta, prefill_x, verify_x, attn_gain[None], w_query, w_keyval,
        qk_gain, jnp.cos(angles), jnp.sin(angles), page_table, pool_pages * PAGE,
    )
    asked, queries = lax.optimization_barrier((asked, queries))
    asked = beside(asked, 2)
    attn, own = prompts(
        prompt_len, queries, near_kv, sent, draft_kv,
        page_pool.reshape(pool_pages * PAGE, -1), own_count,
    )
    partial = spread(attn, w_out)
    asked, partial = lax.optimization_barrier((asked, partial))
    asked = beside(asked, 1)
    other = lax.ppermute(partial, "head", swap)

    slots = page_table.shape[1]
    size = asked[:, 5, slots : slots + 2].astype(f32)
    position = (size[:, 0] * 8.0 + size[:, 1])[:, None] + jnp.arange(PAD, dtype=f32)[None, :]
    angles = position.reshape(-1)[:, None] * inv_freq[None, :]
    queries = ask(
        where, asked, attn_gain[None], w_query, qk_gain, jnp.cos(angles), jnp.sin(angles)
    )
    arrived, queries = lax.optimization_barrier((arrived, queries))
    pieces = remote_pieces(where, queries, arrived.reshape(planes, DEEP, PAGE, -1))
    pieces, other = lax.optimization_barrier((pieces, other))
    prefill_out = finish(side, partial, other, prefill_x, post_gain[None], "finish_prompts")
    pieces = lax.all_to_all(pieces, "req", 0, 0, tiled=True, axis_index_groups=column)
    pieces, prefill_out = lax.optimization_barrier((pieces, prefill_out))
    partial = join(pieces, own, w_out)
    other = lax.ppermute(partial, "head", swap)
    verify_out = finish(side, partial, other, verify_x, post_gain[None], "finish_drafts")
    return (verify_out, prefill_out, verify_kv, prefill_kv)


def solution(mesh):
    devices = mesh.shape["req"]
    plane = [list(range(z, devices, DEEP)) for z in range(DEEP)]
    placed = (
        P("req", None, None),
        P("req", None),
        P(),
        P(None, "head"),
        P(None, "head"),
        P(),
        P("head", None),
        P(),
        P("req", None, "head"),
        P("req", None),
        P("req", None),
        P("req"),
        P("req", None),
        P("req"),
    )
    return jax.shard_map(
        functools.partial(on_device, plane),
        mesh=mesh,
        in_specs=placed,
        out_specs=(
            P("req", None, "head"),
            P("req", "head"),
            P("req", None, "head"),
            P("req", "head"),
        ),
        check_vma=False,
    )
```

```python
import functools

import jax
import jax.numpy as jnp
from jax import lax
from jax.experimental import pallas as pl
from jax.experimental.pallas import tpu as pltpu
from jax.sharding import PartitionSpec as P

HEAD = 256
PAGE = 16
QH = 4
PAD = 8
DEEP = 8
eps_norm = 1e-06
rope_base = 1000000.0
neg_large = -1e30
bf16, f32, i32 = jnp.bfloat16, jnp.float32, jnp.int32
HBM = pl.BlockSpec(memory_space=pltpu.MemorySpace.HBM)
VMEM = pl.BlockSpec(memory_space=pltpu.MemorySpace.VMEM)
TOKEN = jax.ShapeDtypeStruct((8, 128), f32)
SMEM = pl.BlockSpec(memory_space=pltpu.MemorySpace.SMEM)


def dot_t(a, b):
    return lax.dot_general(a, b, (((1,), (1,)), ((), ())), preferred_element_type=f32)


def dot_n(a, b):
    return jnp.dot(a, b, preferred_element_type=f32)


def iota(shape, dim):
    return lax.broadcasted_iota(i32, shape, dim)


def unit(values):
    return values * lax.rsqrt(jnp.mean(values * values, axis=-1, keepdims=True) + eps_norm)


def tally(table, length, lanes, first, step):
    slots = table.shape[1]
    eye = iota((slots, slots), 0) == iota((slots, slots), 1)
    page = jnp.sum(jnp.where(eye, table, 0), axis=1, keepdims=True)
    base = iota((slots, 1), 0) * PAGE
    lane = iota((slots, lanes), 1)
    named = page == first + (lane >> 4) * step
    valid = base + (lane & (PAGE - 1)) < length
    return jnp.sum(jnp.where(named & valid, 1.0, 0.0), axis=0, keepdims=True)


def pick_kernel(index, pool, out, token):
    token[...] = jnp.zeros_like(token)
    for i in range(out.shape[0]):
        out[i] = pool[jnp.clip(index[0, i], 0, pool.shape[0] - 1)]


def pick_pages(index, pool):
    count = index.shape[1]
    return pl.pallas_call(
        pick_kernel,
        in_specs=[SMEM, VMEM],
        out_specs=[VMEM, VMEM],
        out_shape=[jax.ShapeDtypeStruct((count,) + pool.shape[1:], pool.dtype), TOKEN],
        cost_estimate=pl.CostEstimate(flops=0, transcendentals=0, bytes_accessed=4 << 20),
        name="pick_pages",
    )(index, pool)


def project_kernel(
    meta, x, draft, gain, wq, wkv, qk_gain, cosine, sine, table,
    queries, prompt_kv, near_kv, sent, draft_kv, own_count, verify_kv,
    weights, normed, wide, rows_q, sems,
):
    rows, drafted = x.shape[0], draft.shape[1]
    copies = []
    for h in range(3):
        part = wq.at[:, h * 2 * HEAD : (h + 1) * 2 * HEAD] if h < 2 else wkv
        copy = pltpu.make_async_copy(part, weights.at[h], sems.at[h])
        copy.start()
        copies.append(copy)

    normed[:rows] = (unit(x[...].astype(f32)) * gain[...]).astype(bf16)
    wide[...] = jnp.zeros_like(wide)
    wide[:drafted] = unit(draft[0].astype(f32)) * gain[...]
    normed[rows:] = wide[...].astype(bf16)

    own_count[...] = tally(table[...], meta[0], own_count.shape[1], 0, 1)

    half = HEAD // 2
    cos, sin = cosine[...], sine[...]

    def rotated(values):
        a, b = values[:, :half], values[:, half:]
        return jnp.concatenate([a * cos - b * sin, b * cos + a * sin], axis=-1)

    keep = iota((PAD, HEAD), 0) < meta[1]

    for pair in range(3):
        copies[pair].wait()
        both = dot_n(normed[...], weights[pair])
        for j in range(2):
            h = 2 * pair + j
            value = unit(both[:, j * HEAD : (j + 1) * HEAD])
            if h < QH:
                query = rotated(value * qk_gain[0:1, :])
                queries[h] = query[:rows].astype(bf16)
                mine = query[rows : rows + PAD]
                rows_q[h * PAD : (h + 1) * PAD, :] = mine
                continue
            if h == QH:
                value = rotated(value * qk_gain[1:2, :])
            cols = slice(j * HEAD, (j + 1) * HEAD)
            prompt_kv[:, cols] = value[:rows].astype(bf16)
            near_kv[:, cols] = value[:rows].astype(bf16)
            mine = value[rows : rows + PAD]
            draft_kv[:, cols] = mine
            verify_kv[0, :, cols] = jnp.where(keep, mine, 0.0)[:drafted].astype(bf16)
    sent[...] = rows_q[...].astype(bf16)


def project(meta, x, draft, gain, wq, wkv, qk_gain, cosine, sine, table, own):
    rows, width = x.shape
    drafted = draft.shape[1]
    total = rows + 16
    shapes = [
        jax.ShapeDtypeStruct((QH, rows, HEAD), bf16),
        jax.ShapeDtypeStruct((rows, 2 * HEAD), bf16),
        jax.ShapeDtypeStruct((rows, 2 * HEAD), bf16),
        jax.ShapeDtypeStruct((QH * PAD, HEAD), bf16),
        jax.ShapeDtypeStruct((PAD, 2 * HEAD), f32),
        jax.ShapeDtypeStruct((1, own), f32),
        jax.ShapeDtypeStruct((1, drafted, 2 * HEAD), bf16),
    ]
    return pl.pallas_call(
        project_kernel,
        in_specs=[SMEM, VMEM, VMEM, VMEM, HBM, HBM, VMEM, VMEM, VMEM, VMEM],
        out_specs=[VMEM] * len(shapes),
        out_shape=shapes,
        scratch_shapes=[
            pltpu.VMEM((3, width, 2 * HEAD), bf16),
            pltpu.VMEM((total, width), bf16),
            pltpu.VMEM((16, width), f32),
            pltpu.VMEM((QH * PAD, HEAD), f32),
            pltpu.SemaphoreType.DMA((3,)),
        ],
        compiler_params=pltpu.CompilerParams(vmem_limit_bytes=55 << 20),
        cost_estimate=pl.CostEstimate(
            flops=2 * total * width * 6 * HEAD, transcendentals=0, bytes_accessed=9 << 20
        ),
        name="project",
    )(meta, x, draft, gain, wq, wkv, qk_gain, cosine, sine, table)


def pack_kernel(meta, draft, table, after, out, wide):
    drafted, slots = draft.shape[1], table.shape[1]
    wide[...] = jnp.zeros_like(wide)
    wide[:drafted] = draft[0].astype(f32)
    lane = iota((1, 128), 1)
    size = jnp.where(lane == slots, meta[0] >> 3, jnp.where(lane == slots + 1, meta[0] & 7, 0))
    wide[5:6, :128] = size.astype(f32)
    wide[5:6, :slots] = table[...].astype(f32)
    out[0] = wide[...].astype(bf16)


def pack(meta, draft, table, after):
    width = draft.shape[2]
    return pl.pallas_call(
        pack_kernel,
        in_specs=[SMEM, VMEM, VMEM, VMEM],
        out_specs=VMEM,
        out_shape=jax.ShapeDtypeStruct((1, PAD, width), bf16),
        scratch_shapes=[pltpu.VMEM((PAD, width), f32)],
        compiler_params=pltpu.CompilerParams(vmem_limit_bytes=4 << 20),
        cost_estimate=pl.CostEstimate(flops=0, transcendentals=0, bytes_accessed=1 << 17),
        name="pack",
    )(meta, draft, table, after)


def ask_kernel(where, x, gain, wq, qk_gain, cosine, sine, out, weights, sems):
    groups = x.shape[0]
    copies = []
    for i in range(2):
        cols = slice(i * 2 * HEAD, (i + 1) * 2 * HEAD)
        copy = pltpu.make_async_copy(wq.at[:, cols], weights.at[i], sems.at[i])
        copy.start()
        copies.append(copy)
    rows = x[...].astype(f32).reshape(groups * PAD, -1)
    normed = (unit(rows) * gain[...]).astype(bf16)
    counts = []
    for e in range(groups):
        note = x[e][5:6, :128].astype(f32).astype(i32)
        size = jnp.sum(jnp.where(iota((1, 128), 1) == 64, note * 8, 0), keepdims=True)
        size += jnp.sum(jnp.where(iota((1, 128), 1) == 65, note, 0), keepdims=True)
        counts.append(tally(note[:, :64], size, HEAD, 64 + where[0], DEEP))
    count = jnp.concatenate(counts, axis=0).reshape(groups, 1, HEAD)
    half = HEAD // 2
    cos, sin = cosine[...], sine[...]
    mark = iota((groups, PAD, HEAD), 1) == 5
    heads = []
    for i in range(2):
        copies[i].wait()
        both = dot_n(normed, weights[i])
        for j in range(2):
            value = unit(both[:, j * HEAD : (j + 1) * HEAD]) * qk_gain[0:1, :]
            a, b = value[:, :half], value[:, half:]
            value = jnp.concatenate([a * cos - b * sin, b * cos + a * sin], axis=-1)
            value = value.reshape(groups, PAD, HEAD)
            heads.append(jnp.where(mark, count, value) if not heads else value)
    out[...] = jnp.concatenate(heads, axis=1).astype(bf16)


def ask(where, x, gain, wq, qk_gain, cosine, sine):
    groups, _, width = x.shape
    return pl.pallas_call(
        ask_kernel,
        in_specs=[SMEM, VMEM, VMEM, HBM, VMEM, VMEM, VMEM],
        out_specs=VMEM,
        out_shape=jax.ShapeDtypeStruct((groups, QH * PAD, HEAD), bf16),
        scratch_shapes=[
            pltpu.VMEM((2, width, 2 * HEAD), bf16),
            pltpu.SemaphoreType.DMA((2,)),
        ],
        compiler_params=pltpu.CompilerParams(vmem_limit_bytes=50 << 20),
        cost_estimate=pl.CostEstimate(
            flops=2 * groups * PAD * width * QH * HEAD, transcendentals=0, bytes_accessed=5 << 20
        ),
        name="ask",
    )(where, x, gain, wq, qk_gain, cosine, sine)


def prompt_kernel(
    lengths, q, kv, query, draft_kv, pool, count, w_out, out, local, attn, weights, sems
):
    split = sems.shape[0]
    cols = out.shape[1] // split
    copies = []
    for i in range(split):
        part = slice(i * cols, (i + 1) * cols)
        copy = pltpu.make_async_copy(w_out.at[:, part], weights.at[:, part], sems.at[i])
        copy.start()
        copies.append(copy)
    rows = attn.shape[0]
    row, col = iota((rows, rows), 0), iota((rows, rows), 1)
    start = jnp.zeros((rows, rows), i32)
    end = jnp.int32(0)
    for i in range(3):
        end = end + lengths[0, i]
        start = jnp.where(row >= end, end, start)
    allowed = (col <= row) & (col >= start)
    key, value = kv[:, :HEAD], kv[:, HEAD:]
    for h in range(QH):
        scores = jnp.where(allowed, dot_t(q[h], key), neg_large)
        parts = jnp.exp(scores - jnp.max(scores, axis=-1, keepdims=True))
        probs = (parts / jnp.sum(parts, axis=-1, keepdims=True)).astype(bf16)
        attn[:, h * HEAD : (h + 1) * HEAD] = dot_n(probs, value).astype(bf16)

    mine = query[...]
    times = count[...]
    scores = jnp.where(times > 0.0, dot_t(mine, pool[:, :HEAD]), neg_large)
    fresh = dot_t(mine, draft_kv[:, :HEAD].astype(bf16))
    allowed = iota(fresh.shape, 1) <= (iota(fresh.shape, 0) & (PAD - 1))
    fresh = jnp.where(allowed, fresh, neg_large)
    peak = jnp.maximum(
        jnp.max(scores, axis=-1, keepdims=True), jnp.max(fresh, axis=-1, keepdims=True)
    )
    parts = jnp.where(times > 0.0, jnp.exp(scores - peak) * times, 0.0)
    fresh = jnp.where(allowed, jnp.exp(fresh - peak), 0.0)
    denom = jnp.sum(parts, axis=-1, keepdims=True) + jnp.sum(fresh, axis=-1, keepdims=True)
    local[:, :HEAD] = dot_n(parts.astype(bf16), pool[:, HEAD:]) + dot_n(
        fresh.astype(bf16), draft_kv[:, HEAD:].astype(bf16)
    )
    local[:, HEAD : HEAD + 128] = jnp.broadcast_to(peak, (QH * PAD, 128))
    local[:, HEAD + 128 :] = jnp.broadcast_to(denom, (QH * PAD, 128))

    for i in range(split):
        copies[i].wait()
        part = slice(i * cols, (i + 1) * cols)
        out[:, part] = dot_n(attn[...], weights[:, part]).astype(bf16)


def prompts(lengths, q, kv, query, draft_kv, pool, count, w_out):
    rows = kv.shape[0]
    depth, width = w_out.shape
    return pl.pallas_call(
        prompt_kernel,
        in_specs=[SMEM] + [VMEM] * 6 + [HBM],
        out_specs=[VMEM, VMEM],
        out_shape=[
            jax.ShapeDtypeStruct((rows, width), bf16),
            jax.ShapeDtypeStruct((QH * PAD, 2 * HEAD), f32),
        ],
        scratch_shapes=[
            pltpu.VMEM((rows, depth), bf16),
            pltpu.VMEM((depth, width), bf16),
            pltpu.SemaphoreType.DMA((4,)),
        ],
        compiler_params=pltpu.CompilerParams(vmem_limit_bytes=54 << 20),
        cost_estimate=pl.CostEstimate(
            flops=16 * rows * rows * HEAD, transcendentals=4 * rows * rows, bytes_accessed=4 << 20
        ),
        name="prompts",
    )(lengths, q, kv, query, draft_kv, pool, count, w_out)


def remote_kernel(where, queries, pages, after, out):
    here = where[0]
    groups, rows = queries.shape[0], queries.shape[1]
    asked = [here ^ mask for mask in ORDER]
    scores, counts = [], []
    for e in range(groups):
        query = queries[e]
        count = query.astype(f32)[5:6, :]
        held = pages[:, asked[e], :, :HEAD].reshape(HEAD, HEAD)
        scores.append(jnp.where(count > 0.0, dot_t(query, held), neg_large))
        counts.append(jnp.broadcast_to(count, (rows, HEAD)))
    score = jnp.concatenate(scores, axis=0)
    count = jnp.concatenate(counts, axis=0)
    peak = jnp.max(score, axis=-1, keepdims=True).astype(bf16).astype(f32)
    parts = jnp.where(count > 0.0, jnp.exp(score - peak) * count, 0.0)
    denom = jnp.sum(parts, axis=-1, keepdims=True)
    high = denom.astype(bf16).astype(f32)

    shape = (groups * rows // PAD, PAD, 128)
    token, lane = iota(shape, 1), iota(shape, 2)

    def along(values):
        wide = jnp.broadcast_to(values, (groups * rows, 128)).reshape(shape)
        wide = jnp.sum(jnp.where(token == lane, wide, 0.0), axis=1, keepdims=True)
        return jnp.broadcast_to(wide, shape)

    stats = jnp.where(
        token == 5, along(peak), jnp.where(token == 6, along(high), along(denom - high))
    ).reshape(groups * rows, 128)
    spare = (iota((rows, 128), 0) & (PAD - 1)) >= 5
    parts = parts.astype(bf16)
    for e in range(groups):
        own = slice(e * rows, (e + 1) * rows)
        held = pages[:, asked[e], :, HEAD:].reshape(HEAD, HEAD)
        total = dot_n(parts[own], held)
        out[asked[e], :, :128] = jnp.where(spare, stats[own], total[:, :128]).astype(bf16)
        out[asked[e], :, 128:] = total[:, 128:].astype(bf16)


ORDER = (0, 4, 2, 6, 1, 5, 3, 7)


def remote_pieces(where, queries, pages, after):
    groups, rows, _ = queries.shape
    return pl.pallas_call(
        remote_kernel,
        in_specs=[SMEM, VMEM, VMEM, VMEM],
        out_specs=VMEM,
        out_shape=jax.ShapeDtypeStruct((groups, rows, HEAD), bf16),
        compiler_params=pltpu.CompilerParams(vmem_limit_bytes=12 << 20),
        cost_estimate=pl.CostEstimate(flops=1 << 26, transcendentals=1 << 16, bytes_accessed=3 << 20),
        name="remote_pieces",
    )(where, queries, pages, after)


def join_kernel(pieces, local, w_out, out, attn, weights, sems):
    depth, width = w_out.shape
    parts = sems.shape[0]
    cols = width // parts
    copies = []
    for i in range(parts):
        part = slice(i * cols, (i + 1) * cols)
        copy = pltpu.make_async_copy(w_out.at[:, part], weights.at[:, part], sems.at[i])
        copy.start()
        copies.append(copy)
    groups, rows = pieces.shape[0], pieces.shape[1]
    shape = (groups * rows // PAD, PAD, 128)
    token, lane = iota(shape, 1), iota(shape, 2)
    spare = pieces[:, :, :128].astype(f32).reshape(shape)

    def upright(which):
        row = jnp.sum(jnp.where(token == which, spare, 0.0), axis=1, keepdims=True)
        row = jnp.where(token == lane, jnp.broadcast_to(row, shape), 0.0)
        return jnp.sum(row, axis=2, keepdims=True).reshape(groups, rows, 1)

    peaks = upright(5)
    sums = upright(6) + upright(7)
    own = local[:, HEAD : HEAD + 1]
    top = jnp.maximum(jnp.max(peaks, axis=0), own)
    scale = jnp.exp(peaks - top[None])
    near = jnp.exp(own - top)
    total = local[:, :HEAD] * near + jnp.sum(pieces[...].astype(f32) * scale, axis=0)
    denom = local[:, HEAD + 128 : HEAD + 129] * near + jnp.sum(sums * scale, axis=0)
    attn[...] = total / denom
    heads = [attn[h * PAD : (h + 1) * PAD, :].astype(bf16) for h in range(QH)]
    for i in range(parts):
        copies[i].wait()
        part = slice(i * cols, (i + 1) * cols)
        out[:, part] = functools.reduce(
            jnp.add,
            [dot_n(heads[h], weights[h * HEAD : (h + 1) * HEAD, part]) for h in range(QH)],
        )


def join(pieces, local, w_out):
    depth, width = w_out.shape
    return pl.pallas_call(
        join_kernel,
        in_specs=[VMEM, VMEM, HBM],
        out_specs=VMEM,
        out_shape=jax.ShapeDtypeStruct((PAD, width), f32),
        scratch_shapes=[
            pltpu.VMEM((QH * PAD, HEAD), f32),
            pltpu.VMEM((depth, width), bf16),
            pltpu.SemaphoreType.DMA((4,)),
        ],
        compiler_params=pltpu.CompilerParams(vmem_limit_bytes=50 << 20),
        cost_estimate=pl.CostEstimate(flops=1 << 25, transcendentals=0, bytes_accessed=4 << 20),
        name="join",
    )(pieces, local, w_out)


def finish_kernel(side, own, other, x, gain, out, token):
    token[...] = jnp.zeros_like(token)
    half = out.shape[-1]
    total = own[...].astype(f32) + other[...].astype(f32)
    scale = lax.rsqrt(jnp.mean(total * total, axis=-1, keepdims=True) + eps_norm)
    mine = jnp.where(side[0] == 0, total[:, :half], total[:, half:]) * scale * gain[...]
    if len(out.shape) == 3:
        out[0] = (x[0].astype(f32) + mine[: out.shape[1]]).astype(bf16)
    else:
        out[...] = (x[...].astype(f32) + mine).astype(bf16)


def finish(side, own, other, x, gain, name):
    rows, width = own.shape
    half = width // 2
    block = min(rows, 128)
    if x.ndim == 3:
        shape = x.shape[:2] + (half,)
        x_spec = pl.BlockSpec(shape, lambda i, s: (0, 0, s[0]))
        o_spec = pl.BlockSpec(shape, lambda i, s: (0, 0, 0))
    else:
        shape = (rows, half)
        x_spec = pl.BlockSpec((block, half), lambda i, s: (i, s[0]))
        o_spec = pl.BlockSpec((block, half), lambda i, s: (i, 0))
    return pl.pallas_call(
        finish_kernel,
        grid_spec=pltpu.PrefetchScalarGridSpec(
            num_scalar_prefetch=1,
            grid=(rows // block,),
            in_specs=[
                pl.BlockSpec((block, width), lambda i, s: (i, 0)),
                pl.BlockSpec((block, width), lambda i, s: (i, 0)),
                x_spec,
                pl.BlockSpec((1, half), lambda i, s: (0, s[0])),
            ],
            out_specs=[o_spec, pl.BlockSpec(TOKEN.shape, lambda i, s: (0, 0))],
        ),
        out_shape=[jax.ShapeDtypeStruct(shape, bf16), TOKEN],
        compiler_params=pltpu.CompilerParams(vmem_limit_bytes=12 << 20),
        cost_estimate=pl.CostEstimate(
            flops=8 * rows * width, transcendentals=0, bytes_accessed=6 * rows * width
        ),
        name=name,
    )(side, own, other, x, gain)


def on_device(
    plane,
    verify_x,
    prefill_x,
    attn_gain,
    w_query,
    w_keyval,
    qk_gain,
    w_out,
    post_gain,
    page_pool,
    outbound,
    page_table,
    cache_len,
    prompt_len,
    accepted,
):
    devices = outbound.shape[1]
    rows = prefill_x.shape[0]
    pool_pages = page_pool.shape[0]
    planes = len(plane[0])
    column = [list(range(i, i + DEEP)) for i in range(0, devices, DEEP)]

    outgoing, picked = pick_pages(outbound, page_pool)
    outgoing, prefill_x, cache_len = lax.optimization_barrier((outgoing, prefill_x, cache_len))
    arrived = lax.all_to_all(outgoing, "req", 0, 0, tiled=True, axis_index_groups=plane)

    meta = jnp.where(jnp.arange(8, dtype=i32) == 0, cache_len[0], accepted[0])
    meta, verify_x = lax.optimization_barrier((meta, verify_x))
    side = lax.axis_index("head").reshape(1)
    where = (lax.axis_index("req") & (DEEP - 1)).reshape(1)
    swap = [(0, 1), (1, 0)]

    def beside(values, mask):
        pairs = [(i, i ^ mask) for i in range(devices)]
        return jnp.concatenate([values, lax.ppermute(values, "req", pairs)], axis=0)

    asked = beside(pack(meta, verify_x, page_table, picked), 4)

    inv_freq = rope_base ** (-(jnp.arange(HEAD // 2, dtype=f32) * 2.0) / HEAD)
    lengths = prompt_len[0]
    order = jnp.arange(3, dtype=i32)[:, None] >= jnp.arange(4, dtype=i32)[None, :]
    ends = jnp.sum(jnp.where(order, lengths[None, :], 0), axis=1)
    row = jnp.arange(rows, dtype=i32)
    start = jnp.max(jnp.where(row[:, None] >= ends[None, :], ends[None, :], 0), axis=1)
    position = jnp.concatenate(
        [row - start, cache_len[0] + jnp.arange(16, dtype=i32)]
    ).astype(f32)
    angles = position[:, None] * inv_freq[None, :]

    queries, prefill_kv, near_kv, sent, draft_kv, own_count, verify_kv = project(
        meta, prefill_x, verify_x, attn_gain[None], w_query, w_keyval,
        qk_gain, jnp.cos(angles), jnp.sin(angles), page_table, pool_pages * PAGE,
    )
    asked, queries = lax.optimization_barrier((asked, queries))
    asked = beside(asked, 2)
    partial, own = prompts(
        prompt_len, queries, near_kv, sent, draft_kv,
        page_pool.reshape(pool_pages * PAGE, -1), own_count, w_out,
    )
    asked, partial = lax.optimization_barrier((asked, partial))
    asked = beside(asked, 1)
    other = lax.ppermute(partial, "head", swap)
    prefill_out, done = finish(side, partial, other, prefill_x, post_gain[None], "finish_prompts")

    slots = page_table.shape[1]
    size = asked[:, 5, slots : slots + 2].astype(f32)
    position = (size[:, 0] * 8.0 + size[:, 1])[:, None] + jnp.arange(PAD, dtype=f32)[None, :]
    angles = position.reshape(-1)[:, None] * inv_freq[None, :]
    queries = ask(
        where, asked, attn_gain[None], w_query, qk_gain, jnp.cos(angles), jnp.sin(angles)
    )
    pieces = remote_pieces(
        where, queries, arrived.reshape(planes, DEEP, PAGE, -1), done
    )
    pieces = lax.all_to_all(pieces, "req", 0, 0, tiled=True, axis_index_groups=column)
    partial = join(pieces, own, w_out)
    other = lax.ppermute(partial, "head", swap)
    verify_out, _ = finish(side, partial, other, verify_x, post_gain[None], "finish_drafts")
    return (verify_out, prefill_out, verify_kv, prefill_kv)


def solution(mesh):
    devices = mesh.shape["req"]
    plane = [list(range(z, devices, DEEP)) for z in range(DEEP)]
    placed = (
        P("req", None, None),
        P("req", None),
        P(),
        P(None, "head"),
        P(None, "head"),
        P(),
        P("head", None),
        P(),
        P("req", None, "head"),
        P("req", None),
        P("req", None),
        P("req"),
        P("req", None),
        P("req"),
    )
    return jax.shard_map(
        functools.partial(on_device, plane),
        mesh=mesh,
        in_specs=placed,
        out_specs=(
            P("req", None, "head"),
            P("req", "head"),
            P("req", None, "head"),
            P("req", "head"),
        ),
        check_vma=False,
    )
```

```python
import functools

import jax
import jax.numpy as jnp
import numpy as np
from jax import lax
from jax.experimental import pallas as pl
from jax.experimental.pallas import tpu as pltpu
from jax.sharding import PartitionSpec as P

HEAD = 256
PAGE = 16
QH = 4
PAD = 8
DEEP = 8
eps_norm = 1e-06
rope_base = 1000000.0
neg_large = -1e30
bf16, f32, i32 = jnp.bfloat16, jnp.float32, jnp.int32
HBM = pl.BlockSpec(memory_space=pltpu.MemorySpace.HBM)
VMEM = pl.BlockSpec(memory_space=pltpu.MemorySpace.VMEM)
TOKEN = jax.ShapeDtypeStruct((8, 128), f32)
SMEM = pl.BlockSpec(memory_space=pltpu.MemorySpace.SMEM)


def dot_t(a, b):
    return lax.dot_general(a, b, (((1,), (1,)), ((), ())), preferred_element_type=f32)


def dot_n(a, b):
    return jnp.dot(a, b, preferred_element_type=f32)


def iota(shape, dim):
    return lax.broadcasted_iota(i32, shape, dim)


def unit(values):
    return values * lax.rsqrt(jnp.mean(values * values, axis=-1, keepdims=True) + eps_norm)


def tally(table, length, lanes, first, step):
    slots = table.shape[1]
    eye = iota((slots, slots), 0) == iota((slots, slots), 1)
    page = jnp.sum(jnp.where(eye, table, 0), axis=1, keepdims=True)
    base = iota((slots, 1), 0) * PAGE
    lane = iota((slots, lanes), 1)
    named = page == first + (lane >> 4) * step
    valid = base + (lane & (PAGE - 1)) < length
    return jnp.sum(jnp.where(named & valid, 1.0, 0.0), axis=0, keepdims=True)


def pick_kernel(index, pool, out, token):
    token[...] = jnp.zeros_like(token)
    for i in range(out.shape[0]):
        out[i] = pool[jnp.clip(index[0, i], 0, pool.shape[0] - 1)]


def pick_pages(index, pool):
    count = index.shape[1]
    return pl.pallas_call(
        pick_kernel,
        in_specs=[SMEM, VMEM],
        out_specs=[VMEM, VMEM],
        out_shape=[jax.ShapeDtypeStruct((count,) + pool.shape[1:], pool.dtype), TOKEN],
        cost_estimate=pl.CostEstimate(flops=0, transcendentals=0, bytes_accessed=4 << 20),
        name="pick_pages",
    )(index, pool)


def project_kernel(
    meta, lengths, x, draft, gain, wq, wkv, qk_gain, freq, table,
    queries, prompt_kv, near_kv, sent, draft_kv, own_count, verify_kv,
    weights, normed, wide, rows_q, sems,
):
    rows, drafted = x.shape[0], draft.shape[1]
    copies = []
    for h in range(3):
        part = wq.at[:, h * 2 * HEAD : (h + 1) * 2 * HEAD] if h < 2 else wkv
        copy = pltpu.make_async_copy(part, weights.at[h], sems.at[h])
        copy.start()
        copies.append(copy)

    normed[:rows] = (unit(x[...].astype(f32)) * gain[...]).astype(bf16)
    wide[...] = jnp.zeros_like(wide)
    wide[:drafted] = unit(draft[0].astype(f32)) * gain[...]
    normed[rows:] = wide[...].astype(bf16)

    own_count[...] = tally(table[...], meta[0], own_count.shape[1], 0, 1)

    half = HEAD // 2
    row = iota((normed.shape[0], half), 0)
    start = jnp.zeros_like(row)
    end = jnp.int32(0)
    for i in range(3):
        end = end + lengths[0, i]
        start = jnp.where(row >= end, end, start)
    position = jnp.where(row < rows, row - start, row - rows + meta[0])
    angles = position.astype(f32) * freq[...]
    cos, sin = jnp.cos(angles), jnp.sin(angles)

    def rotated(values):
        a, b = values[:, :half], values[:, half:]
        return jnp.concatenate([a * cos - b * sin, b * cos + a * sin], axis=-1)

    keep = iota((PAD, HEAD), 0) < meta[1]

    for pair in range(3):
        copies[pair].wait()
        both = dot_n(normed[...], weights[pair])
        for j in range(2):
            h = 2 * pair + j
            value = unit(both[:, j * HEAD : (j + 1) * HEAD])
            if h < QH:
                query = rotated(value * qk_gain[0:1, :])
                queries[h] = query[:rows].astype(bf16)
                mine = query[rows : rows + PAD]
                rows_q[h * PAD : (h + 1) * PAD, :] = mine
                continue
            if h == QH:
                value = rotated(value * qk_gain[1:2, :])
            cols = slice(j * HEAD, (j + 1) * HEAD)
            prompt_kv[:, cols] = value[:rows].astype(bf16)
            near_kv[:, cols] = value[:rows].astype(bf16)
            mine = value[rows : rows + PAD]
            draft_kv[:, cols] = mine
            verify_kv[0, :, cols] = jnp.where(keep, mine, 0.0)[:drafted].astype(bf16)
    sent[...] = rows_q[...].astype(bf16)


def project(meta, lengths, x, draft, gain, wq, wkv, qk_gain, freq, table, own):
    rows, width = x.shape
    drafted = draft.shape[1]
    total = rows + 16
    shapes = [
        jax.ShapeDtypeStruct((QH, rows, HEAD), bf16),
        jax.ShapeDtypeStruct((rows, 2 * HEAD), bf16),
        jax.ShapeDtypeStruct((rows, 2 * HEAD), bf16),
        jax.ShapeDtypeStruct((QH * PAD, HEAD), bf16),
        jax.ShapeDtypeStruct((PAD, 2 * HEAD), f32),
        jax.ShapeDtypeStruct((1, own), f32),
        jax.ShapeDtypeStruct((1, drafted, 2 * HEAD), bf16),
    ]
    return pl.pallas_call(
        project_kernel,
        in_specs=[SMEM, SMEM, VMEM, VMEM, VMEM, HBM, HBM, VMEM, VMEM, VMEM],
        out_specs=[VMEM] * len(shapes),
        out_shape=shapes,
        scratch_shapes=[
            pltpu.VMEM((3, width, 2 * HEAD), bf16),
            pltpu.VMEM((total, width), bf16),
            pltpu.VMEM((16, width), f32),
            pltpu.VMEM((QH * PAD, HEAD), f32),
            pltpu.SemaphoreType.DMA((3,)),
        ],
        compiler_params=pltpu.CompilerParams(vmem_limit_bytes=55 << 20),
        cost_estimate=pl.CostEstimate(
            flops=2 * total * width * 6 * HEAD, transcendentals=0, bytes_accessed=9 << 20
        ),
        name="project",
    )(meta, lengths, x, draft, gain, wq, wkv, qk_gain, freq, table)


def pack_kernel(meta, draft, table, after, out, wide):
    drafted, slots = draft.shape[1], table.shape[1]
    wide[...] = jnp.zeros_like(wide)
    wide[:drafted] = draft[0].astype(f32)
    lane = iota((1, 128), 1)
    size = jnp.where(lane == slots, meta[0] >> 3, jnp.where(lane == slots + 1, meta[0] & 7, 0))
    wide[5:6, :128] = size.astype(f32)
    wide[5:6, :slots] = table[...].astype(f32)
    out[0] = wide[...].astype(bf16)


def pack(meta, draft, table, after):
    width = draft.shape[2]
    return pl.pallas_call(
        pack_kernel,
        in_specs=[SMEM, VMEM, VMEM, VMEM],
        out_specs=VMEM,
        out_shape=jax.ShapeDtypeStruct((1, PAD, width), bf16),
        scratch_shapes=[pltpu.VMEM((PAD, width), f32)],
        compiler_params=pltpu.CompilerParams(vmem_limit_bytes=4 << 20),
        cost_estimate=pl.CostEstimate(flops=0, transcendentals=0, bytes_accessed=1 << 17),
        name="pack",
    )(meta, draft, table, after)


def ask_kernel(where, x, gain, wq, qk_gain, freq, out, weights, sems):
    groups = x.shape[0]
    copies = []
    for i in range(2):
        cols = slice(i * 2 * HEAD, (i + 1) * 2 * HEAD)
        copy = pltpu.make_async_copy(wq.at[:, cols], weights.at[i], sems.at[i])
        copy.start()
        copies.append(copy)
    rows = x[...].astype(f32).reshape(groups * PAD, -1)
    normed = (unit(rows) * gain[...]).astype(bf16)
    half = HEAD // 2
    counts, starts = [], []
    for e in range(groups):
        note = x[e][5:6, :128].astype(f32).astype(i32)
        size = jnp.sum(jnp.where(iota((1, 128), 1) == 64, note * 8, 0), keepdims=True)
        size += jnp.sum(jnp.where(iota((1, 128), 1) == 65, note, 0), keepdims=True)
        starts.append(jnp.broadcast_to(size, (PAD, half)))
        counts.append(tally(note[:, :64], size, HEAD, 64 + where[0], DEEP))
    count = jnp.concatenate(counts, axis=0).reshape(groups, 1, HEAD)
    position = jnp.concatenate(starts, axis=0) + (iota((groups * PAD, half), 0) & (PAD - 1))
    angles = position.astype(f32) * freq[...]
    cos, sin = jnp.cos(angles), jnp.sin(angles)
    mark = iota((groups, PAD, HEAD), 1) == 5
    heads = []
    for i in range(2):
        copies[i].wait()
        both = dot_n(normed, weights[i])
        for j in range(2):
            value = unit(both[:, j * HEAD : (j + 1) * HEAD]) * qk_gain[0:1, :]
            a, b = value[:, :half], value[:, half:]
            value = jnp.concatenate([a * cos - b * sin, b * cos + a * sin], axis=-1)
            value = value.reshape(groups, PAD, HEAD)
            heads.append(jnp.where(mark, count, value) if not heads else value)
    out[...] = jnp.concatenate(heads, axis=1).astype(bf16)


def ask(where, x, gain, wq, qk_gain, freq):
    groups, _, width = x.shape
    return pl.pallas_call(
        ask_kernel,
        in_specs=[SMEM, VMEM, VMEM, HBM, VMEM, VMEM],
        out_specs=VMEM,
        out_shape=jax.ShapeDtypeStruct((groups, QH * PAD, HEAD), bf16),
        scratch_shapes=[
            pltpu.VMEM((2, width, 2 * HEAD), bf16),
            pltpu.SemaphoreType.DMA((2,)),
        ],
        compiler_params=pltpu.CompilerParams(vmem_limit_bytes=50 << 20),
        cost_estimate=pl.CostEstimate(
            flops=2 * groups * PAD * width * QH * HEAD, transcendentals=0, bytes_accessed=5 << 20
        ),
        name="ask",
    )(where, x, gain, wq, qk_gain, freq)


def prompt_kernel(
    lengths, q, kv, query, draft_kv, pages, count, w_out, out, local, attn, weights, pool, sems, pool_sem
):
    fetch = pltpu.make_async_copy(pages, pool, pool_sem)
    fetch.start()
    split = sems.shape[0]
    cols = out.shape[1] // split
    copies = []
    for i in range(split):
        part = slice(i * cols, (i + 1) * cols)
        copy = pltpu.make_async_copy(w_out.at[:, part], weights.at[:, part], sems.at[i])
        copy.start()
        copies.append(copy)
    rows = attn.shape[0]
    row, col = iota((rows, rows), 0), iota((rows, rows), 1)
    start = jnp.zeros((rows, rows), i32)
    end = jnp.int32(0)
    for i in range(3):
        end = end + lengths[0, i]
        start = jnp.where(row >= end, end, start)
    allowed = (col <= row) & (col >= start)
    key, value = kv[:, :HEAD], kv[:, HEAD:]
    for h in range(QH):
        scores = jnp.where(allowed, dot_t(q[h], key), neg_large)
        parts = jnp.exp(scores - jnp.max(scores, axis=-1, keepdims=True))
        probs = (parts / jnp.sum(parts, axis=-1, keepdims=True)).astype(bf16)
        attn[:, h * HEAD : (h + 1) * HEAD] = dot_n(probs, value).astype(bf16)

    fetch.wait()
    mine = query[...]
    times = count[...]
    scores = jnp.where(times > 0.0, dot_t(mine, pool[:, :HEAD]), neg_large)
    fresh = dot_t(mine, draft_kv[:, :HEAD].astype(bf16))
    allowed = iota(fresh.shape, 1) <= (iota(fresh.shape, 0) & (PAD - 1))
    fresh = jnp.where(allowed, fresh, neg_large)
    peak = jnp.maximum(
        jnp.max(scores, axis=-1, keepdims=True), jnp.max(fresh, axis=-1, keepdims=True)
    )
    parts = jnp.where(times > 0.0, jnp.exp(scores - peak) * times, 0.0)
    fresh = jnp.where(allowed, jnp.exp(fresh - peak), 0.0)
    denom = jnp.sum(parts, axis=-1, keepdims=True) + jnp.sum(fresh, axis=-1, keepdims=True)
    local[:, :HEAD] = dot_n(parts.astype(bf16), pool[:, HEAD:]) + dot_n(
        fresh.astype(bf16), draft_kv[:, HEAD:].astype(bf16)
    )
    local[:, HEAD : HEAD + 128] = jnp.broadcast_to(peak, (QH * PAD, 128))
    local[:, HEAD + 128 :] = jnp.broadcast_to(denom, (QH * PAD, 128))

    for i in range(split):
        copies[i].wait()
        part = slice(i * cols, (i + 1) * cols)
        out[:, part] = dot_n(attn[...], weights[:, part]).astype(bf16)


def prompts(lengths, q, kv, query, draft_kv, pool, count, w_out):
    rows = kv.shape[0]
    depth, width = w_out.shape
    return pl.pallas_call(
        prompt_kernel,
        in_specs=[SMEM] + [VMEM] * 4 + [HBM, VMEM, HBM],
        out_specs=[VMEM, VMEM],
        out_shape=[
            jax.ShapeDtypeStruct((rows, width), bf16),
            jax.ShapeDtypeStruct((QH * PAD, 2 * HEAD), f32),
        ],
        scratch_shapes=[
            pltpu.VMEM((rows, depth), bf16),
            pltpu.VMEM((depth, width), bf16),
            pltpu.VMEM(pool.shape, bf16),
            pltpu.SemaphoreType.DMA((4,)),
            pltpu.SemaphoreType.DMA,
        ],
        compiler_params=pltpu.CompilerParams(vmem_limit_bytes=54 << 20),
        cost_estimate=pl.CostEstimate(
            flops=16 * rows * rows * HEAD, transcendentals=4 * rows * rows, bytes_accessed=4 << 20
        ),
        name="prompts",
    )(lengths, q, kv, query, draft_kv, pool, count, w_out)


def remote_kernel(where, queries, pages, after, out):
    here = where[0]
    groups, rows = queries.shape[0], queries.shape[1]
    asked = [here ^ mask for mask in ORDER]
    scores, counts = [], []
    for e in range(groups):
        query = queries[e]
        count = query.astype(f32)[5:6, :]
        held = pages[:, asked[e], :, :HEAD].reshape(HEAD, HEAD)
        scores.append(jnp.where(count > 0.0, dot_t(query, held), neg_large))
        counts.append(jnp.broadcast_to(count, (rows, HEAD)))
    score = jnp.concatenate(scores, axis=0)
    count = jnp.concatenate(counts, axis=0)
    peak = jnp.max(score, axis=-1, keepdims=True).astype(bf16).astype(f32)
    parts = jnp.where(count > 0.0, jnp.exp(score - peak) * count, 0.0)
    denom = jnp.sum(parts, axis=-1, keepdims=True)
    high = denom.astype(bf16).astype(f32)

    shape = (groups * rows // PAD, PAD, 128)
    token, lane = iota(shape, 1), iota(shape, 2)

    def along(values):
        wide = jnp.broadcast_to(values, (groups * rows, 128)).reshape(shape)
        wide = jnp.sum(jnp.where(token == lane, wide, 0.0), axis=1, keepdims=True)
        return jnp.broadcast_to(wide, shape)

    stats = jnp.where(
        token == 5, along(peak), jnp.where(token == 6, along(high), along(denom - high))
    ).reshape(groups * rows, 128)
    spare = (iota((rows, 128), 0) & (PAD - 1)) >= 5
    parts = parts.astype(bf16)
    for e in range(groups):
        own = slice(e * rows, (e + 1) * rows)
        held = pages[:, asked[e], :, HEAD:].reshape(HEAD, HEAD)
        total = dot_n(parts[own], held)
        out[asked[e], :, :128] = jnp.where(spare, stats[own], total[:, :128]).astype(bf16)
        out[asked[e], :, 128:] = total[:, 128:].astype(bf16)


ORDER = (0, 4, 2, 6, 1, 5, 3, 7)


def remote_pieces(where, queries, pages, after):
    groups, rows, _ = queries.shape
    return pl.pallas_call(
        remote_kernel,
        in_specs=[SMEM, VMEM, VMEM, VMEM],
        out_specs=VMEM,
        out_shape=jax.ShapeDtypeStruct((groups, rows, HEAD), bf16),
        compiler_params=pltpu.CompilerParams(vmem_limit_bytes=12 << 20),
        cost_estimate=pl.CostEstimate(flops=1 << 26, transcendentals=1 << 16, bytes_accessed=3 << 20),
        name="remote_pieces",
    )(where, queries, pages, after)


def join_kernel(pieces, local, w_out, out, attn, weights, sems):
    depth, width = w_out.shape
    parts = sems.shape[0]
    cols = width // parts
    copies = []
    for i in range(parts):
        part = slice(i * cols, (i + 1) * cols)
        copy = pltpu.make_async_copy(w_out.at[:, part], weights.at[:, part], sems.at[i])
        copy.start()
        copies.append(copy)
    groups, rows = pieces.shape[0], pieces.shape[1]
    shape = (groups * rows // PAD, PAD, 128)
    token, lane = iota(shape, 1), iota(shape, 2)
    spare = pieces[:, :, :128].astype(f32).reshape(shape)

    def upright(which):
        row = jnp.sum(jnp.where(token == which, spare, 0.0), axis=1, keepdims=True)
        row = jnp.where(token == lane, jnp.broadcast_to(row, shape), 0.0)
        return jnp.sum(row, axis=2, keepdims=True).reshape(groups, rows, 1)

    peaks = upright(5)
    sums = upright(6) + upright(7)
    own = local[:, HEAD : HEAD + 1]
    top = jnp.maximum(jnp.max(peaks, axis=0), own)
    scale = jnp.exp(peaks - top[None])
    near = jnp.exp(own - top)
    total = local[:, :HEAD] * near + jnp.sum(pieces[...].astype(f32) * scale, axis=0)
    denom = local[:, HEAD + 128 : HEAD + 129] * near + jnp.sum(sums * scale, axis=0)
    attn[...] = total / denom
    heads = [attn[h * PAD : (h + 1) * PAD, :].astype(bf16) for h in range(QH)]
    for i in range(parts):
        copies[i].wait()
        part = slice(i * cols, (i + 1) * cols)
        out[:, part] = functools.reduce(
            jnp.add,
            [dot_n(heads[h], weights[h * HEAD : (h + 1) * HEAD, part]) for h in range(QH)],
        )


def join(pieces, local, w_out):
    depth, width = w_out.shape
    return pl.pallas_call(
        join_kernel,
        in_specs=[VMEM, VMEM, HBM],
        out_specs=VMEM,
        out_shape=jax.ShapeDtypeStruct((PAD, width), f32),
        scratch_shapes=[
            pltpu.VMEM((QH * PAD, HEAD), f32),
            pltpu.VMEM((depth, width), bf16),
            pltpu.SemaphoreType.DMA((4,)),
        ],
        compiler_params=pltpu.CompilerParams(vmem_limit_bytes=50 << 20),
        cost_estimate=pl.CostEstimate(flops=1 << 25, transcendentals=0, bytes_accessed=4 << 20),
        name="join",
    )(pieces, local, w_out)


def finish_kernel(side, own, other, x, gain, out, token):
    token[...] = jnp.zeros_like(token)
    half = out.shape[-1]
    total = own[...].astype(f32) + other[...].astype(f32)
    scale = lax.rsqrt(jnp.mean(total * total, axis=-1, keepdims=True) + eps_norm)
    mine = jnp.where(side[0] == 0, total[:, :half], total[:, half:]) * scale * gain[...]
    if len(out.shape) == 3:
        out[0] = (x[0].astype(f32) + mine[: out.shape[1]]).astype(bf16)
    else:
        out[...] = (x[...].astype(f32) + mine).astype(bf16)


def finish(side, own, other, x, gain, name):
    rows, width = own.shape
    half = width // 2
    block = min(rows, 128)
    if x.ndim == 3:
        shape = x.shape[:2] + (half,)
        x_spec = pl.BlockSpec(shape, lambda i, s: (0, 0, s[0]))
        o_spec = pl.BlockSpec(shape, lambda i, s: (0, 0, 0))
    else:
        shape = (rows, half)
        x_spec = pl.BlockSpec((block, half), lambda i, s: (i, s[0]))
        o_spec = pl.BlockSpec((block, half), lambda i, s: (i, 0))
    return pl.pallas_call(
        finish_kernel,
        grid_spec=pltpu.PrefetchScalarGridSpec(
            num_scalar_prefetch=1,
            grid=(rows // block,),
            in_specs=[
                pl.BlockSpec((block, width), lambda i, s: (i, 0)),
                pl.BlockSpec((block, width), lambda i, s: (i, 0)),
                x_spec,
                pl.BlockSpec((1, half), lambda i, s: (0, s[0])),
            ],
            out_specs=[o_spec, pl.BlockSpec(TOKEN.shape, lambda i, s: (0, 0))],
        ),
        out_shape=[jax.ShapeDtypeStruct(shape, bf16), TOKEN],
        compiler_params=pltpu.CompilerParams(vmem_limit_bytes=12 << 20),
        cost_estimate=pl.CostEstimate(
            flops=8 * rows * width, transcendentals=0, bytes_accessed=6 * rows * width
        ),
        name=name,
    )(side, own, other, x, gain)


def on_device(
    plane,
    verify_x,
    prefill_x,
    attn_gain,
    w_query,
    w_keyval,
    qk_gain,
    w_out,
    post_gain,
    page_pool,
    outbound,
    page_table,
    cache_len,
    prompt_len,
    accepted,
):
    devices = outbound.shape[1]
    rows = prefill_x.shape[0]
    pool_pages = page_pool.shape[0]
    planes = len(plane[0])
    column = [list(range(i, i + DEEP)) for i in range(0, devices, DEEP)]

    outgoing, picked = pick_pages(outbound, page_pool)
    outgoing, prefill_x, cache_len = lax.optimization_barrier((outgoing, prefill_x, cache_len))
    arrived = lax.all_to_all(outgoing, "req", 0, 0, tiled=True, axis_index_groups=plane)

    meta = jnp.where(jnp.arange(8, dtype=i32) == 0, cache_len, accepted)
    side = lax.axis_index("head").reshape(1)
    where = (lax.axis_index("req") & (DEEP - 1)).reshape(1)
    swap = [(0, 1), (1, 0)]

    def beside(values, mask):
        pairs = [(i, i ^ mask) for i in range(devices)]
        return jnp.concatenate([values, lax.ppermute(values, "req", pairs)], axis=0)

    asked = beside(pack(meta, verify_x, page_table, picked), 4)

    power = -(np.arange(HEAD // 2, dtype=np.float64) * 2.0) / HEAD
    freq = jnp.asarray((rope_base**power)[None], f32)
    queries, prefill_kv, near_kv, sent, draft_kv, own_count, verify_kv = project(
        meta, prompt_len, prefill_x, verify_x, attn_gain[None], w_query, w_keyval,
        qk_gain, freq, page_table, pool_pages * PAGE,
    )
    asked, queries = lax.optimization_barrier((asked, queries))
    asked = beside(asked, 2)
    partial, own = prompts(
        prompt_len, queries, near_kv, sent, draft_kv,
        page_pool.reshape(pool_pages * PAGE, -1), own_count, w_out,
    )
    asked, partial = lax.optimization_barrier((asked, partial))
    asked = beside(asked, 1)
    other = lax.ppermute(partial, "head", swap)
    prefill_out, done = finish(side, partial, other, prefill_x, post_gain[None], "finish_prompts")

    queries = ask(where, asked, attn_gain[None], w_query, qk_gain, freq)
    pieces = remote_pieces(
        where, queries, arrived.reshape(planes, DEEP, PAGE, -1), done
    )
    pieces = lax.all_to_all(pieces, "req", 0, 0, tiled=True, axis_index_groups=column)
    partial = join(pieces, own, w_out)
    other = lax.ppermute(partial, "head", swap)
    verify_out, _ = finish(side, partial, other, verify_x, post_gain[None], "finish_drafts")
    return (verify_out, prefill_out, verify_kv, prefill_kv)


def solution(mesh):
    devices = mesh.shape["req"]
    plane = [list(range(z, devices, DEEP)) for z in range(DEEP)]
    placed = (
        P("req", None, None),
        P("req", None),
        P(),
        P(None, "head"),
        P(None, "head"),
        P(),
        P("head", None),
        P(),
        P("req", None, "head"),
        P("req", None),
        P("req", None),
        P("req"),
        P("req", None),
        P("req"),
    )
    return jax.shard_map(
        functools.partial(on_device, plane),
        mesh=mesh,
        in_specs=placed,
        out_specs=(
            P("req", None, "head"),
            P("req", "head"),
            P("req", None, "head"),
            P("req", "head"),
        ),
        check_vma=False,
    )
```

```python
import functools

import jax
import jax.numpy as jnp
import numpy as np
from jax import lax
from jax.experimental import pallas as pl
from jax.experimental.pallas import tpu as pltpu
from jax.sharding import PartitionSpec as P

HEAD = 256
PAGE = 16
QH = 4
PAD = 8
DEEP = 8
eps_norm = 1e-06
rope_base = 1000000.0
neg_large = -1e30
bf16, f32, i32 = jnp.bfloat16, jnp.float32, jnp.int32
HBM = pl.BlockSpec(memory_space=pltpu.MemorySpace.HBM)
VMEM = pl.BlockSpec(memory_space=pltpu.MemorySpace.VMEM)
TOKEN = jax.ShapeDtypeStruct((8, 128), f32)
SMEM = pl.BlockSpec(memory_space=pltpu.MemorySpace.SMEM)


def dot_t(a, b):
    return lax.dot_general(a, b, (((1,), (1,)), ((), ())), preferred_element_type=f32)


def dot_n(a, b):
    return jnp.dot(a, b, preferred_element_type=f32)


def iota(shape, dim):
    return lax.broadcasted_iota(i32, shape, dim)


def unit(values):
    return values * lax.rsqrt(jnp.mean(values * values, axis=-1, keepdims=True) + eps_norm)


def tally(table, length, lanes, first, step):
    slots = table.shape[1]
    eye = iota((slots, slots), 0) == iota((slots, slots), 1)
    page = jnp.sum(jnp.where(eye, table, 0), axis=1, keepdims=True)
    base = iota((slots, 1), 0) * PAGE
    lane = iota((slots, lanes), 1)
    named = page == first + (lane >> 4) * step
    valid = base + (lane & (PAGE - 1)) < length
    return jnp.sum(jnp.where(named & valid, 1.0, 0.0), axis=0, keepdims=True)


def pick_kernel(index, pool, out, token):
    token[...] = jnp.zeros_like(token)
    for i in range(out.shape[0]):
        out[i] = pool[jnp.clip(index[0, i], 0, pool.shape[0] - 1)]


def pick_pages(index, pool):
    count = index.shape[1]
    return pl.pallas_call(
        pick_kernel,
        in_specs=[SMEM, VMEM],
        out_specs=[VMEM, VMEM],
        out_shape=[jax.ShapeDtypeStruct((count,) + pool.shape[1:], pool.dtype), TOKEN],
        cost_estimate=pl.CostEstimate(flops=0, transcendentals=0, bytes_accessed=4 << 20),
        name="pick_pages",
    )(index, pool)


def project_kernel(
    meta, lengths, x, draft, gain, wq, wkv, qk_gain, freq, table,
    queries, prompt_kv, near_kv, sent, draft_kv, own_count, verify_kv,
    weights, normed, wide, rows_q, sems,
):
    rows, drafted = x.shape[0], draft.shape[1]
    copies = []
    for h in range(3):
        part = wq.at[:, h * 2 * HEAD : (h + 1) * 2 * HEAD] if h < 2 else wkv
        copy = pltpu.make_async_copy(part, weights.at[h], sems.at[h])
        copy.start()
        copies.append(copy)

    normed[:rows] = (unit(x[...].astype(f32)) * gain[...]).astype(bf16)
    wide[...] = jnp.zeros_like(wide)
    wide[:drafted] = unit(draft[0].astype(f32)) * gain[...]
    normed[rows:] = wide[...].astype(bf16)

    own_count[...] = tally(table[...], meta[0], own_count.shape[1], 0, 1)

    half = HEAD // 2
    row = iota((normed.shape[0], half), 0)
    start = jnp.zeros_like(row)
    end = jnp.int32(0)
    for i in range(3):
        end = end + lengths[0, i]
        start = jnp.where(row >= end, end, start)
    position = jnp.where(row < rows, row - start, row - rows + meta[0])
    angles = position.astype(f32) * freq[...]
    cos, sin = jnp.cos(angles), jnp.sin(angles)

    def rotated(values):
        a, b = values[:, :half], values[:, half:]
        return jnp.concatenate([a * cos - b * sin, b * cos + a * sin], axis=-1)

    keep = iota((PAD, HEAD), 0) < meta[1]

    for pair in range(3):
        copies[pair].wait()
        both = dot_n(normed[...], weights[pair])
        for j in range(2):
            h = 2 * pair + j
            value = unit(both[:, j * HEAD : (j + 1) * HEAD])
            if h < QH:
                query = rotated(value * qk_gain[0:1, :])
                queries[h] = query[:rows].astype(bf16)
                mine = query[rows : rows + PAD]
                rows_q[h * PAD : (h + 1) * PAD, :] = mine
                continue
            if h == QH:
                value = rotated(value * qk_gain[1:2, :])
            cols = slice(j * HEAD, (j + 1) * HEAD)
            prompt_kv[:, cols] = value[:rows].astype(bf16)
            near_kv[:, cols] = value[:rows].astype(bf16)
            mine = value[rows : rows + PAD]
            draft_kv[:, cols] = mine
            verify_kv[0, :, cols] = jnp.where(keep, mine, 0.0)[:drafted].astype(bf16)
    sent[...] = rows_q[...].astype(bf16)


def project(meta, lengths, x, draft, gain, wq, wkv, qk_gain, freq, table, own):
    rows, width = x.shape
    drafted = draft.shape[1]
    total = rows + 16
    shapes = [
        jax.ShapeDtypeStruct((QH, rows, HEAD), bf16),
        jax.ShapeDtypeStruct((rows, 2 * HEAD), bf16),
        jax.ShapeDtypeStruct((rows, 2 * HEAD), bf16),
        jax.ShapeDtypeStruct((QH * PAD, HEAD), bf16),
        jax.ShapeDtypeStruct((PAD, 2 * HEAD), f32),
        jax.ShapeDtypeStruct((1, own), f32),
        jax.ShapeDtypeStruct((1, drafted, 2 * HEAD), bf16),
    ]
    return pl.pallas_call(
        project_kernel,
        in_specs=[SMEM, SMEM, VMEM, VMEM, VMEM, HBM, HBM, VMEM, VMEM, VMEM],
        out_specs=[VMEM] * len(shapes),
        out_shape=shapes,
        scratch_shapes=[
            pltpu.VMEM((3, width, 2 * HEAD), bf16),
            pltpu.VMEM((total, width), bf16),
            pltpu.VMEM((16, width), f32),
            pltpu.VMEM((QH * PAD, HEAD), f32),
            pltpu.SemaphoreType.DMA((3,)),
        ],
        compiler_params=pltpu.CompilerParams(vmem_limit_bytes=55 << 20),
        cost_estimate=pl.CostEstimate(
            flops=2 * total * width * 6 * HEAD, transcendentals=0, bytes_accessed=9 << 20
        ),
        name="project",
    )(meta, lengths, x, draft, gain, wq, wkv, qk_gain, freq, table)


def pack_kernel(meta, draft, table, after, out, wide):
    drafted, slots = draft.shape[1], table.shape[1]
    wide[...] = jnp.zeros_like(wide)
    wide[:drafted] = draft[0].astype(f32)
    lane = iota((1, 128), 1)
    size = jnp.where(lane == slots, meta[0] >> 3, jnp.where(lane == slots + 1, meta[0] & 7, 0))
    wide[5:6, :128] = size.astype(f32)
    wide[5:6, :slots] = table[...].astype(f32)
    out[0] = wide[...].astype(bf16)


def pack(meta, draft, table, after):
    width = draft.shape[2]
    return pl.pallas_call(
        pack_kernel,
        in_specs=[SMEM, VMEM, VMEM, VMEM],
        out_specs=VMEM,
        out_shape=jax.ShapeDtypeStruct((1, PAD, width), bf16),
        scratch_shapes=[pltpu.VMEM((PAD, width), f32)],
        compiler_params=pltpu.CompilerParams(vmem_limit_bytes=4 << 20),
        cost_estimate=pl.CostEstimate(flops=0, transcendentals=0, bytes_accessed=1 << 17),
        name="pack",
    )(meta, draft, table, after)


def ask_kernel(where, x, gain, wq, qk_gain, freq, out, weights, sems):
    groups = x.shape[0]
    copies = []
    for i in range(2):
        cols = slice(i * 2 * HEAD, (i + 1) * 2 * HEAD)
        copy = pltpu.make_async_copy(wq.at[:, cols], weights.at[i], sems.at[i])
        copy.start()
        copies.append(copy)
    rows = x[...].astype(f32).reshape(groups * PAD, -1)
    normed = (unit(rows) * gain[...]).astype(bf16)
    half = HEAD // 2
    counts, starts = [], []
    for e in range(groups):
        note = x[e][5:6, :128].astype(f32).astype(i32)
        size = jnp.sum(jnp.where(iota((1, 128), 1) == 64, note * 8, 0), keepdims=True)
        size += jnp.sum(jnp.where(iota((1, 128), 1) == 65, note, 0), keepdims=True)
        starts.append(jnp.broadcast_to(size, (PAD, half)))
        counts.append(tally(note[:, :64], size, HEAD, 64 + where[0], DEEP))
    count = jnp.concatenate(counts, axis=0).reshape(groups, 1, HEAD)
    position = jnp.concatenate(starts, axis=0) + (iota((groups * PAD, half), 0) & (PAD - 1))
    angles = position.astype(f32) * freq[...]
    cos, sin = jnp.cos(angles), jnp.sin(angles)
    mark = iota((groups, PAD, HEAD), 1) == 5
    heads = []
    for i in range(2):
        copies[i].wait()
        both = dot_n(normed, weights[i])
        for j in range(2):
            value = unit(both[:, j * HEAD : (j + 1) * HEAD]) * qk_gain[0:1, :]
            a, b = value[:, :half], value[:, half:]
            value = jnp.concatenate([a * cos - b * sin, b * cos + a * sin], axis=-1)
            value = value.reshape(groups, PAD, HEAD)
            heads.append(jnp.where(mark, count, value) if not heads else value)
    out[...] = jnp.concatenate(heads, axis=1).astype(bf16)


def ask(where, x, gain, wq, qk_gain, freq):
    groups, _, width = x.shape
    return pl.pallas_call(
        ask_kernel,
        in_specs=[SMEM, VMEM, VMEM, HBM, VMEM, VMEM],
        out_specs=VMEM,
        out_shape=jax.ShapeDtypeStruct((groups, QH * PAD, HEAD), bf16),
        scratch_shapes=[
            pltpu.VMEM((2, width, 2 * HEAD), bf16),
            pltpu.SemaphoreType.DMA((2,)),
        ],
        compiler_params=pltpu.CompilerParams(vmem_limit_bytes=50 << 20),
        cost_estimate=pl.CostEstimate(
            flops=2 * groups * PAD * width * QH * HEAD, transcendentals=0, bytes_accessed=5 << 20
        ),
        name="ask",
    )(where, x, gain, wq, qk_gain, freq)


def prompt_kernel(
    lengths, q, kv, query, draft_kv, pool, count, w_out, out, local, attn, weights, sems
):
    split = sems.shape[0]
    cols = out.shape[1] // split
    copies = []
    for i in range(split):
        part = slice(i * cols, (i + 1) * cols)
        copy = pltpu.make_async_copy(w_out.at[:, part], weights.at[:, part], sems.at[i])
        copy.start()
        copies.append(copy)
    rows = attn.shape[0]
    row, col = iota((rows, rows), 0), iota((rows, rows), 1)
    start = jnp.zeros((rows, rows), i32)
    end = jnp.int32(0)
    for i in range(3):
        end = end + lengths[0, i]
        start = jnp.where(row >= end, end, start)
    allowed = (col <= row) & (col >= start)
    key, value = kv[:, :HEAD], kv[:, HEAD:]
    for h in range(QH):
        scores = jnp.where(allowed, dot_t(q[h], key), neg_large)
        parts = jnp.exp(scores - jnp.max(scores, axis=-1, keepdims=True))
        probs = (parts / jnp.sum(parts, axis=-1, keepdims=True)).astype(bf16)
        attn[:, h * HEAD : (h + 1) * HEAD] = dot_n(probs, value).astype(bf16)

    mine = query[...]
    times = count[...]
    scores = jnp.where(times > 0.0, dot_t(mine, pool[:, :HEAD]), neg_large)
    fresh = dot_t(mine, draft_kv[:, :HEAD].astype(bf16))
    allowed = iota(fresh.shape, 1) <= (iota(fresh.shape, 0) & (PAD - 1))
    fresh = jnp.where(allowed, fresh, neg_large)
    peak = jnp.maximum(
        jnp.max(scores, axis=-1, keepdims=True), jnp.max(fresh, axis=-1, keepdims=True)
    )
    parts = jnp.where(times > 0.0, jnp.exp(scores - peak) * times, 0.0)
    fresh = jnp.where(allowed, jnp.exp(fresh - peak), 0.0)
    denom = jnp.sum(parts, axis=-1, keepdims=True) + jnp.sum(fresh, axis=-1, keepdims=True)
    local[:, :HEAD] = dot_n(parts.astype(bf16), pool[:, HEAD:]) + dot_n(
        fresh.astype(bf16), draft_kv[:, HEAD:].astype(bf16)
    )
    local[:, HEAD : HEAD + 128] = jnp.broadcast_to(peak, (QH * PAD, 128))
    local[:, HEAD + 128 :] = jnp.broadcast_to(denom, (QH * PAD, 128))

    for i in range(split):
        copies[i].wait()
        part = slice(i * cols, (i + 1) * cols)
        out[:, part] = dot_n(attn[...], weights[:, part]).astype(bf16)


def prompts(lengths, q, kv, query, draft_kv, pool, count, w_out):
    rows = kv.shape[0]
    depth, width = w_out.shape
    return pl.pallas_call(
        prompt_kernel,
        in_specs=[SMEM] + [VMEM] * 6 + [HBM],
        out_specs=[VMEM, VMEM],
        out_shape=[
            jax.ShapeDtypeStruct((rows, width), bf16),
            jax.ShapeDtypeStruct((QH * PAD, 2 * HEAD), f32),
        ],
        scratch_shapes=[
            pltpu.VMEM((rows, depth), bf16),
            pltpu.VMEM((depth, width), bf16),
            pltpu.SemaphoreType.DMA((4,)),
        ],
        compiler_params=pltpu.CompilerParams(vmem_limit_bytes=54 << 20),
        cost_estimate=pl.CostEstimate(
            flops=16 * rows * rows * HEAD, transcendentals=4 * rows * rows, bytes_accessed=4 << 20
        ),
        name="prompts",
    )(lengths, q, kv, query, draft_kv, pool, count, w_out)


def remote_kernel(where, queries, pages, after, out):
    here = where[0]
    groups, rows = queries.shape[0], queries.shape[1]
    asked = [here ^ mask for mask in ORDER]
    scores, counts = [], []
    for e in range(groups):
        query = queries[e]
        count = query.astype(f32)[5:6, :]
        held = pages[:, asked[e], :, :HEAD].reshape(HEAD, HEAD)
        scores.append(jnp.where(count > 0.0, dot_t(query, held), neg_large))
        counts.append(jnp.broadcast_to(count, (rows, HEAD)))
    score = jnp.concatenate(scores, axis=0)
    count = jnp.concatenate(counts, axis=0)
    peak = jnp.max(score, axis=-1, keepdims=True).astype(bf16).astype(f32)
    parts = jnp.where(count > 0.0, jnp.exp(score - peak) * count, 0.0)
    denom = jnp.sum(parts, axis=-1, keepdims=True)
    high = denom.astype(bf16).astype(f32)

    shape = (groups * rows // PAD, PAD, 128)
    token, lane = iota(shape, 1), iota(shape, 2)

    def along(values):
        wide = jnp.broadcast_to(values, (groups * rows, 128)).reshape(shape)
        wide = jnp.sum(jnp.where(token == lane, wide, 0.0), axis=1, keepdims=True)
        return jnp.broadcast_to(wide, shape)

    stats = jnp.where(
        token == 5, along(peak), jnp.where(token == 6, along(high), along(denom - high))
    ).reshape(groups * rows, 128)
    spare = (iota((rows, 128), 0) & (PAD - 1)) >= 5
    parts = parts.astype(bf16)
    for e in range(groups):
        own = slice(e * rows, (e + 1) * rows)
        held = pages[:, asked[e], :, HEAD:].reshape(HEAD, HEAD)
        total = dot_n(parts[own], held)
        out[asked[e], :, :128] = jnp.where(spare, stats[own], total[:, :128]).astype(bf16)
        out[asked[e], :, 128:] = total[:, 128:].astype(bf16)


ORDER = (0, 4, 2, 6, 1, 5, 3, 7)


def remote_pieces(where, queries, pages, after):
    groups, rows, _ = queries.shape
    return pl.pallas_call(
        remote_kernel,
        in_specs=[SMEM, VMEM, VMEM, VMEM],
        out_specs=VMEM,
        out_shape=jax.ShapeDtypeStruct((groups, rows, HEAD), bf16),
        compiler_params=pltpu.CompilerParams(vmem_limit_bytes=12 << 20),
        cost_estimate=pl.CostEstimate(flops=1 << 26, transcendentals=1 << 16, bytes_accessed=3 << 20),
        name="remote_pieces",
    )(where, queries, pages, after)


def join_kernel(pieces, local, w_out, out, attn, weights, sems):
    depth, width = w_out.shape
    parts = sems.shape[0]
    cols = width // parts
    copies = []
    for i in range(parts):
        part = slice(i * cols, (i + 1) * cols)
        copy = pltpu.make_async_copy(w_out.at[:, part], weights.at[:, part], sems.at[i])
        copy.start()
        copies.append(copy)
    groups, rows = pieces.shape[0], pieces.shape[1]
    shape = (groups * rows // PAD, PAD, 128)
    token, lane = iota(shape, 1), iota(shape, 2)
    spare = pieces[:, :, :128].astype(f32).reshape(shape)

    def upright(which):
        row = jnp.sum(jnp.where(token == which, spare, 0.0), axis=1, keepdims=True)
        row = jnp.where(token == lane, jnp.broadcast_to(row, shape), 0.0)
        return jnp.sum(row, axis=2, keepdims=True).reshape(groups, rows, 1)

    peaks = upright(5)
    sums = upright(6) + upright(7)
    own = local[:, HEAD : HEAD + 1]
    top = jnp.maximum(jnp.max(peaks, axis=0), own)
    scale = jnp.exp(peaks - top[None])
    near = jnp.exp(own - top)
    total = local[:, :HEAD] * near + jnp.sum(pieces[...].astype(f32) * scale, axis=0)
    denom = local[:, HEAD + 128 : HEAD + 129] * near + jnp.sum(sums * scale, axis=0)
    attn[...] = total / denom
    heads = [attn[h * PAD : (h + 1) * PAD, :].astype(bf16) for h in range(QH)]
    for i in range(parts):
        copies[i].wait()
        part = slice(i * cols, (i + 1) * cols)
        out[:, part] = functools.reduce(
            jnp.add,
            [dot_n(heads[h], weights[h * HEAD : (h + 1) * HEAD, part]) for h in range(QH)],
        )


def join(pieces, local, w_out):
    depth, width = w_out.shape
    return pl.pallas_call(
        join_kernel,
        in_specs=[VMEM, VMEM, HBM],
        out_specs=VMEM,
        out_shape=jax.ShapeDtypeStruct((PAD, width), f32),
        scratch_shapes=[
            pltpu.VMEM((QH * PAD, HEAD), f32),
            pltpu.VMEM((depth, width), bf16),
            pltpu.SemaphoreType.DMA((4,)),
        ],
        compiler_params=pltpu.CompilerParams(vmem_limit_bytes=50 << 20),
        cost_estimate=pl.CostEstimate(flops=1 << 25, transcendentals=0, bytes_accessed=4 << 20),
        name="join",
    )(pieces, local, w_out)


def finish_kernel(side, own, other, x, gain, out, token):
    token[...] = jnp.zeros_like(token)
    half = out.shape[-1]
    total = own[...].astype(f32) + other[...].astype(f32)
    scale = lax.rsqrt(jnp.mean(total * total, axis=-1, keepdims=True) + eps_norm)
    mine = jnp.where(side[0] == 0, total[:, :half], total[:, half:]) * scale * gain[...]
    if len(out.shape) == 3:
        out[0] = (x[0].astype(f32) + mine[: out.shape[1]]).astype(bf16)
    else:
        out[...] = (x[...].astype(f32) + mine).astype(bf16)


def finish(side, own, other, x, gain, name):
    rows, width = own.shape
    half = width // 2
    block = min(rows, 128)
    if x.ndim == 3:
        shape = x.shape[:2] + (half,)
        x_spec = pl.BlockSpec(shape, lambda i, s: (0, 0, s[0]))
        o_spec = pl.BlockSpec(shape, lambda i, s: (0, 0, 0))
    else:
        shape = (rows, half)
        x_spec = pl.BlockSpec((block, half), lambda i, s: (i, s[0]))
        o_spec = pl.BlockSpec((block, half), lambda i, s: (i, 0))
    return pl.pallas_call(
        finish_kernel,
        grid_spec=pltpu.PrefetchScalarGridSpec(
            num_scalar_prefetch=1,
            grid=(rows // block,),
            in_specs=[
                pl.BlockSpec((block, width), lambda i, s: (i, 0)),
                pl.BlockSpec((block, width), lambda i, s: (i, 0)),
                x_spec,
                pl.BlockSpec((1, half), lambda i, s: (0, s[0])),
            ],
            out_specs=[o_spec, pl.BlockSpec(TOKEN.shape, lambda i, s: (0, 0))],
        ),
        out_shape=[jax.ShapeDtypeStruct(shape, bf16), TOKEN],
        compiler_params=pltpu.CompilerParams(vmem_limit_bytes=12 << 20),
        cost_estimate=pl.CostEstimate(
            flops=8 * rows * width, transcendentals=0, bytes_accessed=6 * rows * width
        ),
        name=name,
    )(side, own, other, x, gain)


def on_device(
    plane,
    verify_x,
    prefill_x,
    attn_gain,
    w_query,
    w_keyval,
    qk_gain,
    w_out,
    post_gain,
    page_pool,
    outbound,
    page_table,
    cache_len,
    prompt_len,
    accepted,
):
    devices = outbound.shape[1]
    rows = prefill_x.shape[0]
    pool_pages = page_pool.shape[0]
    planes = len(plane[0])
    column = [list(range(i, i + DEEP)) for i in range(0, devices, DEEP)]

    outgoing, picked = pick_pages(outbound, page_pool)
    outgoing, prefill_x, cache_len = lax.optimization_barrier((outgoing, prefill_x, cache_len))
    arrived = lax.all_to_all(outgoing, "req", 0, 0, tiled=True, axis_index_groups=plane)

    meta = jnp.where(jnp.arange(8, dtype=i32) == 0, cache_len, accepted)
    side = lax.axis_index("head").reshape(1)
    where = (lax.axis_index("req") & (DEEP - 1)).reshape(1)
    swap = [(0, 1), (1, 0)]

    def beside(values, *masks):
        parts = [values]
        for mask in masks:
            pairs = [(i, i ^ mask) for i in range(devices)]
            parts.append(lax.ppermute(values, "req", pairs))
        return jnp.concatenate(parts, axis=0)

    asked = beside(pack(meta, verify_x, page_table, picked), 4)

    power = -(np.arange(HEAD // 2, dtype=np.float64) * 2.0) / HEAD
    freq = jnp.asarray((rope_base**power)[None], f32)
    queries, prefill_kv, near_kv, sent, draft_kv, own_count, verify_kv = project(
        meta, prompt_len, prefill_x, verify_x, attn_gain[None], w_query, w_keyval,
        qk_gain, freq, page_table, pool_pages * PAGE,
    )
    asked, queries = lax.optimization_barrier((asked, queries))
    asked = beside(asked, 2, 1, 3)
    partial, own = prompts(
        prompt_len, queries, near_kv, sent, draft_kv,
        page_pool.reshape(pool_pages * PAGE, -1), own_count, w_out,
    )
    asked, partial = lax.optimization_barrier((asked, partial))
    other = lax.ppermute(partial, "head", swap)
    prefill_out, done = finish(side, partial, other, prefill_x, post_gain[None], "finish_prompts")

    queries = ask(where, asked, attn_gain[None], w_query, qk_gain, freq)
    pieces = remote_pieces(
        where, queries, arrived.reshape(planes, DEEP, PAGE, -1), done
    )
    pieces = lax.all_to_all(pieces, "req", 0, 0, tiled=True, axis_index_groups=column)
    partial = join(pieces, own, w_out)
    other = lax.ppermute(partial, "head", swap)
    verify_out, _ = finish(side, partial, other, verify_x, post_gain[None], "finish_drafts")
    return (verify_out, prefill_out, verify_kv, prefill_kv)


def solution(mesh):
    devices = mesh.shape["req"]
    plane = [list(range(z, devices, DEEP)) for z in range(DEEP)]
    placed = (
        P("req", None, None),
        P("req", None),
        P(),
        P(None, "head"),
        P(None, "head"),
        P(),
        P("head", None),
        P(),
        P("req", None, "head"),
        P("req", None),
        P("req", None),
        P("req"),
        P("req", None),
        P("req"),
    )
    return jax.shard_map(
        functools.partial(on_device, plane),
        mesh=mesh,
        in_specs=placed,
        out_specs=(
            P("req", None, "head"),
            P("req", "head"),
            P("req", None, "head"),
            P("req", "head"),
        ),
        check_vma=False,
    )
```

```python
import functools

import jax
import jax.numpy as jnp
import numpy as np
from jax import lax
from jax.experimental import pallas as pl
from jax.experimental.pallas import tpu as pltpu
from jax.sharding import PartitionSpec as P

HEAD = 256
PAGE = 16
QH = 4
PAD = 8
DEEP = 8
eps_norm = 1e-06
rope_base = 1000000.0
neg_large = -1e30
bf16, f32, i32 = jnp.bfloat16, jnp.float32, jnp.int32
HBM = pl.BlockSpec(memory_space=pltpu.MemorySpace.HBM)
VMEM = pl.BlockSpec(memory_space=pltpu.MemorySpace.VMEM)
TOKEN = jax.ShapeDtypeStruct((8, 128), f32)
SMEM = pl.BlockSpec(memory_space=pltpu.MemorySpace.SMEM)


def dot_t(a, b):
    return lax.dot_general(a, b, (((1,), (1,)), ((), ())), preferred_element_type=f32)


def dot_n(a, b):
    return jnp.dot(a, b, preferred_element_type=f32)


def iota(shape, dim):
    return lax.broadcasted_iota(i32, shape, dim)


def unit(values):
    return values * lax.rsqrt(jnp.mean(values * values, axis=-1, keepdims=True) + eps_norm)


def tally(table, length, lanes, first, step):
    slots = table.shape[1]
    eye = iota((slots, slots), 0) == iota((slots, slots), 1)
    page = jnp.sum(jnp.where(eye, table, 0), axis=1, keepdims=True)
    base = iota((slots, 1), 0) * PAGE
    lane = iota((slots, lanes), 1)
    named = page == first + (lane >> 4) * step
    valid = base + (lane & (PAGE - 1)) < length
    return jnp.sum(jnp.where(named & valid, 1.0, 0.0), axis=0, keepdims=True)


def pick_kernel(index, pool, out, token):
    token[...] = jnp.zeros_like(token)
    for i in range(out.shape[0]):
        out[i] = pool[jnp.clip(index[0, i], 0, pool.shape[0] - 1)]


def pick_pages(index, pool):
    count = index.shape[1]
    return pl.pallas_call(
        pick_kernel,
        in_specs=[SMEM, VMEM],
        out_specs=[VMEM, VMEM],
        out_shape=[jax.ShapeDtypeStruct((count,) + pool.shape[1:], pool.dtype), TOKEN],
        cost_estimate=pl.CostEstimate(flops=0, transcendentals=0, bytes_accessed=4 << 20),
        name="pick_pages",
    )(index, pool)


def project_kernel(
    meta, lengths, x, draft, gain, wq, wkv, qk_gain, freq, table,
    queries, prompt_kv, near_kv, sent, draft_kv, own_count, verify_kv, small,
    weights, normed, wide, rows_q, held, sems,
):
    rows, drafted = x.shape[0], draft.shape[1]
    fetch = pltpu.make_async_copy(x, held, sems.at[3])
    fetch.start()
    copies = []
    for h in range(3):
        part = wq.at[:, h * 2 * HEAD : (h + 1) * 2 * HEAD] if h < 2 else wkv
        copy = pltpu.make_async_copy(part, weights.at[h], sems.at[h])
        copy.start()
        copies.append(copy)

    wide[...] = jnp.zeros_like(wide)
    wide[:drafted] = unit(draft[0].astype(f32)) * gain[...]
    normed[rows:] = wide[...].astype(bf16)
    small[...] = jnp.zeros_like(small)
    small[0:1, :] = qk_gain[0:1, :]
    small[1:2, : HEAD // 2] = freq[...]

    own_count[...] = tally(table[...], meta[0], own_count.shape[1], 0, 1)

    half = HEAD // 2
    row = iota((normed.shape[0], half), 0)
    start = jnp.zeros_like(row)
    end = jnp.int32(0)
    for i in range(3):
        end = end + lengths[0, i]
        start = jnp.where(row >= end, end, start)
    position = jnp.where(row < rows, row - start, row - rows + meta[0])
    angles = position.astype(f32) * freq[...]
    cos, sin = jnp.cos(angles), jnp.sin(angles)

    def rotated(values):
        a, b = values[:, :half], values[:, half:]
        return jnp.concatenate([a * cos - b * sin, b * cos + a * sin], axis=-1)

    fetch.wait()
    normed[:rows] = (unit(held[...].astype(f32)) * gain[...]).astype(bf16)

    keep = iota((PAD, HEAD), 0) < meta[1]

    for pair in range(3):
        copies[pair].wait()
        both = dot_n(normed[...], weights[pair])
        for j in range(2):
            h = 2 * pair + j
            value = unit(both[:, j * HEAD : (j + 1) * HEAD])
            if h < QH:
                query = rotated(value * qk_gain[0:1, :])
                queries[h] = query[:rows].astype(bf16)
                mine = query[rows : rows + PAD]
                rows_q[h * PAD : (h + 1) * PAD, :] = mine
                continue
            if h == QH:
                value = rotated(value * qk_gain[1:2, :])
            cols = slice(j * HEAD, (j + 1) * HEAD)
            prompt_kv[:, cols] = value[:rows].astype(bf16)
            near_kv[:, cols] = value[:rows].astype(bf16)
            mine = value[rows : rows + PAD]
            draft_kv[:, cols] = mine
            verify_kv[0, :, cols] = jnp.where(keep, mine, 0.0)[:drafted].astype(bf16)
    sent[...] = rows_q[...].astype(bf16)


def project(meta, lengths, x, draft, gain, wq, wkv, qk_gain, freq, table, own):
    rows, width = x.shape
    drafted = draft.shape[1]
    total = rows + 16
    shapes = [
        jax.ShapeDtypeStruct((QH, rows, HEAD), bf16),
        jax.ShapeDtypeStruct((rows, 2 * HEAD), bf16),
        jax.ShapeDtypeStruct((rows, 2 * HEAD), bf16),
        jax.ShapeDtypeStruct((QH * PAD, HEAD), bf16),
        jax.ShapeDtypeStruct((PAD, 2 * HEAD), f32),
        jax.ShapeDtypeStruct((1, own), f32),
        jax.ShapeDtypeStruct((1, drafted, 2 * HEAD), bf16),
        jax.ShapeDtypeStruct((8, HEAD), f32),
    ]
    return pl.pallas_call(
        project_kernel,
        in_specs=[SMEM, SMEM, HBM, VMEM, VMEM, HBM, HBM, VMEM, VMEM, VMEM],
        out_specs=[VMEM] * len(shapes),
        out_shape=shapes,
        scratch_shapes=[
            pltpu.VMEM((3, width, 2 * HEAD), bf16),
            pltpu.VMEM((total, width), bf16),
            pltpu.VMEM((16, width), f32),
            pltpu.VMEM((QH * PAD, HEAD), f32),
            pltpu.VMEM((rows, width), bf16),
            pltpu.SemaphoreType.DMA((4,)),
        ],
        compiler_params=pltpu.CompilerParams(vmem_limit_bytes=55 << 20),
        cost_estimate=pl.CostEstimate(
            flops=2 * total * width * 6 * HEAD, transcendentals=0, bytes_accessed=9 << 20
        ),
        name="project",
    )(meta, lengths, x, draft, gain, wq, wkv, qk_gain, freq, table)


def pack_kernel(meta, draft, gain, table, after, out, wide):
    drafted, slots = draft.shape[1], table.shape[1]
    wide[...] = jnp.zeros_like(wide)
    wide[:drafted] = unit(draft[0].astype(f32)) * gain[...]
    lane = iota((1, 128), 1)
    size = jnp.where(lane == slots, meta[0] >> 3, jnp.where(lane == slots + 1, meta[0] & 7, 0))
    wide[5:6, :128] = size.astype(f32)
    wide[5:6, :slots] = table[...].astype(f32)
    out[0] = wide[...].astype(bf16)


def pack(meta, draft, gain, table, after):
    width = draft.shape[2]
    return pl.pallas_call(
        pack_kernel,
        in_specs=[SMEM, VMEM, VMEM, VMEM, VMEM],
        out_specs=VMEM,
        out_shape=jax.ShapeDtypeStruct((1, PAD, width), bf16),
        scratch_shapes=[pltpu.VMEM((PAD, width), f32)],
        compiler_params=pltpu.CompilerParams(vmem_limit_bytes=4 << 20),
        cost_estimate=pl.CostEstimate(flops=0, transcendentals=0, bytes_accessed=1 << 17),
        name="pack",
    )(meta, draft, gain, table, after)


def ask_kernel(where, x, wq, small, out, weights, sems):
    groups = x.shape[0]
    copies = []
    for i in range(2):
        cols = slice(i * 2 * HEAD, (i + 1) * 2 * HEAD)
        copy = pltpu.make_async_copy(wq.at[:, cols], weights.at[i], sems.at[i])
        copy.start()
        copies.append(copy)
    normed = x[...].astype(f32).reshape(groups * PAD, -1).astype(bf16)
    half = HEAD // 2
    counts, starts = [], []
    for e in range(groups):
        note = x[e][5:6, :128].astype(f32).astype(i32)
        size = jnp.sum(jnp.where(iota((1, 128), 1) == 64, note * 8, 0), keepdims=True)
        size += jnp.sum(jnp.where(iota((1, 128), 1) == 65, note, 0), keepdims=True)
        starts.append(jnp.broadcast_to(size, (PAD, half)))
        counts.append(tally(note[:, :64], size, HEAD, 64 + where[0], DEEP))
    count = jnp.concatenate(counts, axis=0).reshape(groups, 1, HEAD)
    position = jnp.concatenate(starts, axis=0) + (iota((groups * PAD, half), 0) & (PAD - 1))
    angles = position.astype(f32) * small[1:2, : HEAD // 2]
    cos, sin = jnp.cos(angles), jnp.sin(angles)
    mark = iota((groups, PAD, HEAD), 1) == 5
    heads = []
    for i in range(2):
        copies[i].wait()
        both = dot_n(normed, weights[i])
        for j in range(2):
            value = unit(both[:, j * HEAD : (j + 1) * HEAD]) * small[0:1, :]
            a, b = value[:, :half], value[:, half:]
            value = jnp.concatenate([a * cos - b * sin, b * cos + a * sin], axis=-1)
            value = value.reshape(groups, PAD, HEAD)
            heads.append(jnp.where(mark, count, value) if not heads else value)
    out[...] = jnp.concatenate(heads, axis=1).astype(bf16)


def ask(where, x, wq, small):
    groups, _, width = x.shape
    return pl.pallas_call(
        ask_kernel,
        in_specs=[SMEM, VMEM, HBM, VMEM],
        out_specs=VMEM,
        out_shape=jax.ShapeDtypeStruct((groups, QH * PAD, HEAD), bf16),
        scratch_shapes=[
            pltpu.VMEM((2, width, 2 * HEAD), bf16),
            pltpu.SemaphoreType.DMA((2,)),
        ],
        compiler_params=pltpu.CompilerParams(vmem_limit_bytes=50 << 20),
        cost_estimate=pl.CostEstimate(
            flops=2 * groups * PAD * width * QH * HEAD, transcendentals=0, bytes_accessed=5 << 20
        ),
        name="ask",
    )(where, x, wq, small)


def prompt_kernel(
    lengths, q, kv, query, draft_kv, pool, count, w_out, out, local, attn, weights, sems
):
    split = sems.shape[0]
    cols = out.shape[1] // split
    copies = []
    for i in range(split):
        part = slice(i * cols, (i + 1) * cols)
        copy = pltpu.make_async_copy(w_out.at[:, part], weights.at[:, part], sems.at[i])
        copy.start()
        copies.append(copy)
    rows = attn.shape[0]
    row, col = iota((rows, rows), 0), iota((rows, rows), 1)
    start = jnp.zeros((rows, rows), i32)
    end = jnp.int32(0)
    for i in range(3):
        end = end + lengths[0, i]
        start = jnp.where(row >= end, end, start)
    allowed = (col <= row) & (col >= start)
    key, value = kv[:, :HEAD], kv[:, HEAD:]
    for h in range(QH):
        scores = jnp.where(allowed, dot_t(q[h], key), neg_large)
        parts = jnp.exp(scores - jnp.max(scores, axis=-1, keepdims=True))
        probs = (parts / jnp.sum(parts, axis=-1, keepdims=True)).astype(bf16)
        attn[:, h * HEAD : (h + 1) * HEAD] = dot_n(probs, value).astype(bf16)

    mine = query[...]
    times = count[...]
    scores = jnp.where(times > 0.0, dot_t(mine, pool[:, :HEAD]), neg_large)
    fresh = dot_t(mine, draft_kv[:, :HEAD].astype(bf16))
    allowed = iota(fresh.shape, 1) <= (iota(fresh.shape, 0) & (PAD - 1))
    fresh = jnp.where(allowed, fresh, neg_large)
    peak = jnp.maximum(
        jnp.max(scores, axis=-1, keepdims=True), jnp.max(fresh, axis=-1, keepdims=True)
    )
    parts = jnp.where(times > 0.0, jnp.exp(scores - peak) * times, 0.0)
    fresh = jnp.where(allowed, jnp.exp(fresh - peak), 0.0)
    denom = jnp.sum(parts, axis=-1, keepdims=True) + jnp.sum(fresh, axis=-1, keepdims=True)
    local[:, :HEAD] = dot_n(parts.astype(bf16), pool[:, HEAD:]) + dot_n(
        fresh.astype(bf16), draft_kv[:, HEAD:].astype(bf16)
    )
    local[:, HEAD : HEAD + 128] = jnp.broadcast_to(peak, (QH * PAD, 128))
    local[:, HEAD + 128 :] = jnp.broadcast_to(denom, (QH * PAD, 128))

    for i in range(split):
        copies[i].wait()
        part = slice(i * cols, (i + 1) * cols)
        out[:, part] = dot_n(attn[...], weights[:, part]).astype(bf16)


def prompts(lengths, q, kv, query, draft_kv, pool, count, w_out):
    rows = kv.shape[0]
    depth, width = w_out.shape
    return pl.pallas_call(
        prompt_kernel,
        in_specs=[SMEM] + [VMEM] * 6 + [HBM],
        out_specs=[VMEM, VMEM],
        out_shape=[
            jax.ShapeDtypeStruct((rows, width), bf16),
            jax.ShapeDtypeStruct((QH * PAD, 2 * HEAD), f32),
        ],
        scratch_shapes=[
            pltpu.VMEM((rows, depth), bf16),
            pltpu.VMEM((depth, width), bf16),
            pltpu.SemaphoreType.DMA((4,)),
        ],
        compiler_params=pltpu.CompilerParams(vmem_limit_bytes=54 << 20),
        cost_estimate=pl.CostEstimate(
            flops=16 * rows * rows * HEAD, transcendentals=4 * rows * rows, bytes_accessed=4 << 20
        ),
        name="prompts",
    )(lengths, q, kv, query, draft_kv, pool, count, w_out)


def remote_kernel(where, queries, pages, after, out):
    here = where[0]
    groups, rows = queries.shape[0], queries.shape[1]
    asked = [here ^ mask for mask in ORDER]
    scores, counts = [], []
    for e in range(groups):
        query = queries[e]
        count = query.astype(f32)[5:6, :]
        held = pages[:, asked[e], :, :HEAD].reshape(HEAD, HEAD)
        scores.append(jnp.where(count > 0.0, dot_t(query, held), neg_large))
        counts.append(jnp.broadcast_to(count, (rows, HEAD)))
    score = jnp.concatenate(scores, axis=0)
    count = jnp.concatenate(counts, axis=0)
    peak = jnp.max(score, axis=-1, keepdims=True).astype(bf16).astype(f32)
    parts = jnp.where(count > 0.0, jnp.exp(score - peak) * count, 0.0)
    denom = jnp.sum(parts, axis=-1, keepdims=True)
    high = denom.astype(bf16).astype(f32)

    shape = (groups * rows // PAD, PAD, 128)
    token, lane = iota(shape, 1), iota(shape, 2)

    def along(values):
        wide = jnp.broadcast_to(values, (groups * rows, 128)).reshape(shape)
        wide = jnp.sum(jnp.where(token == lane, wide, 0.0), axis=1, keepdims=True)
        return jnp.broadcast_to(wide, shape)

    stats = jnp.where(
        token == 5, along(peak), jnp.where(token == 6, along(high), along(denom - high))
    ).reshape(groups * rows, 128)
    spare = (iota((rows, 128), 0) & (PAD - 1)) >= 5
    parts = parts.astype(bf16)
    for e in range(groups):
        own = slice(e * rows, (e + 1) * rows)
        held = pages[:, asked[e], :, HEAD:].reshape(HEAD, HEAD)
        total = dot_n(parts[own], held)
        out[asked[e], :, :128] = jnp.where(spare, stats[own], total[:, :128]).astype(bf16)
        out[asked[e], :, 128:] = total[:, 128:].astype(bf16)


ORDER = (0, 4, 2, 6, 1, 5, 3, 7)


def remote_pieces(where, queries, pages, after):
    groups, rows, _ = queries.shape
    return pl.pallas_call(
        remote_kernel,
        in_specs=[SMEM, VMEM, VMEM, VMEM],
        out_specs=VMEM,
        out_shape=jax.ShapeDtypeStruct((groups, rows, HEAD), bf16),
        compiler_params=pltpu.CompilerParams(vmem_limit_bytes=12 << 20),
        cost_estimate=pl.CostEstimate(flops=1 << 26, transcendentals=1 << 16, bytes_accessed=3 << 20),
        name="remote_pieces",
    )(where, queries, pages, after)


def join_kernel(pieces, local, w_out, out, attn, weights, sems):
    depth, width = w_out.shape
    parts = sems.shape[0]
    cols = width // parts
    copies = []
    for i in range(parts):
        part = slice(i * cols, (i + 1) * cols)
        copy = pltpu.make_async_copy(w_out.at[:, part], weights.at[:, part], sems.at[i])
        copy.start()
        copies.append(copy)
    groups, rows = pieces.shape[0], pieces.shape[1]
    shape = (groups * rows // PAD, PAD, 128)
    token, lane = iota(shape, 1), iota(shape, 2)
    spare = pieces[:, :, :128].astype(f32).reshape(shape)

    def upright(which):
        row = jnp.sum(jnp.where(token == which, spare, 0.0), axis=1, keepdims=True)
        row = jnp.where(token == lane, jnp.broadcast_to(row, shape), 0.0)
        return jnp.sum(row, axis=2, keepdims=True).reshape(groups, rows, 1)

    peaks = upright(5)
    sums = upright(6) + upright(7)
    own = local[:, HEAD : HEAD + 1]
    top = jnp.maximum(jnp.max(peaks, axis=0), own)
    scale = jnp.exp(peaks - top[None])
    near = jnp.exp(own - top)
    total = local[:, :HEAD] * near + jnp.sum(pieces[...].astype(f32) * scale, axis=0)
    denom = local[:, HEAD + 128 : HEAD + 129] * near + jnp.sum(sums * scale, axis=0)
    attn[...] = total / denom
    heads = [attn[h * PAD : (h + 1) * PAD, :].astype(bf16) for h in range(QH)]
    for i in range(parts):
        copies[i].wait()
        part = slice(i * cols, (i + 1) * cols)
        out[:, part] = functools.reduce(
            jnp.add,
            [dot_n(heads[h], weights[h * HEAD : (h + 1) * HEAD, part]) for h in range(QH)],
        )


def join(pieces, local, w_out):
    depth, width = w_out.shape
    return pl.pallas_call(
        join_kernel,
        in_specs=[VMEM, VMEM, HBM],
        out_specs=VMEM,
        out_shape=jax.ShapeDtypeStruct((PAD, width), f32),
        scratch_shapes=[
            pltpu.VMEM((QH * PAD, HEAD), f32),
            pltpu.VMEM((depth, width), bf16),
            pltpu.SemaphoreType.DMA((4,)),
        ],
        compiler_params=pltpu.CompilerParams(vmem_limit_bytes=50 << 20),
        cost_estimate=pl.CostEstimate(flops=1 << 25, transcendentals=0, bytes_accessed=4 << 20),
        name="join",
    )(pieces, local, w_out)


def finish_kernel(side, own, other, x, gain, out, token):
    token[...] = jnp.zeros_like(token)
    half = out.shape[-1]
    total = own[...].astype(f32) + other[...].astype(f32)
    scale = lax.rsqrt(jnp.mean(total * total, axis=-1, keepdims=True) + eps_norm)
    mine = jnp.where(side[0] == 0, total[:, :half], total[:, half:]) * scale * gain[...]
    if len(out.shape) == 3:
        out[0] = (x[0].astype(f32) + mine[: out.shape[1]]).astype(bf16)
    else:
        out[...] = (x[...].astype(f32) + mine).astype(bf16)


def finish(side, own, other, x, gain, name):
    rows, width = own.shape
    half = width // 2
    block = min(rows, 128)
    if x.ndim == 3:
        shape = x.shape[:2] + (half,)
        x_spec = pl.BlockSpec(shape, lambda i, s: (0, 0, s[0]))
        o_spec = pl.BlockSpec(shape, lambda i, s: (0, 0, 0))
    else:
        shape = (rows, half)
        x_spec = pl.BlockSpec((block, half), lambda i, s: (i, s[0]))
        o_spec = pl.BlockSpec((block, half), lambda i, s: (i, 0))
    return pl.pallas_call(
        finish_kernel,
        grid_spec=pltpu.PrefetchScalarGridSpec(
            num_scalar_prefetch=1,
            grid=(rows // block,),
            in_specs=[
                pl.BlockSpec((block, width), lambda i, s: (i, 0)),
                pl.BlockSpec((block, width), lambda i, s: (i, 0)),
                x_spec,
                pl.BlockSpec((1, half), lambda i, s: (0, s[0])),
            ],
            out_specs=[o_spec, pl.BlockSpec(TOKEN.shape, lambda i, s: (0, 0))],
        ),
        out_shape=[jax.ShapeDtypeStruct(shape, bf16), TOKEN],
        compiler_params=pltpu.CompilerParams(vmem_limit_bytes=12 << 20),
        cost_estimate=pl.CostEstimate(
            flops=8 * rows * width, transcendentals=0, bytes_accessed=6 * rows * width
        ),
        name=name,
    )(side, own, other, x, gain)


def on_device(
    plane,
    verify_x,
    prefill_x,
    attn_gain,
    w_query,
    w_keyval,
    qk_gain,
    w_out,
    post_gain,
    page_pool,
    outbound,
    page_table,
    cache_len,
    prompt_len,
    accepted,
):
    devices = outbound.shape[1]
    rows = prefill_x.shape[0]
    pool_pages = page_pool.shape[0]
    planes = len(plane[0])
    column = [list(range(i, i + DEEP)) for i in range(0, devices, DEEP)]

    outgoing, picked = pick_pages(outbound, page_pool)
    outgoing, prefill_x, cache_len = lax.optimization_barrier((outgoing, prefill_x, cache_len))
    arrived = lax.all_to_all(outgoing, "req", 0, 0, tiled=True, axis_index_groups=plane)

    meta = jnp.where(jnp.arange(8, dtype=i32) == 0, cache_len, accepted)
    side = lax.axis_index("head").reshape(1)
    where = (lax.axis_index("req") & (DEEP - 1)).reshape(1)
    swap = [(0, 1), (1, 0)]

    def beside(values, *masks):
        parts = [values]
        for mask in masks:
            pairs = [(i, i ^ mask) for i in range(devices)]
            parts.append(lax.ppermute(values, "req", pairs))
        return jnp.concatenate(parts, axis=0)

    asked = beside(pack(meta, verify_x, attn_gain[None], page_table, picked), 4)

    power = -(np.arange(HEAD // 2, dtype=np.float64) * 2.0) / HEAD
    freq = jnp.asarray((rope_base**power)[None], f32)
    queries, prefill_kv, near_kv, sent, draft_kv, own_count, verify_kv, small = project(
        meta, prompt_len, prefill_x, verify_x, attn_gain[None], w_query, w_keyval,
        qk_gain, freq, page_table, pool_pages * PAGE,
    )
    asked, queries = lax.optimization_barrier((asked, queries))
    asked = beside(asked, 2, 1, 3)
    partial, own = prompts(
        prompt_len, queries, near_kv, sent, draft_kv,
        page_pool.reshape(pool_pages * PAGE, -1), own_count, w_out,
    )
    asked, partial = lax.optimization_barrier((asked, partial))
    other = lax.ppermute(partial, "head", swap)
    prefill_out, done = finish(side, partial, other, prefill_x, post_gain[None], "finish_prompts")

    queries = ask(where, asked, w_query, small)
    pieces = remote_pieces(
        where, queries, arrived.reshape(planes, DEEP, PAGE, -1), done
    )
    pieces = lax.all_to_all(pieces, "req", 0, 0, tiled=True, axis_index_groups=column)
    partial = join(pieces, own, w_out)
    other = lax.ppermute(partial, "head", swap)
    verify_out, _ = finish(side, partial, other, verify_x, post_gain[None], "finish_drafts")
    return (verify_out, prefill_out, verify_kv, prefill_kv)


def solution(mesh):
    devices = mesh.shape["req"]
    plane = [list(range(z, devices, DEEP)) for z in range(DEEP)]
    placed = (
        P("req", None, None),
        P("req", None),
        P(),
        P(None, "head"),
        P(None, "head"),
        P(),
        P("head", None),
        P(),
        P("req", None, "head"),
        P("req", None),
        P("req", None),
        P("req"),
        P("req", None),
        P("req"),
    )
    return jax.shard_map(
        functools.partial(on_device, plane),
        mesh=mesh,
        in_specs=placed,
        out_specs=(
            P("req", None, "head"),
            P("req", "head"),
            P("req", None, "head"),
            P("req", "head"),
        ),
        check_vma=False,
    )
```

```python
import functools

import jax
import jax.numpy as jnp
import numpy as np
from jax import lax
from jax.experimental import pallas as pl
from jax.experimental.pallas import tpu as pltpu
from jax.sharding import PartitionSpec as P

HEAD = 256
PAGE = 16
QH = 4
PAD = 8
DEEP = 8
eps_norm = 1e-06
rope_base = 1000000.0
neg_large = -1e30
bf16, f32, i32 = jnp.bfloat16, jnp.float32, jnp.int32
HBM = pl.BlockSpec(memory_space=pltpu.MemorySpace.HBM)
VMEM = pl.BlockSpec(memory_space=pltpu.MemorySpace.VMEM)
TOKEN = jax.ShapeDtypeStruct((8, 128), f32)
SMEM = pl.BlockSpec(memory_space=pltpu.MemorySpace.SMEM)


def dot_t(a, b):
    return lax.dot_general(a, b, (((1,), (1,)), ((), ())), preferred_element_type=f32)


def dot_n(a, b):
    return jnp.dot(a, b, preferred_element_type=f32)


def iota(shape, dim):
    return lax.broadcasted_iota(i32, shape, dim)


def unit(values):
    return values * lax.rsqrt(jnp.mean(values * values, axis=-1, keepdims=True) + eps_norm)


def tally(table, length, lanes, first, step):
    slots = table.shape[1]
    eye = iota((slots, slots), 0) == iota((slots, slots), 1)
    page = jnp.sum(jnp.where(eye, table, 0), axis=1, keepdims=True)
    base = iota((slots, 1), 0) * PAGE
    lane = iota((slots, lanes), 1)
    named = page == first + (lane >> 4) * step
    valid = base + (lane & (PAGE - 1)) < length
    return jnp.sum(jnp.where(named & valid, 1.0, 0.0), axis=0, keepdims=True)


def pick_kernel(index, pool, out, token):
    token[...] = jnp.zeros_like(token)
    for i in range(out.shape[0]):
        out[i] = pool[jnp.clip(index[0, i], 0, pool.shape[0] - 1)]


def pick_pages(index, pool):
    count = index.shape[1]
    return pl.pallas_call(
        pick_kernel,
        in_specs=[SMEM, VMEM],
        out_specs=[VMEM, VMEM],
        out_shape=[jax.ShapeDtypeStruct((count,) + pool.shape[1:], pool.dtype), TOKEN],
        cost_estimate=pl.CostEstimate(flops=0, transcendentals=0, bytes_accessed=4 << 20),
        name="pick_pages",
    )(index, pool)


def project_kernel(
    meta, lengths, x, draft, gain, wq, wkv, qk_gain, freq, table,
    queries, prompt_kv, near_kv, sent, draft_kv, own_count, verify_kv, small,
    weights, normed, wide, rows_q, held, sems,
):
    rows, drafted = x.shape[0], draft.shape[1]
    fetch = pltpu.make_async_copy(x, held, sems.at[3])
    fetch.start()
    copies = []
    for h in range(3):
        part = wq.at[:, h * 2 * HEAD : (h + 1) * 2 * HEAD] if h < 2 else wkv
        copy = pltpu.make_async_copy(part, weights.at[h], sems.at[h])
        copy.start()
        copies.append(copy)

    wide[...] = jnp.zeros_like(wide)
    wide[:drafted] = unit(draft[0].astype(f32)) * gain[...]
    normed[rows:] = wide[...].astype(bf16)
    small[...] = jnp.zeros_like(small)
    small[0:1, :] = qk_gain[0:1, :]
    small[1:2, : HEAD // 2] = freq[...]

    own_count[...] = tally(table[...], meta[0], own_count.shape[1], 0, 1)

    half = HEAD // 2
    row = iota((normed.shape[0], half), 0)
    start = jnp.zeros_like(row)
    end = jnp.int32(0)
    for i in range(3):
        end = end + lengths[0, i]
        start = jnp.where(row >= end, end, start)
    position = jnp.where(row < rows, row - start, row - rows + meta[0])
    angles = position.astype(f32) * freq[...]
    cos, sin = jnp.cos(angles), jnp.sin(angles)

    def rotated(values):
        a, b = values[:, :half], values[:, half:]
        return jnp.concatenate([a * cos - b * sin, b * cos + a * sin], axis=-1)

    fetch.wait()
    normed[:rows] = (unit(held[...].astype(f32)) * gain[...]).astype(bf16)

    keep = iota((PAD, HEAD), 0) < meta[1]

    for pair in range(3):
        copies[pair].wait()
        both = dot_n(normed[...], weights[pair])
        for j in range(2):
            h = 2 * pair + j
            value = unit(both[:, j * HEAD : (j + 1) * HEAD])
            if h < QH:
                query = rotated(value * qk_gain[0:1, :])
                queries[h] = query[:rows].astype(bf16)
                mine = query[rows : rows + PAD]
                rows_q[h * PAD : (h + 1) * PAD, :] = mine
                continue
            if h == QH:
                value = rotated(value * qk_gain[1:2, :])
            cols = slice(j * HEAD, (j + 1) * HEAD)
            prompt_kv[:, cols] = value[:rows].astype(bf16)
            near_kv[:, cols] = value[:rows].astype(bf16)
            mine = value[rows : rows + PAD]
            draft_kv[:, cols] = mine
            verify_kv[0, :, cols] = jnp.where(keep, mine, 0.0)[:drafted].astype(bf16)
    sent[...] = rows_q[...].astype(bf16)


def project(meta, lengths, x, draft, gain, wq, wkv, qk_gain, freq, table, own):
    rows, width = x.shape
    drafted = draft.shape[1]
    total = rows + 16
    shapes = [
        jax.ShapeDtypeStruct((QH, rows, HEAD), bf16),
        jax.ShapeDtypeStruct((rows, 2 * HEAD), bf16),
        jax.ShapeDtypeStruct((rows, 2 * HEAD), bf16),
        jax.ShapeDtypeStruct((QH * PAD, HEAD), bf16),
        jax.ShapeDtypeStruct((PAD, 2 * HEAD), f32),
        jax.ShapeDtypeStruct((1, own), f32),
        jax.ShapeDtypeStruct((1, drafted, 2 * HEAD), bf16),
        jax.ShapeDtypeStruct((8, HEAD), f32),
    ]
    return pl.pallas_call(
        project_kernel,
        in_specs=[SMEM, SMEM, HBM, VMEM, VMEM, HBM, HBM, VMEM, VMEM, VMEM],
        out_specs=[VMEM] * len(shapes),
        out_shape=shapes,
        scratch_shapes=[
            pltpu.VMEM((3, width, 2 * HEAD), bf16),
            pltpu.VMEM((total, width), bf16),
            pltpu.VMEM((16, width), f32),
            pltpu.VMEM((QH * PAD, HEAD), f32),
            pltpu.VMEM((rows, width), bf16),
            pltpu.SemaphoreType.DMA((4,)),
        ],
        compiler_params=pltpu.CompilerParams(vmem_limit_bytes=55 << 20),
        cost_estimate=pl.CostEstimate(
            flops=2 * total * width * 6 * HEAD, transcendentals=0, bytes_accessed=9 << 20
        ),
        name="project",
    )(meta, lengths, x, draft, gain, wq, wkv, qk_gain, freq, table)


def pack_kernel(meta, draft, gain, table, after, out, wide):
    drafted, slots = draft.shape[1], table.shape[1]
    wide[...] = jnp.zeros_like(wide)
    wide[:drafted] = unit(draft[0].astype(f32)) * gain[...]
    lane = iota((1, 128), 1)
    size = jnp.where(lane == slots, meta[0] >> 3, jnp.where(lane == slots + 1, meta[0] & 7, 0))
    wide[5:6, :128] = size.astype(f32)
    wide[5:6, :slots] = table[...].astype(f32)
    out[0] = wide[...].astype(bf16)


def pack(meta, draft, gain, table, after):
    width = draft.shape[2]
    return pl.pallas_call(
        pack_kernel,
        in_specs=[SMEM, VMEM, VMEM, VMEM, VMEM],
        out_specs=VMEM,
        out_shape=jax.ShapeDtypeStruct((1, PAD, width), bf16),
        scratch_shapes=[pltpu.VMEM((PAD, width), f32)],
        compiler_params=pltpu.CompilerParams(vmem_limit_bytes=4 << 20),
        cost_estimate=pl.CostEstimate(flops=0, transcendentals=0, bytes_accessed=1 << 17),
        name="pack",
    )(meta, draft, gain, table, after)


def ask_kernel(where, x, wq, small, out, weights, sems):
    groups = x.shape[0]
    copies = []
    for i in range(2):
        cols = slice(i * 2 * HEAD, (i + 1) * 2 * HEAD)
        copy = pltpu.make_async_copy(wq.at[:, cols], weights.at[i], sems.at[i])
        copy.start()
        copies.append(copy)
    normed = x[...].astype(f32).reshape(groups * PAD, -1).astype(bf16)
    half = HEAD // 2
    counts, starts = [], []
    for e in range(groups):
        note = x[e][5:6, :128].astype(f32).astype(i32)
        size = jnp.sum(jnp.where(iota((1, 128), 1) == 64, note * 8, 0), keepdims=True)
        size += jnp.sum(jnp.where(iota((1, 128), 1) == 65, note, 0), keepdims=True)
        starts.append(jnp.broadcast_to(size, (PAD, half)))
        counts.append(tally(note[:, :64], size, HEAD, 64 + where[0], DEEP))
    count = jnp.concatenate(counts, axis=0).reshape(groups, 1, HEAD)
    position = jnp.concatenate(starts, axis=0) + (iota((groups * PAD, half), 0) & (PAD - 1))
    angles = position.astype(f32) * small[1:2, : HEAD // 2]
    cos, sin = jnp.cos(angles), jnp.sin(angles)
    mark = iota((groups, PAD, HEAD), 1) == 5
    heads = []
    for i in range(2):
        copies[i].wait()
        both = dot_n(normed, weights[i])
        for j in range(2):
            value = unit(both[:, j * HEAD : (j + 1) * HEAD]) * small[0:1, :]
            a, b = value[:, :half], value[:, half:]
            value = jnp.concatenate([a * cos - b * sin, b * cos + a * sin], axis=-1)
            value = value.reshape(groups, PAD, HEAD)
            heads.append(jnp.where(mark, count, value) if not heads else value)
    out[...] = jnp.concatenate(heads, axis=1).astype(bf16)


def ask(where, x, wq, small):
    groups, _, width = x.shape
    return pl.pallas_call(
        ask_kernel,
        in_specs=[SMEM, VMEM, HBM, VMEM],
        out_specs=VMEM,
        out_shape=jax.ShapeDtypeStruct((groups, QH * PAD, HEAD), bf16),
        scratch_shapes=[
            pltpu.VMEM((2, width, 2 * HEAD), bf16),
            pltpu.SemaphoreType.DMA((2,)),
        ],
        compiler_params=pltpu.CompilerParams(vmem_limit_bytes=50 << 20),
        cost_estimate=pl.CostEstimate(
            flops=2 * groups * PAD * width * QH * HEAD, transcendentals=0, bytes_accessed=5 << 20
        ),
        name="ask",
    )(where, x, wq, small)


def prompt_kernel(
    lengths, q, kv, query, draft_kv, pool, count, w_out, out, local, attn, weights, sems
):
    split = sems.shape[0]
    cols = out.shape[1] // split
    copies = []
    for i in range(split):
        part = slice(i * cols, (i + 1) * cols)
        copy = pltpu.make_async_copy(w_out.at[:, part], weights.at[:, part], sems.at[i])
        copy.start()
        copies.append(copy)
    rows = attn.shape[0]
    row, col = iota((rows, rows), 0), iota((rows, rows), 1)
    start = jnp.zeros((rows, rows), i32)
    end = jnp.int32(0)
    for i in range(3):
        end = end + lengths[0, i]
        start = jnp.where(row >= end, end, start)
    allowed = (col <= row) & (col >= start)
    key, value = kv[:, :HEAD], kv[:, HEAD:]
    for h in range(QH):
        scores = jnp.where(allowed, dot_t(q[h], key), neg_large)
        parts = jnp.exp(scores - jnp.max(scores, axis=-1, keepdims=True))
        probs = (parts / jnp.sum(parts, axis=-1, keepdims=True)).astype(bf16)
        attn[:, h * HEAD : (h + 1) * HEAD] = dot_n(probs, value).astype(bf16)

    mine = query[...]
    times = count[...]
    scores = jnp.where(times > 0.0, dot_t(mine, pool[:, :HEAD]), neg_large)
    fresh = dot_t(mine, draft_kv[:, :HEAD].astype(bf16))
    allowed = iota(fresh.shape, 1) <= (iota(fresh.shape, 0) & (PAD - 1))
    fresh = jnp.where(allowed, fresh, neg_large)
    peak = jnp.maximum(
        jnp.max(scores, axis=-1, keepdims=True), jnp.max(fresh, axis=-1, keepdims=True)
    )
    parts = jnp.where(times > 0.0, jnp.exp(scores - peak) * times, 0.0)
    fresh = jnp.where(allowed, jnp.exp(fresh - peak), 0.0)
    denom = jnp.sum(parts, axis=-1, keepdims=True) + jnp.sum(fresh, axis=-1, keepdims=True)
    local[:, :HEAD] = dot_n(parts.astype(bf16), pool[:, HEAD:]) + dot_n(
        fresh.astype(bf16), draft_kv[:, HEAD:].astype(bf16)
    )
    local[:, HEAD : HEAD + 128] = jnp.broadcast_to(peak, (QH * PAD, 128))
    local[:, HEAD + 128 :] = jnp.broadcast_to(denom, (QH * PAD, 128))

    for i in range(split):
        copies[i].wait()
        part = slice(i * cols, (i + 1) * cols)
        out[:, part] = dot_n(attn[...], weights[:, part]).astype(bf16)


def prompts(lengths, q, kv, query, draft_kv, pool, count, w_out):
    rows = kv.shape[0]
    depth, width = w_out.shape
    return pl.pallas_call(
        prompt_kernel,
        in_specs=[SMEM] + [VMEM] * 6 + [HBM],
        out_specs=[VMEM, VMEM],
        out_shape=[
            jax.ShapeDtypeStruct((rows, width), bf16),
            jax.ShapeDtypeStruct((QH * PAD, 2 * HEAD), f32),
        ],
        scratch_shapes=[
            pltpu.VMEM((rows, depth), bf16),
            pltpu.VMEM((depth, width), bf16),
            pltpu.SemaphoreType.DMA((4,)),
        ],
        compiler_params=pltpu.CompilerParams(vmem_limit_bytes=54 << 20),
        cost_estimate=pl.CostEstimate(
            flops=16 * rows * rows * HEAD, transcendentals=4 * rows * rows, bytes_accessed=4 << 20
        ),
        name="prompts",
    )(lengths, q, kv, query, draft_kv, pool, count, w_out)


def remote_kernel(where, queries, pages, out):
    here = where[0]
    groups, rows = queries.shape[0], queries.shape[1]
    asked = [here ^ mask for mask in ORDER]
    scores, counts = [], []
    for e in range(groups):
        query = queries[e]
        count = query.astype(f32)[5:6, :]
        held = pages[:, asked[e], :, :HEAD].reshape(HEAD, HEAD)
        scores.append(jnp.where(count > 0.0, dot_t(query, held), neg_large))
        counts.append(jnp.broadcast_to(count, (rows, HEAD)))
    score = jnp.concatenate(scores, axis=0)
    count = jnp.concatenate(counts, axis=0)
    peak = jnp.max(score, axis=-1, keepdims=True).astype(bf16).astype(f32)
    parts = jnp.where(count > 0.0, jnp.exp(score - peak) * count, 0.0)
    denom = jnp.sum(parts, axis=-1, keepdims=True)
    high = denom.astype(bf16).astype(f32)

    shape = (groups * rows // PAD, PAD, 128)
    token, lane = iota(shape, 1), iota(shape, 2)

    def along(values):
        wide = jnp.broadcast_to(values, (groups * rows, 128)).reshape(shape)
        wide = jnp.sum(jnp.where(token == lane, wide, 0.0), axis=1, keepdims=True)
        return jnp.broadcast_to(wide, shape)

    stats = jnp.where(
        token == 5, along(peak), jnp.where(token == 6, along(high), along(denom - high))
    ).reshape(groups * rows, 128)
    spare = (iota((rows, 128), 0) & (PAD - 1)) >= 5
    parts = parts.astype(bf16)
    for e in range(groups):
        own = slice(e * rows, (e + 1) * rows)
        held = pages[:, asked[e], :, HEAD:].reshape(HEAD, HEAD)
        total = dot_n(parts[own], held)
        out[asked[e], :, :128] = jnp.where(spare, stats[own], total[:, :128]).astype(bf16)
        out[asked[e], :, 128:] = total[:, 128:].astype(bf16)


ORDER = (0, 4, 2, 6, 1, 5, 3, 7)


def remote_pieces(where, queries, pages):
    groups, rows, _ = queries.shape
    return pl.pallas_call(
        remote_kernel,
        in_specs=[SMEM, VMEM, VMEM],
        out_specs=VMEM,
        out_shape=jax.ShapeDtypeStruct((groups, rows, HEAD), bf16),
        compiler_params=pltpu.CompilerParams(vmem_limit_bytes=12 << 20),
        cost_estimate=pl.CostEstimate(flops=1 << 26, transcendentals=1 << 16, bytes_accessed=3 << 20),
        name="remote_pieces",
    )(where, queries, pages)


def join_kernel(pieces, local, w_out, out, attn, weights, sems):
    depth, width = w_out.shape
    parts = sems.shape[0]
    cols = width // parts
    copies = []
    for i in range(parts):
        part = slice(i * cols, (i + 1) * cols)
        copy = pltpu.make_async_copy(w_out.at[:, part], weights.at[:, part], sems.at[i])
        copy.start()
        copies.append(copy)
    groups, rows = pieces.shape[0], pieces.shape[1]
    shape = (groups * rows // PAD, PAD, 128)
    token, lane = iota(shape, 1), iota(shape, 2)
    spare = pieces[:, :, :128].astype(f32).reshape(shape)

    def upright(which):
        row = jnp.sum(jnp.where(token == which, spare, 0.0), axis=1, keepdims=True)
        row = jnp.where(token == lane, jnp.broadcast_to(row, shape), 0.0)
        return jnp.sum(row, axis=2, keepdims=True).reshape(groups, rows, 1)

    peaks = upright(5)
    sums = upright(6) + upright(7)
    own = local[:, HEAD : HEAD + 1]
    top = jnp.maximum(jnp.max(peaks, axis=0), own)
    scale = jnp.exp(peaks - top[None])
    near = jnp.exp(own - top)
    total = local[:, :HEAD] * near + jnp.sum(pieces[...].astype(f32) * scale, axis=0)
    denom = local[:, HEAD + 128 : HEAD + 129] * near + jnp.sum(sums * scale, axis=0)
    attn[...] = total / denom
    heads = [attn[h * PAD : (h + 1) * PAD, :].astype(bf16) for h in range(QH)]
    for i in range(parts):
        copies[i].wait()
        part = slice(i * cols, (i + 1) * cols)
        out[:, part] = functools.reduce(
            jnp.add,
            [dot_n(heads[h], weights[h * HEAD : (h + 1) * HEAD, part]) for h in range(QH)],
        )


def join(pieces, local, w_out):
    depth, width = w_out.shape
    return pl.pallas_call(
        join_kernel,
        in_specs=[VMEM, VMEM, HBM],
        out_specs=VMEM,
        out_shape=jax.ShapeDtypeStruct((PAD, width), f32),
        scratch_shapes=[
            pltpu.VMEM((QH * PAD, HEAD), f32),
            pltpu.VMEM((depth, width), bf16),
            pltpu.SemaphoreType.DMA((4,)),
        ],
        compiler_params=pltpu.CompilerParams(vmem_limit_bytes=50 << 20),
        cost_estimate=pl.CostEstimate(flops=1 << 25, transcendentals=0, bytes_accessed=4 << 20),
        name="join",
    )(pieces, local, w_out)


def finish_kernel(side, own, other, x, gain, after, out):
    half = out.shape[-1]
    total = own[...].astype(f32) + other[...].astype(f32)
    scale = lax.rsqrt(jnp.mean(total * total, axis=-1, keepdims=True) + eps_norm)
    mine = jnp.where(side[0] == 0, total[:, :half], total[:, half:]) * scale * gain[...]
    if len(out.shape) == 3:
        out[0] = (x[0].astype(f32) + mine[: out.shape[1]]).astype(bf16)
    else:
        out[...] = (x[...].astype(f32) + mine).astype(bf16)


def finish(side, own, other, x, gain, after, name):
    rows, width = own.shape
    half = width // 2
    block = min(rows, 128)
    if x.ndim == 3:
        shape = x.shape[:2] + (half,)
        x_spec = pl.BlockSpec(shape, lambda i, s: (0, 0, s[0]))
        o_spec = pl.BlockSpec(shape, lambda i, s: (0, 0, 0))
    else:
        shape = (rows, half)
        x_spec = pl.BlockSpec((block, half), lambda i, s: (i, s[0]))
        o_spec = pl.BlockSpec((block, half), lambda i, s: (i, 0))
    return pl.pallas_call(
        finish_kernel,
        grid_spec=pltpu.PrefetchScalarGridSpec(
            num_scalar_prefetch=1,
            grid=(rows // block,),
            in_specs=[
                pl.BlockSpec((block, width), lambda i, s: (i, 0)),
                pl.BlockSpec((block, width), lambda i, s: (i, 0)),
                x_spec,
                pl.BlockSpec((1, half), lambda i, s: (0, s[0])),
                pl.BlockSpec((8, 128), lambda i, s: (0, 0)),
            ],
            out_specs=o_spec,
        ),
        out_shape=jax.ShapeDtypeStruct(shape, bf16),
        compiler_params=pltpu.CompilerParams(vmem_limit_bytes=12 << 20),
        cost_estimate=pl.CostEstimate(
            flops=8 * rows * width, transcendentals=0, bytes_accessed=6 * rows * width
        ),
        name=name,
    )(side, own, other, x, gain, after)


def on_device(
    plane,
    verify_x,
    prefill_x,
    attn_gain,
    w_query,
    w_keyval,
    qk_gain,
    w_out,
    post_gain,
    page_pool,
    outbound,
    page_table,
    cache_len,
    prompt_len,
    accepted,
):
    devices = outbound.shape[1]
    rows = prefill_x.shape[0]
    pool_pages = page_pool.shape[0]
    planes = len(plane[0])
    column = [list(range(i, i + DEEP)) for i in range(0, devices, DEEP)]

    outgoing, picked = pick_pages(outbound, page_pool)
    outgoing, prefill_x, cache_len = lax.optimization_barrier((outgoing, prefill_x, cache_len))
    arrived = lax.all_to_all(outgoing, "req", 0, 0, tiled=True, axis_index_groups=plane)

    meta = jnp.where(jnp.arange(8, dtype=i32) == 0, cache_len, accepted)
    side = lax.axis_index("head").reshape(1)
    where = (lax.axis_index("req") & (DEEP - 1)).reshape(1)
    swap = [(0, 1), (1, 0)]

    def beside(values, *masks):
        parts = [values]
        for mask in masks:
            pairs = [(i, i ^ mask) for i in range(devices)]
            parts.append(lax.ppermute(values, "req", pairs))
        return jnp.concatenate(parts, axis=0)

    asked = beside(pack(meta, verify_x, attn_gain[None], page_table, picked), 4)

    power = -(np.arange(HEAD // 2, dtype=np.float64) * 2.0) / HEAD
    freq = jnp.asarray((rope_base**power)[None], f32)
    queries, prefill_kv, near_kv, sent, draft_kv, own_count, verify_kv, small = project(
        meta, prompt_len, prefill_x, verify_x, attn_gain[None], w_query, w_keyval,
        qk_gain, freq, page_table, pool_pages * PAGE,
    )
    asked, queries = lax.optimization_barrier((asked, queries))
    asked = beside(asked, 2, 1, 3)
    partial, own = prompts(
        prompt_len, queries, near_kv, sent, draft_kv,
        page_pool.reshape(pool_pages * PAGE, -1), own_count, w_out,
    )
    asked, partial = lax.optimization_barrier((asked, partial))
    other = lax.ppermute(partial, "head", swap)

    queries = ask(where, asked, w_query, small)
    pieces = remote_pieces(where, queries, arrived.reshape(planes, DEEP, PAGE, -1))
    pieces = lax.all_to_all(pieces, "req", 0, 0, tiled=True, axis_index_groups=column)
    tail = join(pieces, own, w_out)
    prefill_out = finish(
        side, partial, other, prefill_x, post_gain[None], tail, "finish_prompts"
    )
    other = lax.ppermute(tail, "head", swap)
    verify_out = finish(side, tail, other, verify_x, post_gain[None], tail, "finish_drafts")
    return (verify_out, prefill_out, verify_kv, prefill_kv)


def solution(mesh):
    devices = mesh.shape["req"]
    plane = [list(range(z, devices, DEEP)) for z in range(DEEP)]
    placed = (
        P("req", None, None),
        P("req", None),
        P(),
        P(None, "head"),
        P(None, "head"),
        P(),
        P("head", None),
        P(),
        P("req", None, "head"),
        P("req", None),
        P("req", None),
        P("req"),
        P("req", None),
        P("req"),
    )
    return jax.shard_map(
        functools.partial(on_device, plane),
        mesh=mesh,
        in_specs=placed,
        out_specs=(
            P("req", None, "head"),
            P("req", "head"),
            P("req", None, "head"),
            P("req", "head"),
        ),
        check_vma=False,
    )
```
